256 devices in a mesh: dp: 8 (over y, z_lo), fsdp: 32 (over z_hi, x, core).
Axes of the slice: x: 4, y: 4, z: 8 (z_hi: 4, z_lo: 2; z = z_hi * 2 + z_lo), core: 2. Of those that a mesh axis runs over, the one named last changes fastest.
Arguments:
- input_vectors: bfloat16 [16384, 8192], P(('dp', 'fsdp')), may hold values from -48 to 48
- prediction_residual: bfloat16 [16384, 8192], P(('dp', 'fsdp')), may hold values from -48 to 48
- source_category: int32 [16384], P(('dp', 'fsdp')), may hold values from 0 to 63, as said below
- correction_factors: bfloat16 [8192, 128], P('fsdp'), may hold values from -4 to 4
- learning_category_share: float32 [64], replicated, may hold values from 0.25 to 4
- heldout_category_share: float32 [64], replicated, may hold values from 0.25 to 4
Outputs:
- solution: float32 [8192, 128], P('fsdp')
- hyper: float32 [64], replicated
The draws below stay inside these ranges and needn't reach their ends.
Inputs may be any that keep to these rules, and one draw needn't show every extreme that they name: `source_category`: the rows of one device come from at most 3 consecutive domains, counted modulo 64.
All inputs are finite; a program needn't handle non-finite values.
Results may differ from the reference program's by a relative error of at most 0.004.
Values may be sent and summed in bfloat16 or wider, within the bound.
A program may use at most 64 MiB of HBM per device.

```python
import math
import jax
import jax.numpy as jnp
from jax import lax

HIDDEN_FEATURES = 8192
LOW_FACTOR_COUNT = 64
DOMAINS = 64
ITERS = 3
TOK_DEV = 64
ROWS = 16384
DEVICES = 256


def shared_field(key):
    first, second, third = jax.random.split(jax.random.fold_in(key, 11), 3)
    base = jax.random.normal(first, (ROWS, HIDDEN_FEATURES), jnp.float32)
    columns = jnp.exp(jax.random.uniform(second, (1, HIDDEN_FEATURES), jnp.float32, math.log(0.3), math.log(3.0)))
    rows_scale = jnp.exp(jax.random.uniform(third, (ROWS, 1), jnp.float32, math.log(0.5), math.log(2.0)))
    return jnp.clip(base * columns * rows_scale, -48.0, 48.0)


def draw_input_vectors(key, part):
    return shared_field(key).astype(jnp.bfloat16)


def draw_prediction_residual(key, part):
    field = shared_field(key)
    first, second = jax.random.split(jax.random.fold_in(key, 23), 2)
    gains = jax.random.uniform(first, (1, HIDDEN_FEATURES), jnp.float32, 0.3, 0.9)
    noise = 0.5 * jax.random.normal(second, (ROWS, HIDDEN_FEATURES), jnp.float32)
    mixed = -gains * jnp.roll(field, 1, axis=1) + noise
    return jnp.clip(mixed, -48.0, 48.0).astype(jnp.bfloat16)


def draw_source_category(key, part):
    first, second = jax.random.split(jax.random.fold_in(key, 37), 2)
    blocks = ROWS // TOK_DEV
    order = jax.random.permutation(first, DOMAINS)
    starts = order[jnp.arange(blocks, dtype=jnp.int32) % DOMAINS][:, None]
    steps = jax.random.randint(second, (blocks, TOK_DEV), 0, 3)
    return ((starts + steps) % DOMAINS).reshape(ROWS).astype(jnp.int32)


def block_levels(rng, shape, shards, least, high):
    def one(position, parts):
        draws = jax.random.uniform(jax.random.fold_in(jax.random.fold_in(rng, 6), position), (parts,), jnp.float32, least / len(shards), high / len(shards))
        return jnp.repeat(jnp.exp(draws), shape[position] // parts).reshape((-1,) + (1,) * (len(shape) - position - 1))

    loudness = one(*shards[0])
    for cut in shards[1:]:
        loudness = loudness * one(*cut)
    return loudness


def bell_draw(stream_key, shape, spread, limit, pieces=(), kind=jnp.bfloat16):
    result = jax.random.normal(stream_key, shape, jnp.float32) * spread
    if len(pieces) > 0:
        result = block_levels(stream_key, shape, pieces, -0.22, 0.18) * result
    return jnp.clip(result, min=-limit, max=limit).astype(kind)


def setup_inputs(seed: int = 0) -> dict:
    key_list = jax.random.split(jax.random.key(seed), 7)
    return {
        "input_vectors": draw_input_vectors(jax.random.fold_in(key_list[6], 71), 0),
        "prediction_residual": draw_prediction_residual(jax.random.fold_in(key_list[6], 71), 0),
        "source_category": draw_source_category(jax.random.fold_in(key_list[6], 71), 0),
        "correction_factors": bell_draw(key_list[3], (HIDDEN_FEATURES, 2 * LOW_FACTOR_COUNT), 1.0, 4.0, ((0, 32),)),
        "learning_category_share": jnp.clip(jnp.exp(jax.random.uniform(key_list[4], (DOMAINS,), jnp.float32, math.log(0.25), math.log(4.0))), 0.25, 4.0),
        "heldout_category_share": jnp.clip(jnp.exp(jax.random.uniform(key_list[5], (DOMAINS,), jnp.float32, math.log(0.25), math.log(4.0))), 0.25, 4.0),
    }


def reference(input_vectors, prediction_residual, source_category, correction_factors, learning_category_share, heldout_category_share):
    scale_d = HIDDEN_FEATURES ** -0.5
    scale_r = LOW_FACTOR_COUNT ** -0.5
    kappa = DOMAINS / (ROWS * HIDDEN_FEATURES)
    damping = 0.1 * DOMAINS / (HIDDEN_FEATURES * LOW_FACTOR_COUNT)
    reducing_factor = correction_factors[:, :LOW_FACTOR_COUNT]
    expanding_factor_flipped = correction_factors[:, LOW_FACTOR_COUNT:]
    acts_b = input_vectors.reshape(DEVICES, TOK_DEV, HIDDEN_FEATURES)
    offset_b = prediction_residual.reshape(DEVICES, TOK_DEV, HIDDEN_FEATURES)
    domain_b = source_category.reshape(DEVICES, TOK_DEV)
    zero = jnp.zeros((HIDDEN_FEATURES, 2 * LOW_FACTOR_COUNT), jnp.float32)
    highest = lax.Precision.HIGHEST

    def errors(low, off):
        return off.astype(jnp.float32) + jnp.dot(low, expanding_factor_flipped.T, preferred_element_type=jnp.float32) * scale_r

    def tangent(xb, low, dir_full):
        lifted = (jnp.dot(xb.astype(jnp.float32), dir_full[:, :LOW_FACTOR_COUNT], precision=highest) * scale_d).astype(jnp.bfloat16)
        first = jnp.dot(lifted, expanding_factor_flipped.T, preferred_element_type=jnp.float32)
        second = jnp.dot(low.astype(jnp.float32), dir_full[:, LOW_FACTOR_COUNT:].T, precision=highest)
        return (first + second) * scale_r

    def backward(xb, low, cot):
        projected = (jnp.dot(cot, expanding_factor_flipped, preferred_element_type=jnp.float32) * scale_r).astype(jnp.bfloat16)
        grad_down = jnp.dot(xb.T, projected, preferred_element_type=jnp.float32) * scale_d
        grad_up = jnp.dot(cot.T, low, preferred_element_type=jnp.float32) * scale_r
        return jnp.concatenate([grad_down, grad_up], axis=1)

    def rhs_step(total, blk):
        xb, ob, db = blk
        low = (jnp.dot(xb, reducing_factor, preferred_element_type=jnp.float32) * scale_d).astype(jnp.bfloat16)
        error = errors(low, ob)
        cot = (kappa * heldout_category_share[db][:, None] * error).astype(jnp.bfloat16)
        return total + backward(xb, low, cot), low

    rhs, low_b = lax.scan(rhs_step, zero, (acts_b, offset_b, domain_b))

    def product(dir_full):
        def accumulate(total, blk):
            xb, low, db = blk
            along = tangent(xb, low, dir_full)
            weighted = (kappa * learning_category_share[db][:, None] * along).astype(jnp.bfloat16)
            return total + backward(xb, low, weighted), None
        return lax.scan(accumulate, zero, (acts_b, low_b, domain_b))[0]

    solution = zero
    residual = rhs
    direction = rhs
    norm_now = jnp.sum(residual * residual)
    for step in range(ITERS):
        image = product(direction) + damping * direction
        alpha = norm_now / jnp.sum(direction * image)
        solution = solution + alpha * direction
        if step + 1 < ITERS:
            residual = residual - alpha * image
            norm_next = jnp.sum(residual * residual)
            direction = residual + (norm_next / norm_now) * direction
            norm_now = norm_next

    def hyper_step(total, blk):
        xb, ob, low, db = blk
        error = errors(low, ob)
        along = tangent(xb, low, solution)
        per_row = jnp.sum(along * error, axis=1)
        return total + jax.ops.segment_sum(per_row, db, DOMAINS), None

    totals = lax.scan(hyper_step, jnp.zeros((DOMAINS,), jnp.float32), (acts_b, offset_b, low_b, domain_b))[0]
    return solution, -kappa * totals
```

```python
import functools

import jax
import jax.numpy as jnp
from jax import lax
from jax.experimental import pallas as pl
from jax.experimental.pallas import tpu as pltpu
from jax.sharding import PartitionSpec as P

MESH = pl.DeviceIdType.MESH
HIGH = lax.Precision.HIGHEST
RANK = 64
DOMAINS = 64
TOK = 64
HALF = 32
WIDE = 256
F32 = jnp.float32
BF16 = jnp.bfloat16
NN = (((1,), (0,)), ((), ()))
NT = (((1,), (1,)), ((), ()))
TN = (((0,), (0,)), ((), ()))


def mm(a, b, dims=NN):
    return lax.dot_general(a, b, dims, preferred_element_type=F32)


def exact(a, b, dims=NN):
    return lax.dot_general(a, b, dims, precision=HIGH, preferred_element_type=F32)


def split(v):
    hi = v.astype(BF16)
    return hi, (v - hi.astype(F32)).astype(BF16)


def mm2(a, v, dims=NN):
    hi, lo = split(v)
    return mm(a, hi, dims) + mm(a, lo, dims)


def total(v):
    return jnp.sum(v, axis=(0, 1), keepdims=True)


def kernel(
    geo, x, o, cat, coef, tl, th, sol_out, hyp_out,
    xs, os_, cf, wg, p1, rb1, am1, ab1, zp1, zb1, zm1, zg1,
    p2, rb2, am2, ab2, zp2, zb2, zm2, zg2,
    p3, rb3, am3, ab3, zp3, zb3, zm3, zg3,
    p4, rb4, fm, fb, fz, fq, pair_out, pair_in, send, recv, local,
):
    n_plane, n_line, xc, z_lo, blocks = geo
    rows_blk = RANK // blocks
    width = n_plane * WIDE
    rows = n_plane * n_line * TOK
    sd = width ** (-0.5)
    sr = RANK ** (-0.5)
    sr2 = 1.0 / RANK
    kappa = DOMAINS / (rows * width)
    mu = 0.1 * DOMAINS / (width * RANK)
    tall = n_plane * HALF

    dp = lax.axis_index("dp")
    fs = lax.axis_index("fsdp")
    y = lax.div(dp, z_lo)
    low_z = lax.rem(dp, z_lo)
    z_hi = lax.div(fs, xc)
    col = lax.rem(fs, xc)
    me = y * xc + col
    z = z_hi * z_lo + low_z

    def in_plane(j):
        return (lax.div(j, xc) * z_lo + low_z, z_hi * xc + lax.rem(j, xc))

    def in_line(k):
        return (y * z_lo + lax.rem(k, z_lo), lax.div(k, z_lo) * xc + col)

    partner = (z_hi * z_lo + low_z, y * xc + col)
    paired = y != z_hi

    barrier = pltpu.get_barrier_semaphore()

    def greet(i, c):
        pl.semaphore_signal(barrier, inc=1, device_id=in_plane(lax.rem(me + i, n_plane)), device_id_type=MESH)
        return c

    def greet_line(i, c):
        pl.semaphore_signal(barrier, inc=1, device_id=in_line(lax.rem(z + i, n_line)), device_id_type=MESH)
        return c

    lax.fori_loop(1, n_plane, greet, 0)
    lax.fori_loop(1, n_line, greet_line, 0)

    @pl.when(paired)
    def _():
        pl.semaphore_signal(barrier, inc=1, device_id=partner, device_id_type=MESH)
        pl.semaphore_wait(barrier, n_plane + n_line - 1)

    @pl.when(jnp.logical_not(paired))
    def _():
        pl.semaphore_wait(barrier, n_plane + n_line - 2)

    def remote(src, dst, s, device):
        return pltpu.make_async_remote_copy(
            src_ref=src, dst_ref=dst, send_sem=send.at[s], recv_sem=recv.at[s], device_id=device, device_id_type=MESH
        )

    def plane_send(src_of, dst, s):
        def body(i, c):
            j = lax.rem(me + i, n_plane)
            remote(src_of(j), dst.at[me], s, in_plane(j)).start()
            return c

        lax.fori_loop(1, n_plane, body, 0)

    def line_send(src_of, dst, s):
        def body(i, c):
            k = lax.rem(z + i, n_line)
            remote(src_of(k), dst.at[z], s, in_line(k)).start()
            return c

        lax.fori_loop(1, n_line, body, 0)

    def arrived(buf, s):
        part = buf.at[pl.ds(0, buf.shape[0] - 1)]
        pltpu.make_async_copy(part, part, recv.at[s]).wait()

    def left(buf, s):
        part = buf.at[pl.ds(0, buf.shape[0] - 1)]
        pltpu.make_async_copy(part, part, send.at[s]).wait()

    def columns(ref, j):
        return ref.at[:, pl.ds(pl.multiple_of(j * WIDE, WIDE), WIDE)]

    own_x = pltpu.make_async_copy(columns(x, me), xs.at[me], local.at[0])
    own_o = pltpu.make_async_copy(columns(o, me), os_.at[me], local.at[1])

    @pl.when(paired)
    def _():
        remote(coef, cf, 0, partner).start()

    plane_send(lambda j: columns(x, j), xs, 1)
    own_x.start()
    plane_send(lambda j: columns(o, j), os_, 2)
    own_o.start()

    sub = lax.broadcasted_iota(jnp.int32, (RANK, RANK), 0)
    lan = lax.broadcasted_iota(jnp.int32, (RANK, RANK), 1)
    eye = (sub == lan).astype(F32)
    sub2 = lax.broadcasted_iota(jnp.int32, (RANK, 2 * RANK), 0)
    lan2 = lax.broadcasted_iota(jnp.int32, (RANK, 2 * RANK), 1)
    put_l = (lan2 == sub2).astype(F32)
    put_r = (lan2 == sub2 + RANK).astype(F32)
    left_half = lan2 < RANK
    ones_l = left_half.astype(F32)
    ones_r = 1.0 - ones_l
    hot_t = (cat[...] == sub).astype(F32)
    hot = exact(hot_t, eye, TN)

    def weights(table):
        picked = exact(hot, eye * table[...]) * kappa
        return exact(picked[:HALF], ones_l) + exact(picked[HALF:], ones_r)

    own_wl = weights(tl)
    wg[me] = jnp.concatenate([own_wl, weights(th)], axis=0)
    plane_send(lambda j: wg.at[me], wg, 3)

    @pl.when(paired)
    def _():
        remote(coef, cf, 0, partner).wait()

    @pl.when(jnp.logical_not(paired))
    def _():
        own_c = pltpu.make_async_copy(coef, cf, local.at[2])
        own_c.start()
        own_c.wait()

    c = cf[...]
    lanes_c = lax.broadcasted_iota(jnp.int32, c.shape, 1)
    zero_c = jnp.zeros_like(c)
    c_low = jnp.where(lanes_c < RANK, c, zero_c)
    c_up = jnp.where(lanes_c >= RANK, c, zero_c)
    gram = mm(c, c, TN)[RANK:]
    for j in range(n_plane):
        b = (j % blocks) * rows_blk
        p1[j, TOK:] = gram[b : b + rows_blk]
    c_t = exact(put_r, c.astype(F32), NT)

    own_x.wait()
    arrived(xs, 1)
    first = mm(xs[...].reshape(n_plane * TOK, WIDE), c_low)
    own_o.wait()
    arrived(os_, 2)
    first = first + mm(os_[...].reshape(n_plane * TOK, WIDE), c_up)
    p1[:, :TOK] = first.reshape(n_plane, TOK, 2 * RANK)
    rb1[me] = p1[me]
    plane_send(lambda j: p1.at[j], rb1, 4)

    arrived(wg, 3)
    wlp = wg[:, :HALF].reshape(tall, 2 * RANK)
    whp = wg[:, HALF:].reshape(tall, 2 * RANK)

    def spread(v, at):
        return jnp.broadcast_to(v[:, at : at + 1], (tall, 2 * RANK))

    arrived(rb1, 4)
    s1 = jnp.sum(rb1[...], axis=0)
    f_own = jnp.where(left_half, (s1[:TOK] * sd).astype(BF16).astype(F32), s1[:TOK])
    g_hi, g_lo = split(s1[TOK:])
    am1[...] = jnp.concatenate([f_own, g_hi.astype(F32), g_lo.astype(F32)], axis=0).astype(BF16)
    ab1[me] = am1[...]
    plane_send(lambda j: am1, ab1, 5)
    arrived(ab1, 5)

    def assemble(ref, base):
        got = []
        for b in range(blocks):
            v = ref[b, base : base + 2 * rows_blk].astype(F32)
            got.append(v[:rows_blk] + v[rows_blk:])
        return jnp.concatenate(got, axis=0)

    g_wide = assemble(ab1, TOK)
    g_right = jnp.where(left_half, 0.0, g_wide)
    g_left = pltpu.roll(g_right, RANK, 1)
    g = g_left[:, :RANK]
    g_diag = jnp.concatenate([g_left, g_right], axis=0)
    f_a = ab1[:, :HALF].reshape(tall, 2 * RANK)
    f_b = ab1[:, HALF:TOK].reshape(tall, 2 * RANK)
    k_l = jnp.concatenate([g_left * sr2, put_l * sr], axis=0)
    k_r = jnp.concatenate([g_right * sr2, put_r * sr], axis=0)
    p0 = (whp * (mm2(f_a, k_l) + mm2(f_b, k_r))).astype(BF16)
    x_a = xs[:, :HALF].reshape(tall, WIDE)
    x_b = xs[:, HALF:].reshape(tall, WIDE)
    o_a = os_[:, :HALF].reshape(tall, WIDE)
    o_b = os_[:, HALF:].reshape(tall, WIDE)

    def fold(v, a, b):
        return mm(v, a, TN)[:RANK] + mm(v, b, TN)[RANK:]

    wfh_a = (f_a.astype(F32) * spread(whp, 0)).astype(BF16)
    wfh_b = (f_b.astype(F32) * spread(whp, RANK)).astype(BF16)
    wfl_a = (f_a.astype(F32) * spread(wlp, 0)).astype(BF16)
    wfl_b = (f_b.astype(F32) * spread(wlp, RANK)).astype(BF16)
    chunk = RANK // n_line
    zp1[0] = (fold(p0, x_a, x_b) * sd).reshape(n_line, chunk, WIDE)
    zp1[1] = (mm(wfh_a, o_a, TN)[:RANK] + mm(wfh_b, o_b, TN)[:RANK]).reshape(n_line, chunk, WIDE)
    q_h = mm(f_a, wfh_a, TN)[:RANK] + mm(f_b, wfh_b, TN)[:RANK]
    q_l = mm(f_a, wfl_a, TN)[:RANK] + mm(f_b, wfl_b, TN)[:RANK]
    zp1[2] = jnp.concatenate([q_h, q_l], axis=1).reshape(n_line, chunk, WIDE)

    zb1[z] = zp1[:, z]
    line_send(lambda k: zp1.at[:, k], zb1, 6)
    arrived(zb1, 6)
    zm1[...] = jnp.sum(zb1[...], axis=0)
    zg1[z] = zm1[...]
    line_send(lambda k: zm1, zg1, 7)
    arrived(zg1, 7)

    d_t = zg1[:, 0].reshape(RANK, WIDE)
    z_t = zg1[:, 1].reshape(RANK, WIDE)
    stats = zg1[:, 2].reshape(RANK, WIDE)
    s_h = stats[:, :RANK]
    zu = pltpu.roll(stats[:, : 2 * RANK], RANK, 1)[:, :RANK]
    s_l = stats[:, 2 * RANK : 3 * RANK]
    nil = jnp.zeros((RANK, WIDE), BF16)

    def apply(v, a, b, both):
        parts = split(v) if both else (v.astype(BF16),)
        out = None
        for part in parts:
            t = mm(a, jnp.concatenate([part, nil], axis=0), NT) + mm(b, jnp.concatenate([nil, part], axis=0), NT)
            out = t if out is None else out + t
        return out.reshape(n_plane, HALF, 2 * RANK)

    p2[:, :HALF] = apply(d_t, x_a, x_b, True)
    p2[:, HALF:TOK] = apply(z_t, o_a, o_b, False)
    zz_part = exact(exact(z_t, z_t, NT), put_l)
    for j in range(n_plane):
        b = (j % blocks) * rows_blk
        p2[j, TOK:] = zz_part[b : b + rows_blk]
    rb2[me] = p2[me]
    plane_send(lambda j: p2.at[j], rb2, 8)
    d_m = eye * sr
    d_n = s_h * sr2
    d_tu = exact(d_m, zu, TN) + exact(d_n, g, TN)
    e_top = jnp.concatenate([put_l, jnp.zeros_like(put_l)], axis=0)
    e_top_r = jnp.concatenate([put_r, jnp.zeros_like(put_r)], axis=0)
    e_bot = jnp.concatenate([jnp.zeros_like(put_l), put_l], axis=0)
    e_bot_r = jnp.concatenate([jnp.zeros_like(put_r), put_r], axis=0)
    low_p = exact(f_own[:HALF], e_top) + exact(f_own[HALF:], e_top_r)
    ou_p = exact(f_own[:HALF], e_bot) + exact(f_own[HALF:], e_bot_r)
    eu_p = ou_p + sr * exact(low_p, g_diag)

    arrived(rb2, 8)
    s2 = jnp.sum(rb2[...], axis=0)
    d_l = s2[:HALF] * sd
    oz_p = s2[HALF:TOK]
    zz_hi, zz_lo = split(s2[TOK:])
    am2[...] = jnp.concatenate([d_l, zz_hi.astype(F32), zz_lo.astype(F32)], axis=0).astype(BF16)
    ab2[me] = am2[...]
    plane_send(lambda j: am2, ab2, 9)
    arrived(ab2, 9)
    zz = assemble(ab2, HALF)[:, :RANK]

    def gauss(m, n):
        return exact(zz, m) + exact(zu, n), exact(zu, m, TN) + exact(g, n)

    def image_part(l_p, tu, zp):
        tu_l = jnp.concatenate([exact(tu, put_l), jnp.zeros_like(put_l)], axis=0)
        tu_r = jnp.concatenate([exact(tu, put_r), jnp.zeros_like(put_r)], axis=0)
        inner = mm2(l_p, g_diag) + mm2(f_a, tu_l) + mm2(f_b, tu_r)
        y_p = (wlp * sr2 * inner).astype(BF16)
        down = fold(y_p, x_a, x_b) * sd
        cross = fold(l_p, wfl_a, wfl_b)
        zp[...] = jnp.concatenate([down, cross], axis=1).reshape(n_line, chunk, 3 * 2 * RANK)

    def line_sum(zp, zb, zm, zg, s):
        zb[z] = zp[z]
        line_send(lambda k: zp.at[k], zb, s)
        arrived(zb, s)
        zm[...] = jnp.sum(zb[...], axis=0)
        zg[z] = zm[...]
        line_send(lambda k: zm, zg, s + 1)
        arrived(zg, s + 1)
        return zg[...].reshape(RANK, 3 * 2 * RANK)

    r_t, r_m, r_n, r_l, r_tu = d_t, d_m, d_n, d_l, d_tu
    sol_t = jnp.zeros_like(d_t)
    sol_m = jnp.zeros_like(d_m)
    sol_n = jnp.zeros_like(d_n)
    sol_l = jnp.zeros_like(d_l)
    sol_tu = jnp.zeros_like(d_tu)
    gathered = ab2[:, :HALF].reshape(tall, 2 * RANK)
    stage = 10
    rounds = ((zp2, zb2, zm2, zg2, p3, rb3), (zp3, zb3, zm3, zg3, p4, rb4))
    sub8 = lax.broadcasted_iota(jnp.int32, (8, 2 * RANK), 0)
    d_gm, d_gn = gauss(d_m, d_n)
    r_gm, r_gn = d_gm, d_gn
    for turn, (zp, zb, zm, zg, p, rb) in enumerate(rounds):
        image_part(gathered, d_tu, zp)
        full = line_sum(zp, zb, zm, zg, stage)
        i_t = full[:, :WIDE] + mu * d_t
        cross = full[:, WIDE : WIDE + RANK]
        p[:, :HALF] = apply(i_t, x_a, x_b, True)
        sums = [total(d_t * i_t), total(r_t * i_t), total(i_t * i_t), total(r_t * r_t)]
        note = jnp.zeros((8, 2 * RANK), F32)
        for at, value in enumerate(sums):
            note = jnp.where(sub8 == at, value, note)
        for j in range(n_plane):
            p[j, HALF:] = note
        rb[me] = p[me]
        plane_send(lambda j, p=p: p.at[j], rb, stage + 2)
        i_m = sr2 * exact(d_m, s_l) + mu * d_m
        i_n = sr2 * (cross + exact(d_n, s_l)) + mu * d_n
        i_gm, i_gn = gauss(i_m, i_n)
        i_tu = exact(i_m, zu, TN) + exact(i_n, g, TN)
        di = total(d_m * i_gm + d_n * i_gn)
        ri = total(r_m * i_gm + r_n * i_gn)
        ii = total(i_m * i_gm + i_n * i_gn)
        r_r = total(r_m * r_gm + r_n * r_gn)
        arrived(rb, stage + 2)
        s = jnp.sum(rb[...], axis=0)
        i_l = s[:HALF] * sd
        di = di + s[HALF : HALF + 1, :1]
        ri = ri + s[HALF + 1 : HALF + 2, :1]
        ii = ii + s[HALF + 2 : HALF + 3, :1]
        r_r = r_r + s[HALF + 3 : HALF + 4, :1]
        alpha = r_r / di
        rr = r_r - 2.0 * alpha * ri + alpha * alpha * ii
        beta = rr / r_r
        sol_l = sol_l + alpha * d_l
        r_l = r_l - alpha * i_l
        d_l = r_l + beta * d_l
        sol_tu = sol_tu + alpha * d_tu
        r_tu = r_tu - alpha * i_tu
        d_tu = r_tu + beta * d_tu
        if turn == 0:
            am3[...] = d_l.astype(BF16)
            ab3[me] = am3[...]
            plane_send(lambda j: am3, ab3, stage + 3)
        sol_t, sol_m, sol_n = sol_t + alpha * d_t, sol_m + alpha * d_m, sol_n + alpha * d_n
        r_t, r_m, r_n = r_t - alpha * i_t, r_m - alpha * i_m, r_n - alpha * i_n
        r_gm, r_gn = r_gm - alpha * i_gm, r_gn - alpha * i_gn
        d_t, d_m, d_n = r_t + beta * d_t, r_m + beta * d_m, r_n + beta * d_n
        d_gm, d_gn = r_gm + beta * d_gm, r_gn + beta * d_gn
        if turn == 0:
            arrived(ab3, stage + 3)
            gathered = ab3[...].reshape(tall, 2 * RANK)
        stage += 4

    lb = d_l.astype(BF16).astype(F32)
    tu_diag = jnp.concatenate([exact(d_tu, put_l), exact(d_tu, put_r)], axis=0)
    quad = sr2 * own_wl * lb * (exact(lb, g_diag) + 2.0 * exact(low_p, tu_diag))
    curve = total(quad) + (mu / n_line) * total(d_t * d_t)

    def diag(m, dims=NN):
        del dims
        return jnp.concatenate([exact(m, put_l), exact(m, put_r)], axis=0)

    def diag_t(m):
        return jnp.concatenate([exact(m, put_l, TN), exact(m, put_r, TN)], axis=0)

    hot_l = exact(hot, put_l)
    hot_r = exact(hot, put_r)
    left32 = left_half[:HALF]

    def by_domain(l_v, m, n, tu, to):
        q = l_v * eu_p + low_p * (exact(oz_p, diag(m)) + exact(ou_p, diag(n)) + sr * exact(low_p, diag_t(tu)))
        q_left = jnp.where(left32, q, 0.0)
        q_right = jnp.where(left32, 0.0, q)
        return exact(q_left, to[:HALF], TN) + exact(q_right, to[HALF:], TN)

    by = by_domain(sol_l.astype(BF16).astype(F32), sol_m, sol_n, sol_tu, hot_l)
    by = by + by_domain(lb, d_m, d_n, d_tu, hot_r)
    hyper = sr * jnp.sum(by, axis=0, keepdims=True)
    fm[...] = jnp.where(sub8 == 0, hyper, jnp.where(sub8 == 1, curve, 0.0))
    fb[me] = fm[...]
    plane_send(lambda j: fm, fb, stage)

    up_s = exact(sol_m, z_t, TN) + exact(sol_n, c_t, TN)
    up_d = exact(d_m, z_t, TN) + exact(d_n, c_t, TN)
    pair_out[0] = jnp.concatenate([sol_t, up_s], axis=0).T
    pair_out[1] = jnp.concatenate([d_t, up_d], axis=0).T

    @pl.when(paired)
    def _():
        remote(pair_out, pair_in, stage + 2, partner).start()

    @pl.when(jnp.logical_not(paired))
    def _():
        pair_in[...] = pair_out[...]

    fixed = sr2 * total(exact(d_m, s_l) * d_gm + exact(d_n, s_l) * d_gn) + mu * total(d_m * d_gm + d_n * d_gn)
    arrived(fb, stage)
    fq[...] = jnp.sum(fb[...], axis=0)
    fz[z] = fq[...]
    line_send(lambda k: fq, fz, stage + 1)
    arrived(fz, stage + 1)
    last = jnp.sum(fz[...], axis=0)
    step = rr / (last[1:2, :1] + fixed)
    hyp = -kappa * (last + step * pltpu.roll(last, RANK, 1))
    hyp_out[...] = hyp[:1, :RANK]

    @pl.when(paired)
    def _():
        remote(pair_out, pair_in, stage + 2, partner).wait()

    sol_out[...] = pair_in[0] + step * pair_in[1]

    for s, buf in (
        (1, xs), (2, os_), (3, wg), (4, rb1), (5, ab1), (6, zb1), (7, zg1), (8, rb2), (9, ab2),
        (10, zb2), (11, zg2), (12, rb3), (13, ab3), (14, zb3), (15, zg3), (16, rb4), (18, fb), (19, fz),
    ):
        left(buf, s)


def solution(mesh, xc=8, z_lo=2):
    n_dp, n_fsdp = mesh.shape["dp"], mesh.shape["fsdp"]
    n_plane = (n_dp // z_lo) * xc
    n_line = (n_fsdp // xc) * z_lo
    blocks = min(8, n_plane)
    geo = (n_plane, n_line, xc, z_lo, blocks)
    blk = RANK // blocks
    chunk = RANK // n_line
    two = 2 * RANK
    vm = pltpu.VMEM

    def exchange(rows, kind=F32):
        return [vm((n_plane, rows, two), F32), vm((n_plane, rows, two), F32)] if kind is F32 else [
            vm((rows, two), BF16), vm((n_plane, rows, two), BF16)]

    def line(*shape):
        return [vm((n_line, *shape), F32), vm(shape, F32), vm((n_line, *shape), F32)]

    scratch = [
        vm((n_plane, TOK, WIDE), BF16), vm((n_plane, TOK, WIDE), BF16), vm((WIDE, two), BF16), vm((n_plane, TOK, two), F32),
        *exchange(TOK + blk), *exchange(TOK + 2 * blk, BF16),
        vm((3, n_line, chunk, WIDE), F32), *line(3, chunk, WIDE),
        *exchange(TOK + blk), *exchange(HALF + 2 * blk, BF16),
        vm((n_line, chunk, 3 * two), F32), *line(chunk, 3 * two),
        *exchange(HALF + 8), *exchange(HALF, BF16),
        vm((n_line, chunk, 3 * two), F32), *line(chunk, 3 * two),
        *exchange(HALF + 8),
        vm((8, two), F32), vm((n_plane, 8, two), F32), vm((n_line, 8, two), F32), vm((8, two), F32),
        vm((2, WIDE, two), F32), vm((2, WIDE, two), F32),
        pltpu.SemaphoreType.DMA((21,)), pltpu.SemaphoreType.DMA((21,)), pltpu.SemaphoreType.DMA((3,)),
    ]
    anywhere = pl.BlockSpec(memory_space=pl.ANY)
    inside = pl.BlockSpec(memory_space=pltpu.VMEM)

    def on_device(x, o, cat, coef, learn, held):
        sol, hyp = pl.pallas_call(
            functools.partial(kernel, geo),
            out_shape=(
                jax.ShapeDtypeStruct((WIDE, two), F32),
                jax.ShapeDtypeStruct((1, RANK), F32),
            ),
            in_specs=[anywhere, anywhere, inside, anywhere, inside, inside],
            out_specs=(inside, inside),
            scratch_shapes=scratch,
            compiler_params=pltpu.CompilerParams(
                collective_id=0, has_side_effects=True, vmem_limit_bytes=56 * 1024 * 1024
            ),
        )(x, o, cat.reshape(1, TOK), coef, learn.reshape(1, DOMAINS), held.reshape(1, DOMAINS))
        return sol, hyp.reshape(DOMAINS)

    placed = (P(("dp", "fsdp"), None), P(("dp", "fsdp"), None), P(("dp", "fsdp")), P("fsdp", None), P(), P())
    return jax.shard_map(
        on_device, mesh=mesh, in_specs=placed, out_specs=(P("fsdp", None), P()), check_vma=False
    )
```

```python
import functools

import jax
import jax.numpy as jnp
from jax import lax
from jax.experimental import pallas as pl
from jax.experimental.pallas import tpu as pltpu
from jax.sharding import PartitionSpec as P

MESH = pl.DeviceIdType.MESH
HIGH = lax.Precision.HIGHEST
RANK = 64
DOMAINS = 64
TOK = 64
HALF = 32
WIDE = 256
F32 = jnp.float32
BF16 = jnp.bfloat16
NN = (((1,), (0,)), ((), ()))
NT = (((1,), (1,)), ((), ()))
TN = (((0,), (0,)), ((), ()))


def mm(a, b, dims=NN):
    return lax.dot_general(a, b, dims, preferred_element_type=F32)


def exact(a, b, dims=NN):
    return lax.dot_general(a, b, dims, precision=HIGH, preferred_element_type=F32)


def split(v):
    hi = v.astype(BF16)
    return hi, (v - hi.astype(F32)).astype(BF16)


def mm2(a, v, dims=NN):
    hi, lo = split(v)
    return mm(a, hi, dims) + mm(a, lo, dims)


def total(v):
    return jnp.sum(v, axis=(0, 1), keepdims=True)


def kernel(geo, x, o, cat, coef, tl, th, sol_out, hyp_out, *scratch):
    n_plane, n_line, xc, z_lo, blocks, n_sem = geo
    (
        xs, os_, cf, wg,
        po1, sa1, pc1, rb1, am1, ab1, zp1, zb1, zm1, zg1, zp1b, zb1b, zm1b, zg1b,
        po2, sa2, pc2, rb2, am2, ab2, zp2, zb2, zm2, zg2, pz, rz,
        po3, sa3, pc3, rb3, am3, ab3, zp3, zb3, zm3, zg3,
        po4, sa4, pc4, rb4, fm, fb, fq, fz, pair_out, pair_in, send, recv, local,
    ) = scratch
    n_chip = n_plane // 2
    nx = xc // 2
    rows_blk = RANK // blocks
    width = n_plane * WIDE
    rows = n_plane * n_line * TOK
    sd = width ** (-0.5)
    sr = RANK ** (-0.5)
    sr2 = 1.0 / RANK
    kappa = DOMAINS / (rows * width)
    mu = 0.1 * DOMAINS / (width * RANK)
    tall = n_plane * HALF
    two = 2 * RANK
    chunk = RANK // n_line

    dp = lax.axis_index("dp")
    fs = lax.axis_index("fsdp")
    y = lax.div(dp, z_lo)
    low_z = lax.rem(dp, z_lo)
    z_hi = lax.div(fs, xc)
    col = lax.rem(fs, xc)
    core = lax.rem(col, 2)
    chip = y * nx + lax.div(col, 2)
    me = core * n_chip + chip
    z = z_hi * z_lo + low_z

    def at_chip(q, which):
        return (lax.div(q, nx) * z_lo + low_z, z_hi * xc + lax.rem(q, nx) * 2 + which)

    def in_plane(j):
        return at_chip(lax.rem(j, n_chip), lax.div(j, n_chip))

    def in_line(k):
        return (y * z_lo + lax.rem(k, z_lo), lax.div(k, z_lo) * xc + col)

    def shard(j):
        q = lax.rem(j, n_chip)
        return lax.div(q, nx) * xc + lax.rem(q, nx) * 2 + lax.div(j, n_chip)

    partner = (z_hi * z_lo + low_z, y * xc + col)
    paired = y != z_hi
    alone = jnp.logical_not(paired)

    used = [0]

    def fresh():
        used[0] += 1
        assert used[0] <= n_sem
        return used[0] - 1

    sent = []

    def columns(ref, j):
        return ref.at[:, pl.ds(pl.multiple_of(shard(j) * WIDE, WIDE), WIDE)]

    own_x = pltpu.make_async_copy(columns(x, me), xs.at[me], local.at[0])
    own_o = pltpu.make_async_copy(columns(o, me), os_.at[me], local.at[1])
    own_x.start()
    own_o.start()

    barrier = pltpu.get_barrier_semaphore()

    def greet(i, c):
        pl.semaphore_signal(barrier, inc=1, device_id=in_plane(lax.rem(me + i, n_plane)), device_id_type=MESH)
        return c

    def greet_line(i, c):
        pl.semaphore_signal(barrier, inc=1, device_id=in_line(lax.rem(z + i, n_line)), device_id_type=MESH)
        return c

    lax.fori_loop(1, n_plane, greet, 0)
    lax.fori_loop(1, n_line, greet_line, 0)

    @pl.when(paired)
    def _():
        pl.semaphore_signal(barrier, inc=1, device_id=partner, device_id_type=MESH)

    sub = lax.broadcasted_iota(jnp.int32, (RANK, RANK), 0)
    lan = lax.broadcasted_iota(jnp.int32, (RANK, RANK), 1)
    eye = (sub == lan).astype(F32)
    sub2 = lax.broadcasted_iota(jnp.int32, (RANK, two), 0)
    lan2 = lax.broadcasted_iota(jnp.int32, (RANK, two), 1)
    put_l = (lan2 == sub2).astype(F32)
    put_r = (lan2 == sub2 + RANK).astype(F32)
    left_half = lan2 < RANK
    left32 = left_half[:HALF]
    sub8 = lax.broadcasted_iota(jnp.int32, (8, two), 0)
    hot_t = (cat[...] == sub).astype(F32)
    row_w = exact(exact(tl[...], hot_t), put_l) + exact(exact(th[...], hot_t), put_r)
    wg[me] = jnp.broadcast_to(row_w * kappa, (8, two))

    @pl.when(paired)
    def _():
        pl.semaphore_wait(barrier, n_plane + n_line - 1)

    @pl.when(alone)
    def _():
        pl.semaphore_wait(barrier, n_plane + n_line - 2)

    def remote(src, dst, s, device):
        return pltpu.make_async_remote_copy(
            src_ref=src, dst_ref=dst, send_sem=send.at[s], recv_sem=recv.at[s], device_id=device, device_id_type=MESH
        )

    def plane_send(src_of, dst, s):
        def body(i, c):
            j = lax.rem(me + i, n_plane)
            remote(src_of(j), dst.at[me], s, in_plane(j)).start()
            return c

        lax.fori_loop(1, n_plane, body, 0)
        sent.append((dst, n_plane - 1, s))

    def chip_send(src_of, dst, slot, s):
        def body(i, c):
            q = lax.rem(chip + i, n_chip)
            remote(src_of(q), dst.at[slot], s, at_chip(q, core)).start()
            return c

        lax.fori_loop(1, n_chip, body, 0)
        sent.append((dst, n_chip - 1, s))

    def line_send(src_of, dst, s):
        def body(i, c):
            k = lax.rem(z + i, n_line)
            remote(src_of(k), dst.at[z], s, in_line(k)).start()
            return c

        lax.fori_loop(1, n_line, body, 0)
        sent.append((dst, n_line - 1, s))

    def sib_send(src, dst, s):
        remote(src, dst, s, at_chip(chip, 1 - core)).start()
        sent.append((dst, n_chip, s))

    def wait_for(buf, n, sem):
        part = buf.at[pl.ds(0, n)]
        pltpu.make_async_copy(part, part, sem).wait()

    def arrived(buf, n, s):
        wait_for(buf, n, recv.at[s])

    def sum_start(make, po, sa, pc, rb):
        s, t = fresh(), fresh()
        po[...] = make(1 - core)
        sib_send(po, sa, s)
        mine = make(core)
        arrived(sa, n_chip, s)
        pc[...] = mine + sa[...]
        rb[chip] = pc[chip]
        chip_send(lambda q: pc.at[q], rb, chip, t)
        return t

    def sum_end(rb, t):
        arrived(rb, n_chip - 1, t)
        return jnp.sum(rb[...], axis=0)

    def line_start(zp, zb):
        s = fresh()
        zb[z] = zp[z]
        line_send(lambda k: zp.at[k], zb, s)
        return s

    def line_mid(zb, zm, zg, s):
        t = fresh()
        arrived(zb, n_line - 1, s)
        zm[...] = jnp.sum(zb[...], axis=0)
        zg[z] = zm[...]
        line_send(lambda k: zm, zg, t)
        return t

    s_c, s_w, s_x, s_o = fresh(), fresh(), fresh(), fresh()

    @pl.when(paired)
    def _():
        remote(coef, cf, s_c, partner).start()

    plane_send(lambda j: wg.at[me], wg, s_w)
    plane_send(lambda j: columns(x, j), xs, s_x)
    plane_send(lambda j: columns(o, j), os_, s_o)

    n8 = HALF // 8
    deep = 8 * lax.broadcasted_iota(jnp.int32, (n8, 8, two), 0) + lax.broadcasted_iota(jnp.int32, (n8, 8, two), 1)
    wide = lax.broadcasted_iota(jnp.int32, (n8, 8, two), 2)
    big_l = lax.broadcasted_iota(jnp.int32, (two, two), 1) < RANK
    ones_l = big_l.astype(BF16)
    ones_r = jnp.logical_not(big_l).astype(BF16)

    def packed(v, base):
        n = v.shape[0]
        out = None
        for shift, ones in ((0, ones_l), (HALF, ones_r)):
            mask = (wide == deep + (base + shift)).astype(F32)
            picked = (v[:, None] * mask[None]).reshape(n * HALF, two)
            for part in split(picked):
                t = mm(part, ones)
                out = t if out is None else out + t
        return out

    own_wl = packed(wg[pl.ds(me, 1)], 0)

    @pl.when(paired)
    def _():
        remote(coef, cf, s_c, partner).wait()

    @pl.when(alone)
    def _():
        own_c = pltpu.make_async_copy(coef, cf, local.at[2])
        own_c.start()
        own_c.wait()

    c = cf[...]
    lanes_c = lax.broadcasted_iota(jnp.int32, c.shape, 1)
    zero_c = jnp.zeros_like(c)
    c_low = jnp.where(lanes_c < RANK, c, zero_c)
    c_up = jnp.where(lanes_c >= RANK, c, zero_c)
    gram = mm(c, c, TN)[RANK:]
    gram = jnp.concatenate([gram.reshape(blocks, rows_blk, two)] * (n_chip // blocks), axis=0)
    c_t = exact(put_r, c.astype(F32), NT)

    arrived(wg, n_plane - 1, s_w)
    wlp = packed(wg[...], 0)
    whp = packed(wg[...], RANK)

    own_x.wait()
    arrived(xs, n_plane - 1, s_x)
    own_o.wait()
    arrived(os_, n_plane - 1, s_o)

    def half_of(ref, which):
        return ref[pl.ds(which * n_chip, n_chip)]

    def first(which):
        v = mm(half_of(xs, which).reshape(n_chip * TOK, WIDE), c_low)
        v = v + mm(half_of(os_, which).reshape(n_chip * TOK, WIDE), c_up)
        return jnp.concatenate([v.reshape(n_chip, TOK, two), gram], axis=1)

    t1 = sum_start(first, po1, sa1, pc1, rb1)

    def spread(v, at):
        return jnp.broadcast_to(v[:, at : at + 1], (tall, two))

    s1 = sum_end(rb1, t1)
    f_own = jnp.where(left_half, (s1[:TOK] * sd).astype(BF16).astype(F32), s1[:TOK])
    g_hi, g_lo = split(s1[TOK:])
    am1[...] = jnp.concatenate([f_own, g_hi.astype(F32), g_lo.astype(F32)], axis=0).astype(BF16)
    ab1[me] = am1[...]
    s_g, s_h2 = fresh(), fresh()
    chip_send(lambda q: am1, ab1, me, s_g)
    nought = jnp.zeros_like(put_l)
    e_top = jnp.concatenate([put_l, nought], axis=0)
    e_top_r = jnp.concatenate([put_r, nought], axis=0)
    e_bot = jnp.concatenate([nought, put_l], axis=0)
    e_bot_r = jnp.concatenate([nought, put_r], axis=0)
    low_p = exact(f_own[:HALF], e_top) + exact(f_own[HALF:], e_top_r)
    ou_p = exact(f_own[:HALF], e_bot) + exact(f_own[HALF:], e_bot_r)
    hot = exact(hot_t, eye, TN)
    hot_l = exact(hot, put_l)
    hot_r = exact(hot, put_r)
    arrived(ab1, n_chip - 1, s_g)
    mine_half = ab1.at[pl.ds(core * n_chip, n_chip)]
    sib_send(mine_half, mine_half, s_h2)
    arrived(ab1, n_chip, s_h2)

    g_wide = []
    for b in range(blocks):
        v = ab1[b, TOK:].astype(F32)
        g_wide.append(v[:rows_blk] + v[rows_blk:])
    g_wide = jnp.concatenate(g_wide, axis=0)
    g_right = jnp.where(left_half, 0.0, g_wide)
    g_left = pltpu.roll(g_right, RANK, 1)
    g = g_left[:, :RANK]
    g_diag = jnp.concatenate([g_left, g_right], axis=0)
    f_a = ab1[:, :HALF].reshape(tall, two)
    f_b = ab1[:, HALF:TOK].reshape(tall, two)
    k_l = jnp.concatenate([g_left * sr2, put_l * sr], axis=0)
    k_r = jnp.concatenate([g_right * sr2, put_r * sr], axis=0)
    p0 = (whp * (mm2(f_a, k_l) + mm2(f_b, k_r))).astype(BF16)
    x_a = xs[:, :HALF].reshape(tall, WIDE)
    x_b = xs[:, HALF:].reshape(tall, WIDE)
    o_a = os_[:, :HALF].reshape(tall, WIDE)
    o_b = os_[:, HALF:].reshape(tall, WIDE)

    def fold(v, a, b):
        return mm(v, a, TN)[:RANK] + mm(v, b, TN)[RANK:]

    zp1[...] = (fold(p0, x_a, x_b) * sd).reshape(n_line, chunk, WIDE)
    s_r = line_start(zp1, zb1)
    wfh_a = (f_a.astype(F32) * spread(whp, 0)).astype(BF16)
    wfh_b = (f_b.astype(F32) * spread(whp, RANK)).astype(BF16)
    wfl_a = (f_a.astype(F32) * spread(wlp, 0)).astype(BF16)
    wfl_b = (f_b.astype(F32) * spread(wlp, RANK)).astype(BF16)
    zp1b[:, 0] = (mm(wfh_a, o_a, TN)[:RANK] + mm(wfh_b, o_b, TN)[:RANK]).reshape(n_line, chunk, WIDE)
    q_h = mm(f_a, wfh_a, TN)[:RANK] + mm(f_b, wfh_b, TN)[:RANK]
    q_l = mm(f_a, wfl_a, TN)[:RANK] + mm(f_b, wfl_b, TN)[:RANK]
    zp1b[:, 1] = jnp.concatenate([q_h, q_l], axis=1).reshape(n_line, chunk, WIDE)
    s_q = line_start(zp1b, zb1b)
    s_r = line_mid(zb1, zm1, zg1, s_r)
    s_q = line_mid(zb1b, zm1b, zg1b, s_q)
    eu_p = ou_p + sr * exact(low_p, g_diag)
    arrived(zg1, n_line - 1, s_r)

    d_t = zg1[...].reshape(RANK, WIDE)
    nil = jnp.zeros((RANK, WIDE), BF16)

    def apply(v, ref, which, both):
        part = half_of(ref, which)
        a = part[:, :HALF].reshape(n_chip * HALF, WIDE)
        b = part[:, HALF:].reshape(n_chip * HALF, WIDE)
        out = None
        for piece in split(v) if both else (v.astype(BF16),):
            t = mm(a, jnp.concatenate([piece, nil], axis=0), NT) + mm(b, jnp.concatenate([nil, piece], axis=0), NT)
            out = t if out is None else out + t
        return out.reshape(n_chip, HALF, two)

    t2 = sum_start(lambda which: apply(d_t, xs, which, True), po2, sa2, pc2, rb2)
    arrived(zg1b, n_line - 1, s_q)
    z_t = zg1b[:, 0].reshape(RANK, WIDE)
    stats = zg1b[:, 1].reshape(RANK, WIDE)
    s_h = stats[:, :RANK]
    zu = pltpu.roll(stats[:, :two], RANK, 1)[:, :RANK]
    s_l = stats[:, two : two + RANK]
    d_m = eye * sr
    d_n = s_h * sr2
    d_tu = exact(d_m, zu, TN) + exact(d_n, g, TN)

    pair_sems = [fresh(), fresh(), fresh()]

    def hand_over(k, down, m, n):
        up = exact(m, z_t, TN) + exact(n, c_t, TN)
        pair_out[k] = jnp.concatenate([down, up], axis=0).T

        @pl.when(paired)
        def _():
            remote(pair_out.at[k], pair_in.at[k], pair_sems[k], partner).start()

        @pl.when(alone)
        def _():
            pair_in[k] = pair_out[k]

    d_l = sum_end(rb2, t2) * sd
    am2[...] = d_l.astype(BF16)
    ab2[me] = am2[...]
    s_a = fresh()
    plane_send(lambda j: am2, ab2, s_a)
    pz[:n_chip, :HALF] = apply(z_t, os_, 0, False).astype(BF16)
    pz[n_chip:, :HALF] = apply(z_t, os_, 1, False).astype(BF16)
    zz_part = exact(z_t, z_t, NT)
    zz_hi, zz_lo = split(zz_part)
    zz_both = (exact(zz_hi.astype(F32), put_l) + exact(zz_lo.astype(F32), put_r)).astype(BF16)
    pz[:, HALF:] = jnp.broadcast_to(zz_both[None], (n_plane, RANK, two))
    arrived(ab2, n_plane - 1, s_a)
    gathered = ab2[...].reshape(tall, two)

    def image_part(l_p, tu, zp):
        tu_l = jnp.concatenate([exact(tu, put_l), nought], axis=0)
        tu_r = jnp.concatenate([exact(tu, put_r), nought], axis=0)
        inner = mm2(l_p, g_diag) + mm2(f_a, tu_l) + mm2(f_b, tu_r)
        y_p = (wlp * sr2 * inner).astype(BF16)
        down = fold(y_p, x_a, x_b) * sd
        cross = fold(l_p, wfl_a, wfl_b)
        zp[...] = jnp.concatenate([down, cross], axis=1).reshape(n_line, chunk, 3 * two)

    def gauss(m, n):
        return exact(zz, m) + exact(zu, n), exact(zu, m, TN) + exact(g, n)

    def diag(m):
        return jnp.concatenate([exact(m, put_l), exact(m, put_r)], axis=0)

    def diag_t(m):
        return jnp.concatenate([exact(m, put_l, TN), exact(m, put_r, TN)], axis=0)

    def up_rows(m, n, tu):
        return low_p * (exact(oz_p, diag(m)) + exact(ou_p, diag(n)) + sr * exact(low_p, diag_t(tu)))

    def by_domain(q, to):
        q_left = jnp.where(left32, q, 0.0)
        q_right = jnp.where(left32, 0.0, q)
        by = exact(q_left, to[:HALF], TN) + exact(q_right, to[HALF:], TN)
        return sr * jnp.sum(by, axis=0, keepdims=True)

    r_t, r_m, r_n, r_l, r_tu = d_t, d_m, d_n, d_l, d_tu
    first_l, first_m, first_n, first_tu = d_l, d_m, d_n, d_tu
    rounds = (
        (zp2, zb2, zm2, zg2, po3, sa3, pc3, rb3), (zp3, zb3, zm3, zg3, po4, sa4, pc4, rb4),
    )
    steps = []
    for turn, (zp, zb, zm, zg, po, sa, pc, rb) in enumerate(rounds):
        image_part(gathered, d_tu, zp)
        s_z = line_start(zp, zb)
        if turn == 0:
            s_pz = fresh()
            rz[me] = pz[me]
            plane_send(lambda j: pz.at[j], rz, s_pz)
            hand_over(0, d_t, d_m, d_n)
        s_z = line_mid(zb, zm, zg, s_z)
        arrived(zg, n_line - 1, s_z)
        full = zg[...].reshape(RANK, 3 * two)
        i_t = full[:, :WIDE] + mu * d_t
        cross = full[:, WIDE : WIDE + RANK]
        note = jnp.zeros((8, two), F32)
        for at, value in enumerate((total(d_t * i_t), total(r_t * i_t), total(i_t * i_t), total(r_t * r_t))):
            note = jnp.where(sub8 == at, value, note)

        def third(which, i_t=i_t, note=note):
            return jnp.concatenate(
                [apply(i_t, xs, which, True), jnp.broadcast_to(note[None], (n_chip, 8, two))], axis=1
            )

        t3 = sum_start(third, po, sa, pc, rb)
        if turn == 0:
            arrived(rz, n_plane - 1, s_pz)
            late = jnp.sum(rz[...].astype(F32), axis=0)
            oz_p = late[:HALF]
            zz = (late[HALF:] + pltpu.roll(late[HALF:], RANK, 1))[:, :RANK]
            d_gm, d_gn = gauss(d_m, d_n)
            r_gm, r_gn = d_gm, d_gn
        i_m = sr2 * exact(d_m, s_l) + mu * d_m
        i_n = sr2 * (cross + exact(d_n, s_l)) + mu * d_n
        i_gm, i_gn = gauss(i_m, i_n)
        i_tu = exact(i_m, zu, TN) + exact(i_n, g, TN)
        di = total(d_m * i_gm + d_n * i_gn)
        ri = total(r_m * i_gm + r_n * i_gn)
        ii = total(i_m * i_gm + i_n * i_gn)
        r_r = total(r_m * r_gm + r_n * r_gn)
        if turn == 0:
            second_up = up_rows(i_m, i_n, i_tu)
            first_by = by_domain(first_l * eu_p + up_rows(first_m, first_n, first_tu), hot_l)
        else:
            third_up = up_rows(i_m, i_n, i_tu)
            r_lt = exact(low_p, diag(r_tu))
            d_lt = exact(low_p, diag(d_tu))
            i_lt = exact(low_p, diag(i_tu))
            hand_over(2, i_t, i_m, i_n)
        s = sum_end(rb, t3)
        i_l = s[:HALF] * sd
        di = di + s[HALF : HALF + 1, :1]
        ri = ri + s[HALF + 1 : HALF + 2, :1]
        ii = ii + s[HALF + 2 : HALF + 3, :1]
        r_r = r_r + s[HALF + 3 : HALF + 4, :1]
        alpha = r_r / di
        rr = r_r - 2.0 * alpha * ri + alpha * alpha * ii
        beta = rr / r_r
        steps.append((alpha, beta))
        r_l = r_l - alpha * i_l
        d_l = r_l + beta * d_l
        if turn == 0:
            am3[...] = d_l.astype(BF16)
            ab3[me] = am3[...]
            s_a = fresh()
            plane_send(lambda j: am3, ab3, s_a)
            second_by = by_domain(i_l * eu_p + second_up, hot_r)
            r_tu = r_tu - alpha * i_tu
            d_tu = r_tu + beta * d_tu
            hand_over(1, i_t, i_m, i_n)
        else:
            d_lt = r_lt - alpha * i_lt + beta * d_lt
            third_by = by_domain(i_l * eu_p + third_up, hot_l)
        r_t, r_m, r_n = r_t - alpha * i_t, r_m - alpha * i_m, r_n - alpha * i_n
        d_t, d_m, d_n = r_t + beta * d_t, r_m + beta * d_m, r_n + beta * d_n
        r_gm, r_gn = r_gm - alpha * i_gm, r_gn - alpha * i_gn
        d_gm, d_gn = r_gm + beta * d_gm, r_gn + beta * d_gn
        if turn == 0:
            arrived(ab3, n_plane - 1, s_a)
            gathered = ab3[...].reshape(tall, two)

    d_lb = d_l.astype(BF16)
    quad = sr2 * own_wl * d_lb.astype(F32) * (mm2(d_lb, g_diag) + 2.0 * d_lt)
    curve = total(quad) + (mu / n_line) * total(d_t * d_t)
    s_f, s_l2 = fresh(), fresh()
    fm[...] = jnp.where(
        sub8 == 0, first_by + second_by, jnp.where(sub8 == 1, third_by, jnp.where(sub8 == 2, curve, 0.0))
    )
    fb[me] = fm[...]
    plane_send(lambda j: fm, fb, s_f)
    fixed = sr2 * total(exact(d_m, s_l) * d_gm + exact(d_n, s_l) * d_gn) + mu * total(d_m * d_gm + d_n * d_gn)
    arrived(fb, n_plane - 1, s_f)
    fq[...] = jnp.sum(fb[...], axis=0)
    fz[z] = fq[...]
    line_send(lambda k: fq, fz, s_l2)
    (a0, b0), (a1, b1) = steps
    for k in range(3):
        @pl.when(paired)
        def _(k=k):
            remote(pair_out.at[k], pair_in.at[k], pair_sems[k], partner).wait()

    for buf, n, s in sent[:-1]:
        wait_for(buf, n, send.at[s])
    arrived(fz, n_line - 1, s_l2)
    last = jnp.sum(fz[...], axis=0)
    a2 = rr / (last[2:3, :1] + fixed)
    w0 = a0 + a1 * (1.0 + b0) + a2 * (1.0 + b1 * (1.0 + b0))
    w1 = -a0 * (a1 + a2 * (1.0 + b1))
    w2 = -a1 * a2
    hyp = w0 * last[:1] + w1 * pltpu.roll(last, RANK, 1)[:1] + w2 * last[1:2]
    hyp_out[...] = -kappa * hyp[:, :RANK]
    sol_out[...] = w0 * pair_in[0] + w1 * pair_in[1] + w2 * pair_in[2]
    buf, n, s = sent[-1]
    wait_for(buf, n, send.at[s])


def solution(mesh, xc=8, z_lo=2):
    n_dp, n_fsdp = mesh.shape["dp"], mesh.shape["fsdp"]
    n_plane = (n_dp // z_lo) * xc
    n_line = (n_fsdp // xc) * z_lo
    n_chip = n_plane // 2
    blocks = min(8, n_chip)
    n_sem = 40
    geo = (n_plane, n_line, xc, z_lo, blocks, n_sem)
    blk = RANK // blocks
    chunk = RANK // n_line
    two = 2 * RANK
    vm = pltpu.VMEM

    def sums(rows):
        return [vm((n_chip, rows, two), F32)] * 4

    def gather(rows):
        return [vm((rows, two), BF16), vm((n_plane, rows, two), BF16)]

    def line(*shape):
        return [vm((n_line, *shape), F32), vm((n_line, *shape), F32), vm(shape, F32), vm((n_line, *shape), F32)]

    late = vm((n_plane, HALF + RANK, two), BF16)
    scratch = [
        vm((n_plane, TOK, WIDE), BF16), vm((n_plane, TOK, WIDE), BF16), vm((WIDE, two), BF16), vm((n_plane, 8, two), F32),
        *sums(TOK + blk), *gather(TOK + 2 * blk), *line(chunk, WIDE), *line(2, chunk, WIDE),
        *sums(HALF), *gather(HALF), *line(chunk, 3 * two), late, late,
        *sums(HALF + 8), *gather(HALF), *line(chunk, 3 * two),
        *sums(HALF + 8),
        vm((8, two), F32), vm((n_plane, 8, two), F32), vm((8, two), F32), vm((n_line, 8, two), F32),
        vm((3, WIDE, two), F32), vm((3, WIDE, two), F32),
        pltpu.SemaphoreType.DMA((n_sem,)), pltpu.SemaphoreType.DMA((n_sem,)), pltpu.SemaphoreType.DMA((3,)),
    ]
    anywhere = pl.BlockSpec(memory_space=pl.ANY)
    inside = pl.BlockSpec(memory_space=pltpu.VMEM)

    def on_device(x, o, cat, coef, learn, held):
        sol, hyp = pl.pallas_call(
            functools.partial(kernel, geo),
            out_shape=(
                jax.ShapeDtypeStruct((WIDE, two), F32),
                jax.ShapeDtypeStruct((1, RANK), F32),
            ),
            in_specs=[anywhere, anywhere, inside, anywhere, inside, inside],
            out_specs=(inside, inside),
            scratch_shapes=scratch,
            compiler_params=pltpu.CompilerParams(
                collective_id=0, has_side_effects=True, vmem_limit_bytes=56 * 1024 * 1024
            ),
        )(x, o, cat.reshape(1, TOK), coef, learn.reshape(1, DOMAINS), held.reshape(1, DOMAINS))
        return sol, hyp.reshape(DOMAINS)

    placed = (P(("dp", "fsdp"), None), P(("dp", "fsdp"), None), P(("dp", "fsdp")), P("fsdp", None), P(), P())
    return jax.shard_map(
        on_device, mesh=mesh, in_specs=placed, out_specs=(P("fsdp", None), P()), check_vma=False
    )
```

```python
import functools

import jax
import jax.numpy as jnp
from jax import lax
from jax.experimental import pallas as pl
from jax.experimental.pallas import tpu as pltpu
from jax.sharding import PartitionSpec as P

MESH = pl.DeviceIdType.MESH
HIGH = lax.Precision.HIGHEST
RANK = 64
DOMAINS = 64
TOK = 64
HALF = 32
WIDE = 256
F32 = jnp.float32
BF16 = jnp.bfloat16
NN = (((1,), (0,)), ((), ()))
NT = (((1,), (1,)), ((), ()))
TN = (((0,), (0,)), ((), ()))


def mm(a, b, dims=NN):
    return lax.dot_general(a, b, dims, preferred_element_type=F32)


def exact(a, b, dims=NN):
    return lax.dot_general(a, b, dims, precision=HIGH, preferred_element_type=F32)


def split(v):
    hi = v.astype(BF16)
    return hi, (v - hi.astype(F32)).astype(BF16)


def mm2(a, v, dims=NN):
    hi, lo = split(v)
    return mm(a, hi, dims) + mm(a, lo, dims)


def total(v):
    return jnp.sum(v, axis=(0, 1), keepdims=True)


def kernel(geo, x, o, cat, coef, tl, th, sol_out, hyp_out, *scratch):
    n_plane, n_line, xc, z_lo, n_sem = geo
    (
        xs, os_, ca, wg, xr, orow, am1, ab1, zp1, zb1, zm1, zg1, zp1b, zb1b, zm1b, zg1b,
        po2, sa2, pc2, rb2, am2, ab2, zp2, zb2, zm2, zg2, pz, rz,
        po3, sa3, pc3, rb3, am3, ab3, zp3, zb3, zm3, zg3,
        po4, sa4, pc4, rb4, fm, fb, fq, fz, pair_out, pair_in, send, recv, local,
    ) = scratch
    n_chip = n_plane // 2
    nx = xc // 2
    width = n_plane * WIDE
    rows = n_plane * n_line * TOK
    sd = width ** (-0.5)
    sr = RANK ** (-0.5)
    sr2 = 1.0 / RANK
    kappa = DOMAINS / (rows * width)
    mu = 0.1 * DOMAINS / (width * RANK)
    tall = n_plane * HALF
    two = 2 * RANK
    chunk = RANK // n_line

    dp = lax.axis_index("dp")
    fs = lax.axis_index("fsdp")
    y = lax.div(dp, z_lo)
    low_z = lax.rem(dp, z_lo)
    z_hi = lax.div(fs, xc)
    col = lax.rem(fs, xc)
    core = lax.rem(col, 2)
    chip = y * nx + lax.div(col, 2)
    there = core * n_chip + z_hi * nx + lax.div(col, 2)
    me = core * n_chip + chip
    z = z_hi * z_lo + low_z

    def at_chip(q, which):
        return (lax.div(q, nx) * z_lo + low_z, z_hi * xc + lax.rem(q, nx) * 2 + which)

    def in_plane(j):
        return at_chip(lax.rem(j, n_chip), lax.div(j, n_chip))

    def in_line(k):
        return (y * z_lo + lax.rem(k, z_lo), lax.div(k, z_lo) * xc + col)

    def shard(j):
        q = lax.rem(j, n_chip)
        return lax.div(q, nx) * xc + lax.rem(q, nx) * 2 + lax.div(j, n_chip)

    partner = (z_hi * z_lo + low_z, y * xc + col)
    paired = y != z_hi
    alone = jnp.logical_not(paired)

    used = [0]

    def fresh():
        used[0] += 1
        assert used[0] <= n_sem
        return used[0] - 1

    sent = []

    def columns(ref, j):
        return ref.at[:, pl.ds(pl.multiple_of(shard(j) * WIDE, WIDE), WIDE)]

    own_x = pltpu.make_async_copy(columns(x, me), xs.at[me], local.at[0])
    own_o = pltpu.make_async_copy(columns(o, me), os_.at[me], local.at[1])
    rows_x = pltpu.make_async_copy(x, xr, local.at[2])
    rows_o = pltpu.make_async_copy(o, orow, local.at[3])
    for copy in (rows_x, rows_o, own_x, own_o):
        copy.start()

    barrier = pltpu.get_barrier_semaphore()

    def greet(i, c):
        pl.semaphore_signal(barrier, inc=1, device_id=in_plane(lax.rem(me + i, n_plane)), device_id_type=MESH)
        return c

    def greet_line(i, c):
        pl.semaphore_signal(barrier, inc=1, device_id=in_line(lax.rem(z + i, n_line)), device_id_type=MESH)
        return c

    lax.fori_loop(1, n_plane, greet, 0)
    lax.fori_loop(1, n_line, greet_line, 0)

    @pl.when(paired)
    def _():
        pl.semaphore_signal(barrier, inc=1, device_id=partner, device_id_type=MESH)

    sub = lax.broadcasted_iota(jnp.int32, (RANK, RANK), 0)
    lan = lax.broadcasted_iota(jnp.int32, (RANK, RANK), 1)
    eye = (sub == lan).astype(F32)
    sub2 = lax.broadcasted_iota(jnp.int32, (RANK, two), 0)
    lan2 = lax.broadcasted_iota(jnp.int32, (RANK, two), 1)
    put_l = (lan2 == sub2).astype(F32)
    put_r = (lan2 == sub2 + RANK).astype(F32)
    left_half = lan2 < RANK
    left32 = left_half[:HALF]
    sub8 = lax.broadcasted_iota(jnp.int32, (8, two), 0)
    hot_t = (cat[...] == sub).astype(F32)
    row_w = exact(exact(tl[...], hot_t), put_l) + exact(exact(th[...], hot_t), put_r)
    wg[me] = jnp.broadcast_to(row_w * kappa, (8, two))

    @pl.when(paired)
    def _():
        pl.semaphore_wait(barrier, n_plane + n_line - 1)

    @pl.when(alone)
    def _():
        pl.semaphore_wait(barrier, n_plane + n_line - 2)

    def remote(src, dst, s, device):
        return pltpu.make_async_remote_copy(
            src_ref=src, dst_ref=dst, send_sem=send.at[s], recv_sem=recv.at[s], device_id=device, device_id_type=MESH
        )

    def plane_send(src_of, dst, s):
        def body(i, c):
            j = lax.rem(me + i, n_plane)
            remote(src_of(j), dst.at[me], s, in_plane(j)).start()
            return c

        lax.fori_loop(1, n_plane, body, 0)
        sent.append((dst, n_plane - 1, s))

    def chip_send(src_of, dst, slot, s):
        def body(i, c):
            q = lax.rem(chip + i, n_chip)
            remote(src_of(q), dst.at[slot], s, at_chip(q, core)).start()
            return c

        lax.fori_loop(1, n_chip, body, 0)
        sent.append((dst, n_chip - 1, s))

    def line_send(src_of, dst, s):
        def body(i, c):
            k = lax.rem(z + i, n_line)
            remote(src_of(k), dst.at[z], s, in_line(k)).start()
            return c

        lax.fori_loop(1, n_line, body, 0)
        sent.append((dst, n_line - 1, s))

    def sib_send(src, dst, s):
        remote(src, dst, s, at_chip(chip, 1 - core)).start()
        sent.append((dst, n_chip, s))

    def wait_for(buf, n, sem):
        part = buf.at[pl.ds(0, n)]
        pltpu.make_async_copy(part, part, sem).wait()

    def arrived(buf, n, s):
        wait_for(buf, n, recv.at[s])

    def sum_start(make, po, sa, pc, rb):
        s, t = fresh(), fresh()
        po[...] = make(1 - core)
        sib_send(po, sa, s)
        mine = make(core)
        arrived(sa, n_chip, s)
        pc[...] = mine + sa[...]
        rb[chip] = pc[chip]
        chip_send(lambda q: pc.at[q], rb, chip, t)
        return t

    def sum_end(rb, t):
        arrived(rb, n_chip - 1, t)
        return jnp.sum(rb[...], axis=0)

    def line_start(zp, zb):
        s = fresh()
        zb[z] = zp[z]
        line_send(lambda k: zp.at[k], zb, s)
        return s

    def line_mid(zb, zm, zg, s):
        t = fresh()
        arrived(zb, n_line - 1, s)
        zm[...] = jnp.sum(zb[...], axis=0)
        zg[z] = zm[...]
        line_send(lambda k: zm, zg, t)
        return t

    s_c, s_w, s_x, s_o = fresh(), fresh(), fresh(), fresh()

    hand_c = remote(coef, ca.at[there], s_c, partner)

    @pl.when(paired)
    def _():
        hand_c.start()

    plane_send(lambda j: wg.at[me], wg, s_w)
    plane_send(lambda j: columns(x, j), xs, s_x)

    @pl.when(paired)
    def _():
        hand_c.wait_send()
        wait_for(ca.at[pl.ds(me, 1)], 1, recv.at[s_c])

    @pl.when(alone)
    def _():
        own_c = pltpu.make_async_copy(coef, ca.at[me], local.at[4])
        own_c.start()
        own_c.wait()

    pieces = []
    for piece in range(2):
        part = ca.at[:, pl.ds(piece * (WIDE // 2), WIDE // 2)]
        s_p = fresh()
        chip_send(lambda q, part=part: part.at[me], part, me, s_p)
        pieces.append((part, s_p))

    n8 = HALF // 8
    deep = 8 * lax.broadcasted_iota(jnp.int32, (n8, 8, two), 0) + lax.broadcasted_iota(jnp.int32, (n8, 8, two), 1)
    wide = lax.broadcasted_iota(jnp.int32, (n8, 8, two), 2)
    big_l = lax.broadcasted_iota(jnp.int32, (two, two), 1) < RANK
    ones_l = big_l.astype(BF16)
    ones_r = jnp.logical_not(big_l).astype(BF16)

    def packed(v, base):
        n = v.shape[0]
        out = None
        for shift, ones in ((0, ones_l), (HALF, ones_r)):
            mask = (wide == deep + (base + shift)).astype(F32)
            picked = (v[:, None] * mask[None]).reshape(n * HALF, two)
            for part in split(picked):
                t = mm(part, ones)
                out = t if out is None else out + t
        return out

    own_wl = packed(wg[pl.ds(me, 1)], 0)

    arrived(wg, n_plane - 1, s_w)
    wlp = packed(wg[...], 0)
    whp = packed(wg[...], RANK)
    rows_x.wait()
    rows_o.wait()

    passed = []
    for part, s_p in pieces:
        arrived(part, n_chip - 1, s_p)
        mine_half = part.at[pl.ds(core * n_chip, n_chip)]
        s_p = fresh()
        sib_send(mine_half, mine_half, s_p)
        passed.append(s_p)
    both = None
    for piece, ((part, _), s_p) in enumerate(zip(pieces, passed)):
        arrived(part, n_chip, s_p)
        base = piece * (WIDE // 2)
        for j in range(n_plane):
            q = j % n_chip
            at = ((q // nx) * xc + (q % nx) * 2 + j // n_chip) * WIDE + base
            own_rows = jnp.concatenate(
                [xr[:, at : at + WIDE // 2], orow[:, at : at + WIDE // 2]], axis=0
            )
            t = mm(own_rows, ca[j, base : base + WIDE // 2])
            both = t if both is None else both + t

    def half_of(ref, which):
        return ref[pl.ds(which * n_chip, n_chip)]

    def spread(v, at):
        return jnp.broadcast_to(v[:, at : at + 1], (tall, two))

    f_own = jnp.where(left_half, (both[:TOK] * sd).astype(BF16).astype(F32), both[TOK:])
    am1[...] = f_own.astype(BF16)
    ab1[me] = am1[...]
    s_g, s_h2 = fresh(), fresh()
    chip_send(lambda q: am1, ab1, me, s_g)
    plane_send(lambda j: columns(o, j), os_, s_o)
    g_wide = None
    for j in range(n_plane):
        c = ca[j]
        t = mm(c, c, TN)
        g_wide = t if g_wide is None else g_wide + t
    g_wide = g_wide[RANK:]
    c_t = exact(put_r, ca[me].astype(F32), NT)
    nought = jnp.zeros_like(put_l)
    e_top = jnp.concatenate([put_l, nought], axis=0)
    e_top_r = jnp.concatenate([put_r, nought], axis=0)
    e_bot = jnp.concatenate([nought, put_l], axis=0)
    e_bot_r = jnp.concatenate([nought, put_r], axis=0)
    low_p = exact(f_own[:HALF], e_top) + exact(f_own[HALF:], e_top_r)
    ou_p = exact(f_own[:HALF], e_bot) + exact(f_own[HALF:], e_bot_r)
    hot = exact(hot_t, eye, TN)
    hot_l = exact(hot, put_l).astype(BF16)
    hot_r = exact(hot, put_r).astype(BF16)
    arrived(ab1, n_chip - 1, s_g)
    mine_half = ab1.at[pl.ds(core * n_chip, n_chip)]
    sib_send(mine_half, mine_half, s_h2)
    arrived(ab1, n_chip, s_h2)

    g_right = jnp.where(left_half, 0.0, g_wide)
    g_left = pltpu.roll(g_right, RANK, 1)
    g = g_left[:, :RANK]
    g_diag = jnp.concatenate([g_left, g_right], axis=0)
    f_a = ab1[:, :HALF].reshape(tall, two)
    f_b = ab1[:, HALF:].reshape(tall, two)
    k_l = jnp.concatenate([g_left * sr2, put_l * sr], axis=0)
    k_r = jnp.concatenate([g_right * sr2, put_r * sr], axis=0)
    p0 = (whp * (mm2(f_a, k_l) + mm2(f_b, k_r))).astype(BF16)
    def fold(v, a, b):
        return mm(v, a, TN)[:RANK] + mm(v, b, TN)[RANK:]

    own_x.wait()
    arrived(xs, n_plane - 1, s_x)
    x_a = xs[:, :HALF].reshape(tall, WIDE)
    x_b = xs[:, HALF:].reshape(tall, WIDE)
    zp1[...] = (fold(p0, x_a, x_b) * sd).reshape(n_line, chunk, WIDE)
    s_r = line_start(zp1, zb1)
    wfh_a = (f_a.astype(F32) * spread(whp, 0)).astype(BF16)
    wfh_b = (f_b.astype(F32) * spread(whp, RANK)).astype(BF16)
    wfl_a = (f_a.astype(F32) * spread(wlp, 0)).astype(BF16)
    wfl_b = (f_b.astype(F32) * spread(wlp, RANK)).astype(BF16)
    q_h = mm(f_a, wfh_a, TN)[:RANK] + mm(f_b, wfh_b, TN)[:RANK]
    q_l = mm(f_a, wfl_a, TN)[:RANK] + mm(f_b, wfl_b, TN)[:RANK]
    zp1b[:, 1] = jnp.concatenate([q_h, q_l], axis=1).reshape(n_line, chunk, WIDE)
    s_r = line_mid(zb1, zm1, zg1, s_r)
    own_o.wait()
    arrived(os_, n_plane - 1, s_o)
    o_a = os_[:, :HALF].reshape(tall, WIDE)
    o_b = os_[:, HALF:].reshape(tall, WIDE)
    zp1b[:, 0] = (mm(wfh_a, o_a, TN)[:RANK] + mm(wfh_b, o_b, TN)[:RANK]).reshape(n_line, chunk, WIDE)
    s_q = line_start(zp1b, zb1b)
    eu_p = ou_p + sr * exact(low_p, g_diag)
    arrived(zg1, n_line - 1, s_r)

    d_t = zg1[...].reshape(RANK, WIDE)
    nil = jnp.zeros((RANK, WIDE), BF16)

    def apply(v, ref, which, both):
        part = half_of(ref, which)
        a = part[:, :HALF].reshape(n_chip * HALF, WIDE)
        b = part[:, HALF:].reshape(n_chip * HALF, WIDE)
        out = None
        for piece in split(v) if both else (v.astype(BF16),):
            t = mm(a, jnp.concatenate([piece, nil], axis=0), NT) + mm(b, jnp.concatenate([nil, piece], axis=0), NT)
            out = t if out is None else out + t
        return out.reshape(n_chip, HALF, two)

    t2 = sum_start(lambda which: apply(d_t, xs, which, True), po2, sa2, pc2, rb2)
    pair_sems = [fresh(), fresh(), fresh()]

    def hand_over(k, down, m, n):
        up = exact(m, z_t, TN) + exact(n, c_t, TN)
        pair_out[k] = jnp.concatenate([down, up], axis=0).T

        @pl.when(paired)
        def _():
            remote(pair_out.at[k], pair_in.at[k], pair_sems[k], partner).start()

        @pl.when(alone)
        def _():
            pair_in[k] = pair_out[k]

    d_l = sum_end(rb2, t2) * sd
    am2[...] = d_l.astype(BF16)
    ab2[me] = am2[...]
    s_a = fresh()
    plane_send(lambda j: am2, ab2, s_a)
    s_q = line_mid(zb1b, zm1b, zg1b, s_q)
    arrived(zg1b, n_line - 1, s_q)
    z_t = zg1b[:, 0].reshape(RANK, WIDE)
    stats = zg1b[:, 1].reshape(RANK, WIDE)
    s_h = stats[:, :RANK]
    zu = pltpu.roll(stats[:, :two], RANK, 1)[:, :RANK]
    s_l = stats[:, two : two + RANK]
    d_m = eye * sr
    d_n = s_h * sr2
    d_tu = exact(d_m, zu, TN) + exact(d_n, g, TN)
    pz[:n_chip, :HALF] = apply(z_t, os_, 0, False).astype(BF16)
    pz[n_chip:, :HALF] = apply(z_t, os_, 1, False).astype(BF16)
    zz_part = exact(z_t, z_t, NT)
    zz_hi, zz_lo = split(zz_part)
    zz_both = (exact(zz_hi.astype(F32), put_l) + exact(zz_lo.astype(F32), put_r)).astype(BF16)
    pz[:, HALF:] = jnp.broadcast_to(zz_both[None], (n_plane, RANK, two))
    s_pz = fresh()
    rz[me] = pz[me]
    plane_send(lambda j: pz.at[j], rz, s_pz)
    arrived(ab2, n_plane - 1, s_a)
    gathered = ab2[...].reshape(tall, two)

    put_l16, put_r16 = put_l.astype(BF16), put_r.astype(BF16)

    def place(m, put, dims=NN):
        hi, lo = split(m)
        return mm(hi, put, dims) + mm(lo, put, dims)

    def near(a, b):
        a_hi, a_lo = split(a)
        b_hi, b_lo = split(b)
        return mm(a_hi, b_hi) + (mm(a_hi, b_lo) + mm(a_lo, b_hi))

    def image_part(l_p, tu, zp):
        tu_l = jnp.concatenate([place(tu, put_l16), nought], axis=0)
        tu_r = jnp.concatenate([place(tu, put_r16), nought], axis=0)
        inner = mm2(l_p, g_diag) + mm2(f_a, tu_l) + mm2(f_b, tu_r)
        y_p = (wlp * sr2 * inner).astype(BF16)
        down = fold(y_p, x_a, x_b) * sd
        cross = fold(l_p, wfl_a, wfl_b)
        zp[...] = jnp.concatenate([down, cross], axis=1).reshape(n_line, chunk, 3 * two)

    def gauss(m, n):
        return exact(zz, m) + exact(zu, n), exact(zu, m, TN) + exact(g, n)

    def diag(m):
        return jnp.concatenate([place(m, put_l16), place(m, put_r16)], axis=0)

    def diag_t(m):
        return jnp.concatenate([place(m, put_l16, TN), place(m, put_r16, TN)], axis=0)

    def up_rows(m, n, tu):
        return low_p * (near(oz_p, diag(m)) + late_rows(n, tu))

    def late_rows(n, tu):
        return near(ou_p, diag(n)) + sr * near(low_p, diag_t(tu))

    def by_domain(q, to):
        q_left = jnp.where(left32, q, 0.0)
        q_right = jnp.where(left32, 0.0, q)
        by = place(q_left, to[:HALF], TN) + place(q_right, to[HALF:], TN)
        return sr * jnp.sum(by, axis=0, keepdims=True)

    r_t, r_m, r_n, r_l, r_tu = d_t, d_m, d_n, d_l, d_tu
    first_l, first_m, first_n, first_tu = d_l, d_m, d_n, d_tu
    rounds = (
        (zp2, zb2, zm2, zg2, po3, sa3, pc3, rb3), (zp3, zb3, zm3, zg3, po4, sa4, pc4, rb4),
    )
    steps = []
    for turn, (zp, zb, zm, zg, po, sa, pc, rb) in enumerate(rounds):
        image_part(gathered, d_tu, zp)
        s_z = line_start(zp, zb)
        i_m = sr2 * exact(d_m, s_l) + mu * d_m
        i_n = sr2 * exact(d_n, s_l) + mu * d_n
        i_tu = exact(i_m, zu, TN) + exact(i_n, g, TN)
        if turn == 0:
            hand_over(0, d_t, d_m, d_n)
        else:
            i_gm, i_gn = gauss(i_m, i_n)
            r_lt = near(low_p, diag(r_tu))
            d_lt = near(low_p, diag(d_tu))
        s_z = line_mid(zb, zm, zg, s_z)
        if turn == 0:
            arrived(rz, n_plane - 1, s_pz)
            late = jnp.sum(rz[...].astype(F32), axis=0)
            oz_p = late[:HALF]
            zz = (late[HALF:] + pltpu.roll(late[HALF:], RANK, 1))[:, :RANK]
            d_gm, d_gn = gauss(d_m, d_n)
            r_gm, r_gn = d_gm, d_gn
            i_gm, i_gn = gauss(i_m, i_n)
        else:
            third_up = up_rows(i_m, i_n, i_tu)
        arrived(zg, n_line - 1, s_z)
        full = zg[...].reshape(RANK, 3 * two)
        i_t = full[:, :WIDE] + mu * d_t
        cross = full[:, WIDE : WIDE + RANK]
        note = jnp.zeros((8, two), F32)
        for at, value in enumerate((total(d_t * i_t), total(r_t * i_t), total(i_t * i_t), total(r_t * r_t))):
            note = jnp.where(sub8 == at, value, note)

        def third(which, i_t=i_t, note=note):
            return jnp.concatenate(
                [apply(i_t, xs, which, True), jnp.broadcast_to(note[None], (n_chip, 8, two))], axis=1
            )

        t3 = sum_start(third, po, sa, pc, rb)
        cross = sr2 * cross
        cross_tu = exact(cross, g, TN)
        i_n = i_n + cross
        i_gm = i_gm + exact(zu, cross)
        i_gn = i_gn + exact(g, cross)
        i_tu = i_tu + cross_tu
        di = total(d_m * i_gm + d_n * i_gn)
        ri = total(r_m * i_gm + r_n * i_gn)
        ii = total(i_m * i_gm + i_n * i_gn)
        r_r = total(r_m * r_gm + r_n * r_gn)
        if turn == 1:
            third_up = third_up + low_p * late_rows(cross, cross_tu)
            i_lt = near(low_p, diag(i_tu))
        s = sum_end(rb, t3)
        i_l = s[:HALF] * sd
        di = di + s[HALF : HALF + 1, :1]
        ri = ri + s[HALF + 1 : HALF + 2, :1]
        ii = ii + s[HALF + 2 : HALF + 3, :1]
        r_r = r_r + s[HALF + 3 : HALF + 4, :1]
        alpha = r_r / di
        rr = r_r - 2.0 * alpha * ri + alpha * alpha * ii
        beta = rr / r_r
        steps.append((alpha, beta))
        r_l = r_l - alpha * i_l
        d_l = r_l + beta * d_l
        if turn == 0:
            am3[...] = d_l.astype(BF16)
            ab3[me] = am3[...]
            s_a = fresh()
            plane_send(lambda j: am3, ab3, s_a)
            r_tu = r_tu - alpha * i_tu
            d_tu = r_tu + beta * d_tu
            hand_over(1, i_t, i_m, i_n)
            second_by = by_domain(i_l * eu_p + up_rows(i_m, i_n, i_tu), hot_r)
            first_by = by_domain(first_l * eu_p + up_rows(first_m, first_n, first_tu), hot_l)
        else:
            d_lt = r_lt - alpha * i_lt + beta * d_lt
            third_by = by_domain(i_l * eu_p + third_up, hot_l)
        r_t, r_m, r_n = r_t - alpha * i_t, r_m - alpha * i_m, r_n - alpha * i_n
        d_t, d_m, d_n = r_t + beta * d_t, r_m + beta * d_m, r_n + beta * d_n
        r_gm, r_gn = r_gm - alpha * i_gm, r_gn - alpha * i_gn
        d_gm, d_gn = r_gm + beta * d_gm, r_gn + beta * d_gn
        if turn == 0:
            arrived(ab3, n_plane - 1, s_a)
            gathered = ab3[...].reshape(tall, two)

    d_lb = d_l.astype(BF16)
    quad = sr2 * own_wl * d_lb.astype(F32) * (mm2(d_lb, g_diag) + 2.0 * d_lt)
    curve = total(quad) + (mu / n_line) * total(d_t * d_t)
    s_f, s_l2 = fresh(), fresh()
    fm[...] = jnp.where(
        sub8 == 0, first_by + second_by, jnp.where(sub8 == 1, third_by, jnp.where(sub8 == 2, curve, 0.0))
    )
    fb[me] = fm[...]
    plane_send(lambda j: fm, fb, s_f)
    hand_over(2, i_t, i_m, i_n)
    fixed = sr2 * total(exact(d_m, s_l) * d_gm + exact(d_n, s_l) * d_gn) + mu * total(d_m * d_gm + d_n * d_gn)
    arrived(fb, n_plane - 1, s_f)
    fq[...] = jnp.sum(fb[...], axis=0)
    fz[z] = fq[...]
    line_send(lambda k: fq, fz, s_l2)
    (a0, b0), (a1, b1) = steps
    for k in range(3):
        @pl.when(paired)
        def _(k=k):
            remote(pair_out.at[k], pair_in.at[k], pair_sems[k], partner).wait()

    for buf, n, s in sent[:-1]:
        wait_for(buf, n, send.at[s])
    arrived(fz, n_line - 1, s_l2)
    last = jnp.sum(fz[...], axis=0)
    a2 = rr / (last[2:3, :1] + fixed)
    w0 = a0 + a1 * (1.0 + b0) + a2 * (1.0 + b1 * (1.0 + b0))
    w1 = -a0 * (a1 + a2 * (1.0 + b1))
    w2 = -a1 * a2
    hyp = w0 * last[:1] + w1 * pltpu.roll(last, RANK, 1)[:1] + w2 * last[1:2]
    hyp_out[...] = -kappa * hyp[:, :RANK]
    sol_out[...] = w0 * pair_in[0] + w1 * pair_in[1] + w2 * pair_in[2]
    buf, n, s = sent[-1]
    wait_for(buf, n, send.at[s])


def solution(mesh, xc=8, z_lo=2):
    n_dp, n_fsdp = mesh.shape["dp"], mesh.shape["fsdp"]
    n_plane = (n_dp // z_lo) * xc
    n_line = (n_fsdp // xc) * z_lo
    n_chip = n_plane // 2
    n_sem = 44
    geo = (n_plane, n_line, xc, z_lo, n_sem)
    chunk = RANK // n_line
    two = 2 * RANK
    vm = pltpu.VMEM

    def sums(rows):
        return [vm((n_chip, rows, two), F32)] * 4

    def gather(rows):
        return [vm((rows, two), BF16), vm((n_plane, rows, two), BF16)]

    def line(*shape):
        return [vm((n_line, *shape), F32), vm((n_line, *shape), F32), vm(shape, F32), vm((n_line, *shape), F32)]

    late = vm((n_plane, HALF + RANK, two), BF16)
    scratch = [
        vm((n_plane, TOK, WIDE), BF16), vm((n_plane, TOK, WIDE), BF16), vm((n_plane, WIDE, two), BF16),
        vm((n_plane, 8, two), F32), vm((TOK, n_plane * WIDE), BF16), vm((TOK, n_plane * WIDE), BF16),
        *gather(TOK), *line(chunk, WIDE), *line(2, chunk, WIDE),
        *sums(HALF), *gather(HALF), *line(chunk, 3 * two), late, late,
        *sums(HALF + 8), *gather(HALF), *line(chunk, 3 * two),
        *sums(HALF + 8),
        vm((8, two), F32), vm((n_plane, 8, two), F32), vm((8, two), F32), vm((n_line, 8, two), F32),
        vm((3, WIDE, two), F32), vm((3, WIDE, two), F32),
        pltpu.SemaphoreType.DMA((n_sem,)), pltpu.SemaphoreType.DMA((n_sem,)), pltpu.SemaphoreType.DMA((5,)),
    ]
    anywhere = pl.BlockSpec(memory_space=pl.ANY)
    inside = pl.BlockSpec(memory_space=pltpu.VMEM)

    def on_device(x, o, cat, coef, learn, held):
        sol, hyp = pl.pallas_call(
            functools.partial(kernel, geo),
            out_shape=(
                jax.ShapeDtypeStruct((WIDE, two), F32),
                jax.ShapeDtypeStruct((1, RANK), F32),
            ),
            in_specs=[anywhere, anywhere, inside, anywhere, inside, inside],
            out_specs=(inside, inside),
            scratch_shapes=scratch,
            compiler_params=pltpu.CompilerParams(
                collective_id=0, has_side_effects=True, vmem_limit_bytes=56 * 1024 * 1024
            ),
        )(x, o, cat.reshape(1, TOK), coef, learn.reshape(1, DOMAINS), held.reshape(1, DOMAINS))
        return sol, hyp.reshape(DOMAINS)

    placed = (P(("dp", "fsdp"), None), P(("dp", "fsdp"), None), P(("dp", "fsdp")), P("fsdp", None), P(), P())
    return jax.shard_map(
        on_device, mesh=mesh, in_specs=placed, out_specs=(P("fsdp", None), P()), check_vma=False
    )
```

```python
import functools

import jax
import jax.numpy as jnp
from jax import lax
from jax.experimental import pallas as pl
from jax.experimental.pallas import tpu as pltpu
from jax.sharding import PartitionSpec as P

MESH = pl.DeviceIdType.MESH
HIGH = lax.Precision.HIGHEST
RANK = 64
DOMAINS = 64
TOK = 64
HALF = 32
WIDE = 256
F32 = jnp.float32
BF16 = jnp.bfloat16
NN = (((1,), (0,)), ((), ()))
NT = (((1,), (1,)), ((), ()))
TN = (((0,), (0,)), ((), ()))


def mm(a, b, dims=NN):
    return lax.dot_general(a, b, dims, preferred_element_type=F32)


def exact(a, b, dims=NN):
    return lax.dot_general(a, b, dims, precision=HIGH, preferred_element_type=F32)


def split(v):
    hi = v.astype(BF16)
    return hi, (v - hi.astype(F32)).astype(BF16)


def mm2(a, v, dims=NN):
    hi, lo = split(v)
    return mm(a, hi, dims) + mm(a, lo, dims)


def total(v):
    return jnp.sum(v, axis=(0, 1), keepdims=True)


def kernel(geo, x, o, cat, coef, tl, th, sol_out, hyp_out, *scratch):
    n_plane, n_line, xc, z_lo, n_sem = geo
    (
        xs, os_, ca, wg, xr, orow, am1, ab1, zp1, zb1, zm1, zg1, zp1b, zb1b, zm1b, zg1b,
        po2, sa2, pc2, rb2, am2, ab2, zp2, zb2, zm2, zg2, pz, rz,
        po3, sa3, pc3, rb3, am3, ab3, zp3, zb3, zm3, zg3,
        po4, sa4, pc4, rb4, fm, fb, fq, fz, pair_out, pair_in, send, recv, local,
    ) = scratch
    n_chip = n_plane // 2
    nx = xc // 2
    width = n_plane * WIDE
    rows = n_plane * n_line * TOK
    sd = width ** (-0.5)
    sr = RANK ** (-0.5)
    sr2 = 1.0 / RANK
    kappa = DOMAINS / (rows * width)
    mu = 0.1 * DOMAINS / (width * RANK)
    tall = n_plane * HALF
    two = 2 * RANK
    chunk = RANK // n_line

    dp = lax.axis_index("dp")
    fs = lax.axis_index("fsdp")
    y = lax.div(dp, z_lo)
    low_z = lax.rem(dp, z_lo)
    z_hi = lax.div(fs, xc)
    col = lax.rem(fs, xc)
    core = lax.rem(col, 2)
    chip = y * nx + lax.div(col, 2)
    here_x = lax.div(col, 2)
    ny = n_chip // nx
    me = core * n_chip + chip
    z = z_hi * z_lo + low_z

    def at_chip(q, which):
        return (lax.div(q, nx) * z_lo + low_z, z_hi * xc + lax.rem(q, nx) * 2 + which)

    def in_plane(j):
        return at_chip(lax.rem(j, n_chip), lax.div(j, n_chip))

    def in_line(k):
        return (y * z_lo + lax.rem(k, z_lo), lax.div(k, z_lo) * xc + col)

    def shard(j):
        q = lax.rem(j, n_chip)
        return lax.div(q, nx) * xc + lax.rem(q, nx) * 2 + lax.div(j, n_chip)

    partner = (z_hi * z_lo + low_z, y * xc + col)
    paired = y != z_hi
    alone = jnp.logical_not(paired)

    used = [0]

    def fresh():
        used[0] += 1
        assert used[0] <= n_sem
        return used[0] - 1

    sent = []

    def columns(ref, j):
        return ref.at[:, pl.ds(pl.multiple_of(shard(j) * WIDE, WIDE), WIDE)]

    own_x = pltpu.make_async_copy(columns(x, me), xs.at[me], local.at[0])
    own_o = pltpu.make_async_copy(columns(o, me), os_.at[me], local.at[1])
    rows_x = pltpu.make_async_copy(x, xr, local.at[2])
    rows_o = pltpu.make_async_copy(o, orow, local.at[3])
    for copy in (rows_x, rows_o, own_x, own_o):
        copy.start()

    barrier = pltpu.get_barrier_semaphore()

    def greet(i, c):
        pl.semaphore_signal(barrier, inc=1, device_id=in_plane(lax.rem(me + i, n_plane)), device_id_type=MESH)
        return c

    def greet_line(i, c):
        pl.semaphore_signal(barrier, inc=1, device_id=in_line(lax.rem(z + i, n_line)), device_id_type=MESH)
        return c

    lax.fori_loop(1, n_plane, greet, 0)
    lax.fori_loop(1, n_line, greet_line, 0)

    @pl.when(paired)
    def _():
        pl.semaphore_signal(barrier, inc=1, device_id=partner, device_id_type=MESH)

    sub = lax.broadcasted_iota(jnp.int32, (RANK, RANK), 0)
    lan = lax.broadcasted_iota(jnp.int32, (RANK, RANK), 1)
    eye = (sub == lan).astype(F32)
    sub2 = lax.broadcasted_iota(jnp.int32, (RANK, two), 0)
    lan2 = lax.broadcasted_iota(jnp.int32, (RANK, two), 1)
    put_l = (lan2 == sub2).astype(F32)
    put_r = (lan2 == sub2 + RANK).astype(F32)
    left_half = lan2 < RANK
    left32 = left_half[:HALF]
    sub8 = lax.broadcasted_iota(jnp.int32, (8, two), 0)
    hot_t = (cat[...] == sub).astype(F32)
    row_w = exact(exact(tl[...], hot_t), put_l) + exact(exact(th[...], hot_t), put_r)
    wg[me] = jnp.broadcast_to(row_w * kappa, (8, two))

    @pl.when(paired)
    def _():
        pl.semaphore_wait(barrier, n_plane + n_line - 1)

    @pl.when(alone)
    def _():
        pl.semaphore_wait(barrier, n_plane + n_line - 2)

    def remote(src, dst, s, device):
        return pltpu.make_async_remote_copy(
            src_ref=src, dst_ref=dst, send_sem=send.at[s], recv_sem=recv.at[s], device_id=device, device_id_type=MESH
        )

    def plane_send(src_of, dst, s):
        def body(i, c):
            j = lax.rem(me + i, n_plane)
            remote(src_of(j), dst.at[me], s, in_plane(j)).start()
            return c

        lax.fori_loop(1, n_plane, body, 0)
        sent.append((dst, n_plane - 1, s))

    def chip_send(src_of, dst, slot, s):
        def body(i, c):
            q = lax.rem(chip + i, n_chip)
            remote(src_of(q), dst.at[slot], s, at_chip(q, core)).start()
            return c

        lax.fori_loop(1, n_chip, body, 0)
        sent.append((dst, n_chip - 1, s))

    def line_send(src_of, dst, s):
        def body(i, c):
            k = lax.rem(z + i, n_line)
            remote(src_of(k), dst.at[z], s, in_line(k)).start()
            return c

        lax.fori_loop(1, n_line, body, 0)
        sent.append((dst, n_line - 1, s))

    def sib_send(src, dst, s):
        remote(src, dst, s, at_chip(chip, 1 - core)).start()
        sent.append((dst, n_chip, s))

    def wait_for(buf, n, sem):
        part = buf.at[pl.ds(0, n)]
        pltpu.make_async_copy(part, part, sem).wait()

    def arrived(buf, n, s):
        wait_for(buf, n, recv.at[s])

    def sum_start(make, po, sa, pc, rb):
        s, t = fresh(), fresh()
        po[...] = make(1 - core)
        sib_send(po, sa, s)
        mine = make(core)
        arrived(sa, n_chip, s)
        pc[...] = mine + sa[...]
        rb[chip] = pc[chip]
        chip_send(lambda q: pc.at[q], rb, chip, t)
        return t

    def sum_end(rb, t):
        arrived(rb, n_chip - 1, t)
        return jnp.sum(rb[...], axis=0)

    def line_start(zp, zb):
        s = fresh()
        zb[z] = zp[z]
        line_send(lambda k: zp.at[k], zb, s)
        return s

    def line_mid(zb, zm, zg, s):
        t = fresh()
        arrived(zb, n_line - 1, s)
        zm[...] = jnp.sum(zb[...], axis=0)
        zg[z] = zm[...]
        line_send(lambda k: zm, zg, t)
        return t

    s_c, s_w, s_x, s_o = fresh(), fresh(), fresh(), fresh()

    hand_c = remote(coef, ca.at[core, z_hi, here_x], s_c, partner)
    own_slot = ca.at[core, y, here_x]

    @pl.when(paired)
    def _():
        hand_c.start()

    plane_send(lambda j: wg.at[me], wg, s_w)
    plane_send(lambda j: columns(x, j), xs, s_x)

    @pl.when(paired)
    def _():
        hand_c.wait_send()
        pltpu.make_async_copy(own_slot, own_slot, recv.at[s_c]).wait()

    @pl.when(alone)
    def _():
        own_c = pltpu.make_async_copy(coef, own_slot, local.at[4])
        own_c.start()
        own_c.wait()

    lower = pl.ds(0, WIDE // 2)
    upper = pl.ds(WIDE // 2, WIDE // 2)

    def along_y(ref, s):
        def body(i, c):
            remote(ref, ref, s, at_chip(lax.rem(y + i, ny) * nx + here_x, core)).start()
            return c

        lax.fori_loop(1, ny, body, 0)

    def along_x(ref, s):
        def body(i, c):
            remote(ref, ref, s, at_chip(y * nx + lax.rem(here_x + i, nx), core)).start()
            return c

        lax.fori_loop(1, nx, body, 0)

    def both_ends(part, s, n):
        for sem in (recv, send):
            for_all = part.at[pl.ds(0, n)]
            pltpu.make_async_copy(for_all, for_all, sem.at[s]).wait()

    g_a, g_b, g_a2, g_b2 = fresh(), fresh(), fresh(), fresh()
    along_y(ca.at[core, y, here_x, lower], g_a)
    along_x(ca.at[core, y, here_x, upper], g_b)

    n8 = HALF // 8
    deep = 8 * lax.broadcasted_iota(jnp.int32, (n8, 8, two), 0) + lax.broadcasted_iota(jnp.int32, (n8, 8, two), 1)
    wide = lax.broadcasted_iota(jnp.int32, (n8, 8, two), 2)
    big_l = lax.broadcasted_iota(jnp.int32, (two, two), 1) < RANK
    ones_l = big_l.astype(BF16)
    ones_r = jnp.logical_not(big_l).astype(BF16)

    def packed(v, base):
        n = v.shape[0]
        out = None
        for shift, ones in ((0, ones_l), (HALF, ones_r)):
            mask = (wide == deep + (base + shift)).astype(F32)
            picked = (v[:, None] * mask[None]).reshape(n * HALF, two)
            for part in split(picked):
                t = mm(part, ones)
                out = t if out is None else out + t
        return out

    own_wl = packed(wg[pl.ds(me, 1)], 0)

    arrived(wg, n_plane - 1, s_w)
    wlp = packed(wg[...], 0)
    whp = packed(wg[...], RANK)
    rows_x.wait()
    rows_o.wait()

    column_a = ca.at[core, :, here_x, lower]
    row_b = ca.at[core, y, :, upper]
    both_ends(column_a, g_a, ny - 1)
    along_x(column_a, g_a2)
    if nx > 1:
        both_ends(row_b, g_b, nx - 1)
    along_y(row_b, g_b2)
    halves = []
    for span, s_p, n, kind in ((lower, g_a2, nx - 1, 0), (upper, g_b2, ny - 1, 1)):
        if n:
            rest = ca.at[core, :, pl.ds(0, n), span] if kind == 0 else ca.at[core, pl.ds(0, n), :, span]
            for sem in (recv, send):
                pltpu.make_async_copy(rest, rest, sem.at[s_p]).wait()
        whole = ca.at[core, :, :, span]
        s_p = fresh()
        remote(whole, whole, s_p, at_chip(chip, 1 - core)).start()
        halves.append((whole, s_p))
    both = None
    for piece, (whole, s_p) in enumerate(halves):
        pltpu.make_async_copy(whole, whole, recv.at[s_p]).wait()
        base = piece * (WIDE // 2)
        for j in range(n_plane):
            q = j % n_chip
            at = ((q // nx) * xc + (q % nx) * 2 + j // n_chip) * WIDE + base
            own_rows = jnp.concatenate(
                [xr[:, at : at + WIDE // 2], orow[:, at : at + WIDE // 2]], axis=0
            )
            t = mm(own_rows, ca[j // n_chip, q // nx, q % nx, base : base + WIDE // 2])
            both = t if both is None else both + t

    def half_of(ref, which):
        return ref[pl.ds(which * n_chip, n_chip)]

    def spread(v, at):
        return jnp.broadcast_to(v[:, at : at + 1], (tall, two))

    f_own = jnp.where(left_half, (both[:TOK] * sd).astype(BF16).astype(F32), both[TOK:])
    am1[...] = f_own.astype(BF16)
    ab1[me] = am1[...]
    s_g, s_h2 = fresh(), fresh()
    chip_send(lambda q: am1, ab1, me, s_g)
    plane_send(lambda j: columns(o, j), os_, s_o)
    g_wide = None
    for j in range(n_plane):
        c = ca[j // n_chip, (j % n_chip) // nx, j % nx]
        t = mm(c, c, TN)
        g_wide = t if g_wide is None else g_wide + t
    g_wide = g_wide[RANK:]
    c_t = exact(put_r, ca[core, y, here_x].astype(F32), NT)
    nought = jnp.zeros_like(put_l)
    e_top = jnp.concatenate([put_l, nought], axis=0)
    e_top_r = jnp.concatenate([put_r, nought], axis=0)
    e_bot = jnp.concatenate([nought, put_l], axis=0)
    e_bot_r = jnp.concatenate([nought, put_r], axis=0)
    low_p = exact(f_own[:HALF], e_top) + exact(f_own[HALF:], e_top_r)
    ou_p = exact(f_own[:HALF], e_bot) + exact(f_own[HALF:], e_bot_r)
    hot = exact(hot_t, eye, TN)
    hot_l = exact(hot, put_l).astype(BF16)
    hot_r = exact(hot, put_r).astype(BF16)
    arrived(ab1, n_chip - 1, s_g)
    mine_half = ab1.at[pl.ds(core * n_chip, n_chip)]
    sib_send(mine_half, mine_half, s_h2)
    arrived(ab1, n_chip, s_h2)

    g_right = jnp.where(left_half, 0.0, g_wide)
    g_left = pltpu.roll(g_right, RANK, 1)
    g = g_left[:, :RANK]
    g_diag = jnp.concatenate([g_left, g_right], axis=0)
    f_a = ab1[:, :HALF].reshape(tall, two)
    f_b = ab1[:, HALF:].reshape(tall, two)
    k_l = jnp.concatenate([g_left * sr2, put_l * sr], axis=0)
    k_r = jnp.concatenate([g_right * sr2, put_r * sr], axis=0)
    p0 = (whp * (mm2(f_a, k_l) + mm2(f_b, k_r))).astype(BF16)
    def fold(v, a, b):
        return mm(v, a, TN)[:RANK] + mm(v, b, TN)[RANK:]

    own_x.wait()
    arrived(xs, n_plane - 1, s_x)
    x_a = xs[:, :HALF].reshape(tall, WIDE)
    x_b = xs[:, HALF:].reshape(tall, WIDE)
    zp1[...] = (fold(p0, x_a, x_b) * sd).reshape(n_line, chunk, WIDE)
    s_r = line_start(zp1, zb1)
    wfh_a = (f_a.astype(F32) * spread(whp, 0)).astype(BF16)
    wfh_b = (f_b.astype(F32) * spread(whp, RANK)).astype(BF16)
    wfl_a = (f_a.astype(F32) * spread(wlp, 0)).astype(BF16)
    wfl_b = (f_b.astype(F32) * spread(wlp, RANK)).astype(BF16)
    q_h = mm(f_a, wfh_a, TN)[:RANK] + mm(f_b, wfh_b, TN)[:RANK]
    q_l = mm(f_a, wfl_a, TN)[:RANK] + mm(f_b, wfl_b, TN)[:RANK]
    zp1b[:, 1] = jnp.concatenate([q_h, q_l], axis=1).reshape(n_line, chunk, WIDE)
    s_r = line_mid(zb1, zm1, zg1, s_r)
    own_o.wait()
    arrived(os_, n_plane - 1, s_o)
    o_a = os_[:, :HALF].reshape(tall, WIDE)
    o_b = os_[:, HALF:].reshape(tall, WIDE)
    zp1b[:, 0] = (mm(wfh_a, o_a, TN)[:RANK] + mm(wfh_b, o_b, TN)[:RANK]).reshape(n_line, chunk, WIDE)
    s_q = line_start(zp1b, zb1b)
    eu_p = ou_p + sr * exact(low_p, g_diag)
    arrived(zg1, n_line - 1, s_r)

    d_t = zg1[...].reshape(RANK, WIDE)
    nil = jnp.zeros((RANK, WIDE), BF16)

    def apply(v, ref, which, both):
        part = half_of(ref, which)
        a = part[:, :HALF].reshape(n_chip * HALF, WIDE)
        b = part[:, HALF:].reshape(n_chip * HALF, WIDE)
        out = None
        for piece in split(v) if both else (v.astype(BF16),):
            t = mm(a, jnp.concatenate([piece, nil], axis=0), NT) + mm(b, jnp.concatenate([nil, piece], axis=0), NT)
            out = t if out is None else out + t
        return out.reshape(n_chip, HALF, two)

    t2 = sum_start(lambda which: apply(d_t, xs, which, True), po2, sa2, pc2, rb2)
    s_q = line_mid(zb1b, zm1b, zg1b, s_q)

    pair_sems = [fresh(), fresh(), fresh()]

    def hand_over(k, both_halves):
        pair_out[k] = both_halves.T

        @pl.when(paired)
        def _():
            remote(pair_out.at[k], pair_in.at[k], pair_sems[k], partner).start()

        @pl.when(alone)
        def _():
            pair_in[k] = pair_out[k]

    d_l = sum_end(rb2, t2) * sd
    am2[...] = d_l.astype(BF16)
    ab2[me] = am2[...]
    s_a = fresh()
    plane_send(lambda j: am2, ab2, s_a)
    arrived(zg1b, n_line - 1, s_q)
    z_t = zg1b[:, 0].reshape(RANK, WIDE)
    stats = zg1b[:, 1].reshape(RANK, WIDE)
    s_h = stats[:, :RANK]
    zu = pltpu.roll(stats[:, :two], RANK, 1)[:, :RANK]
    s_l = stats[:, two : two + RANK]
    d_m = eye * sr
    d_n = s_h * sr2
    d_tu = exact(d_m, zu, TN) + exact(d_n, g, TN)

    def up_slice(m, n):
        return exact(m, z_t, TN) + exact(n, c_t, TN)

    d_t = jnp.concatenate([d_t, up_slice(d_m, d_n)], axis=0)
    arrived(ab2, n_plane - 1, s_a)
    gathered = ab2[...].reshape(tall, two)

    put_l16, put_r16 = put_l.astype(BF16), put_r.astype(BF16)

    def place(m, put, dims=NN):
        hi, lo = split(m)
        return mm(hi, put, dims) + mm(lo, put, dims)

    def near(a, b):
        a_hi, a_lo = split(a)
        b_hi, b_lo = split(b)
        return mm(a_hi, b_hi) + (mm(a_hi, b_lo) + mm(a_lo, b_hi))

    def image_part(l_p, tu, zp):
        tu_l = jnp.concatenate([place(tu, put_l16), nought], axis=0)
        tu_r = jnp.concatenate([place(tu, put_r16), nought], axis=0)
        inner = mm2(l_p, g_diag) + mm2(f_a, tu_l) + mm2(f_b, tu_r)
        y_p = (wlp * sr2 * inner).astype(BF16)
        down = fold(y_p, x_a, x_b) * sd
        cross = fold(l_p, wfl_a, wfl_b)
        zp[...] = jnp.concatenate([down, cross], axis=1).reshape(n_line, chunk, 3 * two)

    def diag(m):
        return jnp.concatenate([place(m, put_l16), place(m, put_r16)], axis=0)

    def diag_t(m):
        return jnp.concatenate([place(m, put_l16, TN), place(m, put_r16, TN)], axis=0)

    def up_rows(m, n, tu):
        return low_p * (near(oz_p, diag(m)) + late_rows(n, tu))

    def late_rows(n, tu):
        return near(ou_p, diag(n)) + sr * near(low_p, diag_t(tu))

    def by_domain(q, to):
        q_left = jnp.where(left32, q, 0.0)
        q_right = jnp.where(left32, 0.0, q)
        by = place(q_left, to[:HALF], TN) + place(q_right, to[HALF:], TN)
        return sr * jnp.sum(by, axis=0, keepdims=True)

    r_t, r_m, r_n, r_l, r_tu = d_t, d_m, d_n, d_l, d_tu
    first_l, first_m, first_n, first_tu = d_l, d_m, d_n, d_tu
    rounds = (
        (zp2, zb2, zm2, zg2, po3, sa3, pc3, rb3), (zp3, zb3, zm3, zg3, po4, sa4, pc4, rb4),
    )
    steps = []
    for turn, (zp, zb, zm, zg, po, sa, pc, rb) in enumerate(rounds):
        image_part(gathered, d_tu, zp)
        s_z = line_start(zp, zb)
        i_m = sr2 * exact(d_m, s_l) + mu * d_m
        i_n = sr2 * exact(d_n, s_l) + mu * d_n
        i_tu = exact(i_m, zu, TN) + exact(i_n, g, TN)
        i_up = up_slice(i_m, i_n)
        if turn == 0:
            pz[:n_chip] = apply(z_t, os_, 0, False).astype(BF16)
            pz[n_chip:] = apply(z_t, os_, 1, False).astype(BF16)
            s_pz = fresh()
            rz[me] = pz[me]
            plane_send(lambda j: pz.at[j], rz, s_pz)
        else:
            r_lt = near(low_p, diag(r_tu))
            d_lt = near(low_p, diag(d_tu))
        s_z = line_mid(zb, zm, zg, s_z)
        if turn == 0:
            hand_over(0, d_t)
        else:
            third_up = up_rows(i_m, i_n, i_tu)
            d_sv = exact(s_l, d_t[RANK:], TN)
            r_sv = exact(s_l, r_t[RANK:], TN)
        arrived(zg, n_line - 1, s_z)
        full = zg[...].reshape(RANK, 3 * two)
        cross = sr2 * full[:, WIDE : WIDE + RANK]
        i_t = jnp.concatenate(
            [full[:, :WIDE] + mu * d_t[:RANK], i_up + exact(cross, c_t, TN)], axis=0
        )
        note = jnp.zeros((8, two), F32)
        for at, value in enumerate((total(d_t * i_t), total(r_t * i_t), total(i_t * i_t), total(r_t * r_t))):
            note = jnp.where(sub8 == at, value, note)

        def third(which, i_t=i_t, note=note):
            return jnp.concatenate(
                [apply(i_t[:RANK], xs, which, True), jnp.broadcast_to(note[None], (n_chip, 8, two))], axis=1
            )

        t3 = sum_start(third, po, sa, pc, rb)
        cross_tu = exact(cross, g, TN)
        i_n = i_n + cross
        i_tu = i_tu + cross_tu
        if turn == 1:
            third_up = third_up + low_p * late_rows(cross, cross_tu)
            i_lt = near(low_p, diag(i_tu))
            i_sv = exact(s_l, i_t[RANK:], TN)
        s = sum_end(rb, t3)
        i_l = s[:HALF] * sd
        di, ri, ii, r_r = [s[HALF + at : HALF + at + 1, :1] for at in range(4)]
        alpha = r_r / di
        rr = r_r - 2.0 * alpha * ri + alpha * alpha * ii
        beta = rr / r_r
        steps.append((alpha, beta))
        r_l = r_l - alpha * i_l
        d_l = r_l + beta * d_l
        if turn == 0:
            am3[...] = d_l.astype(BF16)
            ab3[me] = am3[...]
            s_a = fresh()
            plane_send(lambda j: am3, ab3, s_a)
            r_tu = r_tu - alpha * i_tu
            d_tu = r_tu + beta * d_tu
            hand_over(1, i_t)
            arrived(rz, n_plane - 1, s_pz)
            oz_p = jnp.sum(rz[...].astype(F32), axis=0)
            second_by = by_domain(i_l * eu_p + up_rows(i_m, i_n, i_tu), hot_r)
            first_by = by_domain(first_l * eu_p + up_rows(first_m, first_n, first_tu), hot_l)
        else:
            d_lt = r_lt - alpha * i_lt + beta * d_lt
            d_sv = r_sv - alpha * i_sv + beta * d_sv
            third_by = by_domain(i_l * eu_p + third_up, hot_l)
        r_t, r_m, r_n = r_t - alpha * i_t, r_m - alpha * i_m, r_n - alpha * i_n
        d_t, d_m, d_n = r_t + beta * d_t, r_m + beta * d_m, r_n + beta * d_n
        if turn == 0:
            arrived(ab3, n_plane - 1, s_a)
            gathered = ab3[...].reshape(tall, two)

    d_lb = d_l.astype(BF16)
    quad = sr2 * own_wl * d_lb.astype(F32) * (mm2(d_lb, g_diag) + 2.0 * d_lt)
    slices = mu * total(d_t * d_t) + sr2 * total(d_sv * d_t[RANK:])
    curve = total(quad) + slices * (1.0 / n_line)
    s_f, s_l2 = fresh(), fresh()
    fm[...] = jnp.where(
        sub8 == 0, first_by + second_by, jnp.where(sub8 == 1, third_by, jnp.where(sub8 == 2, curve, 0.0))
    )
    fb[me] = fm[...]
    plane_send(lambda j: fm, fb, s_f)
    hand_over(2, i_t)
    arrived(fb, n_plane - 1, s_f)
    fq[...] = jnp.sum(fb[...], axis=0)
    fz[z] = fq[...]
    line_send(lambda k: fq, fz, s_l2)
    (a0, b0), (a1, b1) = steps
    for k in range(3):
        @pl.when(paired)
        def _(k=k):
            remote(pair_out.at[k], pair_in.at[k], pair_sems[k], partner).wait()

    for whole, s_p in halves:
        pltpu.make_async_copy(whole, whole, send.at[s_p]).wait()
    for buf, n, s in sent[:-1]:
        wait_for(buf, n, send.at[s])
    arrived(fz, n_line - 1, s_l2)
    last = jnp.sum(fz[...], axis=0)
    a2 = rr / last[2:3, :1]
    w0 = a0 + a1 * (1.0 + b0) + a2 * (1.0 + b1 * (1.0 + b0))
    w1 = -a0 * (a1 + a2 * (1.0 + b1))
    w2 = -a1 * a2
    hyp = w0 * last[:1] + w1 * pltpu.roll(last, RANK, 1)[:1] + w2 * last[1:2]
    hyp_out[...] = -kappa * hyp[:, :RANK]
    sol_out[...] = w0 * pair_in[0] + w1 * pair_in[1] + w2 * pair_in[2]
    buf, n, s = sent[-1]
    wait_for(buf, n, send.at[s])


def solution(mesh, xc=8, z_lo=2):
    n_dp, n_fsdp = mesh.shape["dp"], mesh.shape["fsdp"]
    n_plane = (n_dp // z_lo) * xc
    n_line = (n_fsdp // xc) * z_lo
    n_chip = n_plane // 2
    n_sem = 48
    geo = (n_plane, n_line, xc, z_lo, n_sem)
    chunk = RANK // n_line
    two = 2 * RANK
    vm = pltpu.VMEM

    def sums(rows):
        return [vm((n_chip, rows, two), F32)] * 4

    def gather(rows):
        return [vm((rows, two), BF16), vm((n_plane, rows, two), BF16)]

    def line(*shape):
        return [vm((n_line, *shape), F32), vm((n_line, *shape), F32), vm(shape, F32), vm((n_line, *shape), F32)]

    late = vm((n_plane, HALF, two), BF16)
    scratch = [
        vm((n_plane, TOK, WIDE), BF16), vm((n_plane, TOK, WIDE), BF16), vm((2, n_chip // (xc // 2), xc // 2, WIDE, two), BF16),
        vm((n_plane, 8, two), F32), vm((TOK, n_plane * WIDE), BF16), vm((TOK, n_plane * WIDE), BF16),
        *gather(TOK), *line(chunk, WIDE), *line(2, chunk, WIDE),
        *sums(HALF), *gather(HALF), *line(chunk, 3 * two), late, late,
        *sums(HALF + 8), *gather(HALF), *line(chunk, 3 * two),
        *sums(HALF + 8),
        vm((8, two), F32), vm((n_plane, 8, two), F32), vm((8, two), F32), vm((n_line, 8, two), F32),
        vm((3, WIDE, two), F32), vm((3, WIDE, two), F32),
        pltpu.SemaphoreType.DMA((n_sem,)), pltpu.SemaphoreType.DMA((n_sem,)), pltpu.SemaphoreType.DMA((5,)),
    ]
    anywhere = pl.BlockSpec(memory_space=pl.ANY)
    inside = pl.BlockSpec(memory_space=pltpu.VMEM)

    def on_device(x, o, cat, coef, learn, held):
        sol, hyp = pl.pallas_call(
            functools.partial(kernel, geo),
            out_shape=(
                jax.ShapeDtypeStruct((WIDE, two), F32),
                jax.ShapeDtypeStruct((1, RANK), F32),
            ),
            in_specs=[anywhere, anywhere, inside, anywhere, inside, inside],
            out_specs=(inside, inside),
            scratch_shapes=scratch,
            compiler_params=pltpu.CompilerParams(
                collective_id=0, has_side_effects=True, vmem_limit_bytes=56 * 1024 * 1024
            ),
        )(x, o, cat.reshape(1, TOK), coef, learn.reshape(1, DOMAINS), held.reshape(1, DOMAINS))
        return sol, hyp.reshape(DOMAINS)

    placed = (P(("dp", "fsdp"), None), P(("dp", "fsdp"), None), P(("dp", "fsdp")), P("fsdp", None), P(), P())
    return jax.shard_map(
        on_device, mesh=mesh, in_specs=placed, out_specs=(P("fsdp", None), P()), check_vma=False
    )
```

```python
import functools

import jax
import jax.numpy as jnp
from jax import lax
from jax.experimental import pallas as pl
from jax.experimental.pallas import tpu as pltpu
from jax.sharding import PartitionSpec as P

MESH = pl.DeviceIdType.MESH
HIGH = lax.Precision.HIGHEST
RANK = 64
DOMAINS = 64
TOK = 64
HALF = 32
WIDE = 256
F32 = jnp.float32
BF16 = jnp.bfloat16
NN = (((1,), (0,)), ((), ()))
NT = (((1,), (1,)), ((), ()))
TN = (((0,), (0,)), ((), ()))


def mm(a, b, dims=NN):
    return lax.dot_general(a, b, dims, preferred_element_type=F32)


def exact(a, b, dims=NN):
    return lax.dot_general(a, b, dims, precision=HIGH, preferred_element_type=F32)


def split(v):
    hi = v.astype(BF16)
    return hi, (v - hi.astype(F32)).astype(BF16)


def mm2(a, v, dims=NN):
    hi, lo = split(v)
    return mm(a, hi, dims) + mm(a, lo, dims)


def total(v):
    return jnp.sum(v, axis=(0, 1), keepdims=True)


def kernel(geo, x, o, cat, coef, tl, th, sol_out, hyp_out, *scratch):
    n_plane, n_line, xc, z_lo, n_sem = geo
    (
        xs, os_, ca, wg, xr, orow, am1, ab1, zp1, zb1, zm1, zg1, zp1b, zb1b, zm1b, zg1b,
        po2, sa2, pc2, rb2, am2, ab2, zp2, zb2, zm2, zg2, pz, rz,
        po3, sa3, pc3, rb3, am3, ab3, zp3, zb3, zm3, zg3,
        po4, sa4, pc4, rb4, fm, fb, fq, fz, pair_out, pair_in, send, recv, local,
    ) = scratch
    n_chip = n_plane // 2
    nx = xc // 2
    width = n_plane * WIDE
    rows = n_plane * n_line * TOK
    sd = width ** (-0.5)
    sr = RANK ** (-0.5)
    sr2 = 1.0 / RANK
    kappa = DOMAINS / (rows * width)
    mu = 0.1 * DOMAINS / (width * RANK)
    tall = n_plane * HALF
    two = 2 * RANK
    chunk = RANK // n_line

    dp = lax.axis_index("dp")
    fs = lax.axis_index("fsdp")
    y = lax.div(dp, z_lo)
    low_z = lax.rem(dp, z_lo)
    z_hi = lax.div(fs, xc)
    col = lax.rem(fs, xc)
    core = lax.rem(col, 2)
    chip = y * nx + lax.div(col, 2)
    here_x = lax.div(col, 2)
    ny = n_chip // nx
    me = core * n_chip + chip
    z = z_hi * z_lo + low_z

    def at_chip(q, which):
        return (lax.div(q, nx) * z_lo + low_z, z_hi * xc + lax.rem(q, nx) * 2 + which)

    def in_plane(j):
        return at_chip(lax.rem(j, n_chip), lax.div(j, n_chip))

    def in_line(k):
        return (y * z_lo + lax.rem(k, z_lo), lax.div(k, z_lo) * xc + col)

    def shard(j):
        q = lax.rem(j, n_chip)
        return lax.div(q, nx) * xc + lax.rem(q, nx) * 2 + lax.div(j, n_chip)

    partner = (z_hi * z_lo + low_z, y * xc + col)
    paired = y != z_hi
    alone = jnp.logical_not(paired)

    used = [0]

    def fresh():
        used[0] += 1
        assert used[0] <= n_sem
        return used[0] - 1

    sent = []

    def columns(ref, j):
        return ref.at[:, pl.ds(pl.multiple_of(shard(j) * WIDE, WIDE), WIDE)]

    own_x = pltpu.make_async_copy(columns(x, me), xs.at[me], local.at[0])
    own_o = pltpu.make_async_copy(columns(o, me), os_.at[me], local.at[1])
    rows_x = pltpu.make_async_copy(x, xr, local.at[2])
    rows_o = pltpu.make_async_copy(o, orow, local.at[3])
    for copy in (rows_x, rows_o, own_x, own_o):
        copy.start()

    barrier = pltpu.get_barrier_semaphore()

    def greet(i, c):
        pl.semaphore_signal(barrier, inc=1, device_id=in_plane(lax.rem(me + i, n_plane)), device_id_type=MESH)
        return c

    def greet_line(i, c):
        pl.semaphore_signal(barrier, inc=1, device_id=in_line(lax.rem(z + i, n_line)), device_id_type=MESH)
        return c

    lax.fori_loop(1, n_plane, greet, 0)
    lax.fori_loop(1, n_line, greet_line, 0)

    sub = lax.broadcasted_iota(jnp.int32, (RANK, RANK), 0)
    lan = lax.broadcasted_iota(jnp.int32, (RANK, RANK), 1)
    eye = (sub == lan).astype(F32)
    sub2 = lax.broadcasted_iota(jnp.int32, (RANK, two), 0)
    lan2 = lax.broadcasted_iota(jnp.int32, (RANK, two), 1)
    put_l = (lan2 == sub2).astype(F32)
    put_r = (lan2 == sub2 + RANK).astype(F32)
    left_half = lan2 < RANK
    left32 = left_half[:HALF]
    sub8 = lax.broadcasted_iota(jnp.int32, (8, two), 0)
    hot_t = (cat[...] == sub).astype(F32)
    row_w = exact(exact(tl[...], hot_t), put_l) + exact(exact(th[...], hot_t), put_r)
    wg[me] = jnp.broadcast_to(row_w * kappa, (8, two))

    pl.semaphore_wait(barrier, n_plane + n_line - 2)

    def remote(src, dst, s, device):
        return pltpu.make_async_remote_copy(
            src_ref=src, dst_ref=dst, send_sem=send.at[s], recv_sem=recv.at[s], device_id=device, device_id_type=MESH
        )

    def plane_part(src_of, dst, s, first, stop):
        def body(i, c):
            j = lax.rem(me + i, n_plane)
            remote(src_of(j), dst.at[me], s, in_plane(j)).start()
            return c

        lax.fori_loop(first, stop, body, 0)

    def plane_send(src_of, dst, s):
        plane_part(src_of, dst, s, 1, n_plane)
        sent.append((dst, n_plane - 1, s))

    def chip_send(src_of, dst, slot, s):
        def body(i, c):
            q = lax.rem(chip + i, n_chip)
            remote(src_of(q), dst.at[slot], s, at_chip(q, core)).start()
            return c

        lax.fori_loop(1, n_chip, body, 0)
        sent.append((dst, n_chip - 1, s))

    def line_send(src_of, dst, s):
        def body(i, c):
            k = lax.rem(z + i, n_line)
            remote(src_of(k), dst.at[z], s, in_line(k)).start()
            return c

        lax.fori_loop(1, n_line, body, 0)
        sent.append((dst, n_line - 1, s))

    def sib_send(src, dst, s):
        remote(src, dst, s, at_chip(chip, 1 - core)).start()
        sent.append((dst, n_chip, s))

    def wait_for(buf, n, sem):
        part = buf.at[pl.ds(0, n)]
        pltpu.make_async_copy(part, part, sem).wait()

    def arrived(buf, n, s):
        wait_for(buf, n, recv.at[s])

    def sum_start(make, po, sa, pc, rb):
        s, t = fresh(), fresh()
        po[...] = make(1 - core)
        sib_send(po, sa, s)
        mine = make(core)
        arrived(sa, n_chip, s)
        pc[...] = mine + sa[...]
        rb[chip] = pc[chip]
        chip_send(lambda q: pc.at[q], rb, chip, t)
        return t

    def sum_end(rb, t):
        arrived(rb, n_chip - 1, t)
        return jnp.sum(rb[...], axis=0)

    def line_start(zp, zb):
        s = fresh()
        zb[z] = zp[z]
        line_send(lambda k: zp.at[k], zb, s)
        return s

    def line_mid(zb, zm, zg, s):
        t = fresh()
        arrived(zb, n_line - 1, s)
        zm[...] = jnp.sum(zb[...], axis=0)
        zg[z] = zm[...]
        line_send(lambda k: zm, zg, t)
        return t

    s_c, s_w, s_x, s_o = fresh(), fresh(), fresh(), fresh()

    own_slot = ca.at[core, y, here_x]
    n_hi = n_line // z_lo
    own_c = pltpu.make_async_copy(coef, own_slot, local.at[4])

    @pl.when(alone)
    def _():
        def body(i, c):
            remote(coef, own_slot, s_c, (dp, lax.rem(z_hi + i, n_hi) * xc + col)).start()
            return c

        lax.fori_loop(1, n_hi, body, 0)
        own_c.start()

    plane_send(lambda j: wg.at[me], wg, s_w)
    plane_part(lambda j: columns(x, j), xs, s_x, 1, n_plane // 2)

    @pl.when(paired)
    def _():
        pltpu.make_async_copy(own_slot, own_slot, recv.at[s_c]).wait()

    @pl.when(alone)
    def _():
        own_c.wait()

    lower = pl.ds(0, WIDE // 2)
    upper = pl.ds(WIDE // 2, WIDE // 2)

    def along_y(ref, s):
        def body(i, c):
            remote(ref, ref, s, at_chip(lax.rem(y + i, ny) * nx + here_x, core)).start()
            return c

        lax.fori_loop(1, ny, body, 0)

    def along_x(ref, s):
        def body(i, c):
            remote(ref, ref, s, at_chip(y * nx + lax.rem(here_x + i, nx), core)).start()
            return c

        lax.fori_loop(1, nx, body, 0)

    def both_ends(part, s, n):
        for sem in (recv, send):
            for_all = part.at[pl.ds(0, n)]
            pltpu.make_async_copy(for_all, for_all, sem.at[s]).wait()

    g_a, g_b, g_a2, g_b2 = fresh(), fresh(), fresh(), fresh()
    along_y(ca.at[core, y, here_x, lower], g_a)
    along_x(ca.at[core, y, here_x, upper], g_b)

    n8 = HALF // 8
    deep = 8 * lax.broadcasted_iota(jnp.int32, (n8, 8, two), 0) + lax.broadcasted_iota(jnp.int32, (n8, 8, two), 1)
    wide = lax.broadcasted_iota(jnp.int32, (n8, 8, two), 2)
    big_l = lax.broadcasted_iota(jnp.int32, (two, two), 1) < RANK
    ones_l = big_l.astype(BF16)
    ones_r = jnp.logical_not(big_l).astype(BF16)

    def packed(v, base):
        n = v.shape[0]
        out = None
        for shift, ones in ((0, ones_l), (HALF, ones_r)):
            mask = (wide == deep + (base + shift)).astype(F32)
            picked = (v[:, None] * mask[None]).reshape(n * HALF, two)
            for part in split(picked):
                t = mm(part, ones)
                out = t if out is None else out + t
        return out

    own_wl = packed(wg[pl.ds(me, 1)], 0)

    arrived(wg, n_plane - 1, s_w)
    wlp = packed(wg[...], 0)
    whp = packed(wg[...], RANK)
    rows_x.wait()
    rows_o.wait()

    column_a = ca.at[core, :, here_x, lower]
    row_b = ca.at[core, y, :, upper]
    both_ends(column_a, g_a, ny - 1)
    along_x(column_a, g_a2)
    if nx > 1:
        both_ends(row_b, g_b, nx - 1)
    along_y(row_b, g_b2)
    plane_part(lambda j: columns(x, j), xs, s_x, n_plane // 2, n_plane)
    sent.append((xs, n_plane - 1, s_x))
    halves = []
    for span, s_p, n, kind in ((lower, g_a2, nx - 1, 0), (upper, g_b2, ny - 1, 1)):
        if n:
            rest = ca.at[core, :, pl.ds(0, n), span] if kind == 0 else ca.at[core, pl.ds(0, n), :, span]
            for sem in (recv, send):
                pltpu.make_async_copy(rest, rest, sem.at[s_p]).wait()
        whole = ca.at[core, :, :, span]
        s_p = fresh()
        remote(whole, whole, s_p, at_chip(chip, 1 - core)).start()
        halves.append((whole, s_p))
    both = None
    for piece, (whole, s_p) in enumerate(halves):
        pltpu.make_async_copy(whole, whole, recv.at[s_p]).wait()
        base = piece * (WIDE // 2)
        for j in range(n_plane):
            q = j % n_chip
            at = ((q // nx) * xc + (q % nx) * 2 + j // n_chip) * WIDE + base
            own_rows = jnp.concatenate(
                [xr[:, at : at + WIDE // 2], orow[:, at : at + WIDE // 2]], axis=0
            )
            t = mm(own_rows, ca[j // n_chip, q // nx, q % nx, base : base + WIDE // 2])
            both = t if both is None else both + t

    def half_of(ref, which):
        return ref[pl.ds(which * n_chip, n_chip)]

    def spread(v, at):
        return jnp.broadcast_to(v[:, at : at + 1], (tall, two))

    f_own = jnp.where(left_half, (both[:TOK] * sd).astype(BF16).astype(F32), both[TOK:])
    am1[...] = f_own.astype(BF16)
    ab1[me] = am1[...]
    s_g, s_h2 = fresh(), fresh()
    chip_send(lambda q: am1, ab1, me, s_g)
    plane_send(lambda j: columns(o, j), os_, s_o)
    g_wide = None
    for j in range(n_plane):
        c = ca[j // n_chip, (j % n_chip) // nx, j % nx]
        t = mm(c, c, TN)
        g_wide = t if g_wide is None else g_wide + t
    g_wide = g_wide[RANK:]
    c_t = exact(put_r, ca[core, y, here_x].astype(F32), NT)
    nought = jnp.zeros_like(put_l)
    e_top = jnp.concatenate([put_l, nought], axis=0)
    e_top_r = jnp.concatenate([put_r, nought], axis=0)
    e_bot = jnp.concatenate([nought, put_l], axis=0)
    e_bot_r = jnp.concatenate([nought, put_r], axis=0)
    low_p = exact(f_own[:HALF], e_top) + exact(f_own[HALF:], e_top_r)
    ou_p = exact(f_own[:HALF], e_bot) + exact(f_own[HALF:], e_bot_r)
    hot = exact(hot_t, eye, TN)
    hot_l = exact(hot, put_l).astype(BF16)
    hot_r = exact(hot, put_r).astype(BF16)
    arrived(ab1, n_chip - 1, s_g)
    mine_half = ab1.at[pl.ds(core * n_chip, n_chip)]
    sib_send(mine_half, mine_half, s_h2)
    arrived(ab1, n_chip, s_h2)

    g_right = jnp.where(left_half, 0.0, g_wide)
    g_left = pltpu.roll(g_right, RANK, 1)
    g = g_left[:, :RANK]
    g_diag = jnp.concatenate([g_left, g_right], axis=0)
    f_a = ab1[:, :HALF].reshape(tall, two)
    f_b = ab1[:, HALF:].reshape(tall, two)
    k_l = jnp.concatenate([g_left * sr2, put_l * sr], axis=0)
    k_r = jnp.concatenate([g_right * sr2, put_r * sr], axis=0)
    p0 = (whp * (mm2(f_a, k_l) + mm2(f_b, k_r))).astype(BF16)
    def fold(v, a, b):
        return mm(v, a, TN)[:RANK] + mm(v, b, TN)[RANK:]

    own_x.wait()
    arrived(xs, n_plane - 1, s_x)
    x_a = xs[:, :HALF].reshape(tall, WIDE)
    x_b = xs[:, HALF:].reshape(tall, WIDE)
    zp1[...] = (fold(p0, x_a, x_b) * sd).reshape(n_line, chunk, WIDE)
    s_r = line_start(zp1, zb1)
    wfh_a = (f_a.astype(F32) * spread(whp, 0)).astype(BF16)
    wfh_b = (f_b.astype(F32) * spread(whp, RANK)).astype(BF16)
    wfl_a = (f_a.astype(F32) * spread(wlp, 0)).astype(BF16)
    wfl_b = (f_b.astype(F32) * spread(wlp, RANK)).astype(BF16)
    q_h = mm(f_a, wfh_a, TN)[:RANK] + mm(f_b, wfh_b, TN)[:RANK]
    q_l = mm(f_a, wfl_a, TN)[:RANK] + mm(f_b, wfl_b, TN)[:RANK]
    zp1b[:, 1] = jnp.concatenate([q_h, q_l], axis=1).reshape(n_line, chunk, WIDE)
    s_r = line_mid(zb1, zm1, zg1, s_r)
    own_o.wait()
    arrived(os_, n_plane - 1, s_o)
    o_a = os_[:, :HALF].reshape(tall, WIDE)
    o_b = os_[:, HALF:].reshape(tall, WIDE)
    zp1b[:, 0] = (mm(wfh_a, o_a, TN)[:RANK] + mm(wfh_b, o_b, TN)[:RANK]).reshape(n_line, chunk, WIDE)
    s_q = line_start(zp1b, zb1b)
    eu_p = ou_p + sr * exact(low_p, g_diag)
    arrived(zg1, n_line - 1, s_r)

    d_t = zg1[...].reshape(RANK, WIDE)
    nil = jnp.zeros((RANK, WIDE), BF16)

    def apply(v, ref, which, both):
        part = half_of(ref, which)
        a = part[:, :HALF].reshape(n_chip * HALF, WIDE)
        b = part[:, HALF:].reshape(n_chip * HALF, WIDE)
        out = None
        for piece in split(v) if both else (v.astype(BF16),):
            t = mm(a, jnp.concatenate([piece, nil], axis=0), NT) + mm(b, jnp.concatenate([nil, piece], axis=0), NT)
            out = t if out is None else out + t
        return out.reshape(n_chip, HALF, two)

    t2 = sum_start(lambda which: apply(d_t, xs, which, True), po2, sa2, pc2, rb2)
    s_q = line_mid(zb1b, zm1b, zg1b, s_q)

    pair_sems = [fresh(), fresh(), fresh()]

    def hand_over(k, both_halves):
        pair_out[k] = both_halves.T

        @pl.when(paired)
        def _():
            remote(pair_out.at[k], pair_in.at[k], pair_sems[k], partner).start()

        @pl.when(alone)
        def _():
            pair_in[k] = pair_out[k]

    d_l = sum_end(rb2, t2) * sd
    am2[...] = d_l.astype(BF16)
    ab2[me] = am2[...]
    s_a = fresh()
    plane_send(lambda j: am2, ab2, s_a)
    arrived(zg1b, n_line - 1, s_q)
    z_t = zg1b[:, 0].reshape(RANK, WIDE)
    stats = zg1b[:, 1].reshape(RANK, WIDE)
    s_h = stats[:, :RANK]
    zu = pltpu.roll(stats[:, :two], RANK, 1)[:, :RANK]
    s_l = stats[:, two : two + RANK]
    d_m = eye * sr
    d_n = s_h * sr2
    d_tu = exact(d_m, zu, TN) + exact(d_n, g, TN)

    def up_slice(m, n):
        return exact(m, z_t, TN) + exact(n, c_t, TN)

    d_t = jnp.concatenate([d_t, up_slice(d_m, d_n)], axis=0)
    arrived(ab2, n_plane - 1, s_a)
    gathered = ab2[...].reshape(tall, two)

    put_l16, put_r16 = put_l.astype(BF16), put_r.astype(BF16)

    def place(m, put, dims=NN):
        hi, lo = split(m)
        return mm(hi, put, dims) + mm(lo, put, dims)

    def near(a, b):
        a_hi, a_lo = split(a)
        b_hi, b_lo = split(b)
        return mm(a_hi, b_hi) + (mm(a_hi, b_lo) + mm(a_lo, b_hi))

    def image_part(l_p, tu, zp):
        tu_l = jnp.concatenate([place(tu, put_l16), nought], axis=0)
        tu_r = jnp.concatenate([place(tu, put_r16), nought], axis=0)
        inner = mm2(l_p, g_diag) + mm2(f_a, tu_l) + mm2(f_b, tu_r)
        y_p = (wlp * sr2 * inner).astype(BF16)
        down = fold(y_p, x_a, x_b) * sd
        cross = fold(l_p, wfl_a, wfl_b)
        zp[...] = jnp.concatenate([down, cross], axis=1).reshape(n_line, chunk, 3 * two)

    def diag(m):
        return jnp.concatenate([place(m, put_l16), place(m, put_r16)], axis=0)

    def diag_t(m):
        return jnp.concatenate([place(m, put_l16, TN), place(m, put_r16, TN)], axis=0)

    def up_rows(m, n, tu):
        return low_p * (near(oz_p, diag(m)) + late_rows(n, tu))

    def late_rows(n, tu):
        return near(ou_p, diag(n)) + sr * near(low_p, diag_t(tu))

    def by_domain(q, to):
        q_left = jnp.where(left32, q, 0.0)
        q_right = jnp.where(left32, 0.0, q)
        by = place(q_left, to[:HALF], TN) + place(q_right, to[HALF:], TN)
        return sr * jnp.sum(by, axis=0, keepdims=True)

    r_t, r_m, r_n, r_l, r_tu = d_t, d_m, d_n, d_l, d_tu
    first_l, first_m, first_n, first_tu = d_l, d_m, d_n, d_tu
    rounds = (
        (zp2, zb2, zm2, zg2, po3, sa3, pc3, rb3), (zp3, zb3, zm3, zg3, po4, sa4, pc4, rb4),
    )
    steps = []
    for turn, (zp, zb, zm, zg, po, sa, pc, rb) in enumerate(rounds):
        image_part(gathered, d_tu, zp)
        s_z = line_start(zp, zb)
        i_m = sr2 * exact(d_m, s_l) + mu * d_m
        i_n = sr2 * exact(d_n, s_l) + mu * d_n
        i_tu = exact(i_m, zu, TN) + exact(i_n, g, TN)
        i_up = up_slice(i_m, i_n)
        if turn == 0:
            pz[:n_chip] = apply(z_t, os_, 0, False).astype(BF16)
            pz[n_chip:] = apply(z_t, os_, 1, False).astype(BF16)
            s_pz = fresh()
            rz[me] = pz[me]
            plane_send(lambda j: pz.at[j], rz, s_pz)
        else:
            r_lt = near(low_p, diag(r_tu))
            d_lt = near(low_p, diag(d_tu))
        s_z = line_mid(zb, zm, zg, s_z)
        if turn == 0:
            hand_over(0, d_t)
        else:
            third_up = up_rows(i_m, i_n, i_tu)
            d_sv = exact(s_l, d_t[RANK:], TN)
            r_sv = exact(s_l, r_t[RANK:], TN)
        arrived(zg, n_line - 1, s_z)
        full = zg[...].reshape(RANK, 3 * two)
        cross = sr2 * full[:, WIDE : WIDE + RANK]
        i_t = jnp.concatenate(
            [full[:, :WIDE] + mu * d_t[:RANK], i_up + exact(cross, c_t, TN)], axis=0
        )
        note = jnp.zeros((8, two), F32)
        for at, value in enumerate((total(d_t * i_t), total(r_t * i_t), total(i_t * i_t), total(r_t * r_t))):
            note = jnp.where(sub8 == at, value, note)

        def third(which, i_t=i_t, note=note):
            return jnp.concatenate(
                [apply(i_t[:RANK], xs, which, True), jnp.broadcast_to(note[None], (n_chip, 8, two))], axis=1
            )

        t3 = sum_start(third, po, sa, pc, rb)
        cross_tu = exact(cross, g, TN)
        i_n = i_n + cross
        i_tu = i_tu + cross_tu
        if turn == 1:
            third_up = third_up + low_p * late_rows(cross, cross_tu)
            i_lt = near(low_p, diag(i_tu))
            i_sv = exact(s_l, i_t[RANK:], TN)
        s = sum_end(rb, t3)
        i_l = s[:HALF] * sd
        di, ri, ii, r_r = [s[HALF + at : HALF + at + 1, :1] for at in range(4)]
        alpha = r_r / di
        rr = r_r - 2.0 * alpha * ri + alpha * alpha * ii
        beta = rr / r_r
        steps.append((alpha, beta))
        r_l = r_l - alpha * i_l
        d_l = r_l + beta * d_l
        if turn == 0:
            am3[...] = d_l.astype(BF16)
            ab3[me] = am3[...]
            s_a = fresh()
            plane_send(lambda j: am3, ab3, s_a)
            r_tu = r_tu - alpha * i_tu
            d_tu = r_tu + beta * d_tu
            hand_over(1, i_t)
            arrived(rz, n_plane - 1, s_pz)
            oz_p = jnp.sum(rz[...].astype(F32), axis=0)
            second_by = by_domain(i_l * eu_p + up_rows(i_m, i_n, i_tu), hot_r)
            first_by = by_domain(first_l * eu_p + up_rows(first_m, first_n, first_tu), hot_l)
        else:
            d_lt = r_lt - alpha * i_lt + beta * d_lt
            d_sv = r_sv - alpha * i_sv + beta * d_sv
            third_by = by_domain(i_l * eu_p + third_up, hot_l)
        r_t, r_m, r_n = r_t - alpha * i_t, r_m - alpha * i_m, r_n - alpha * i_n
        d_t, d_m, d_n = r_t + beta * d_t, r_m + beta * d_m, r_n + beta * d_n
        if turn == 0:
            arrived(ab3, n_plane - 1, s_a)
            gathered = ab3[...].reshape(tall, two)

    d_lb = d_l.astype(BF16)
    quad = sr2 * own_wl * d_lb.astype(F32) * (mm2(d_lb, g_diag) + 2.0 * d_lt)
    slices = mu * total(d_t * d_t) + sr2 * total(d_sv * d_t[RANK:])
    curve = total(quad) + slices * (1.0 / n_line)
    s_f, s_l2 = fresh(), fresh()
    fm[...] = jnp.where(
        sub8 == 0, first_by + second_by, jnp.where(sub8 == 1, third_by, jnp.where(sub8 == 2, curve, 0.0))
    )
    fb[me] = fm[...]
    plane_send(lambda j: fm, fb, s_f)
    hand_over(2, i_t)
    arrived(fb, n_plane - 1, s_f)
    fq[...] = jnp.sum(fb[...], axis=0)
    fz[z] = fq[...]
    line_send(lambda k: fq, fz, s_l2)
    (a0, b0), (a1, b1) = steps
    for k in range(3):
        @pl.when(paired)
        def _(k=k):
            remote(pair_out.at[k], pair_in.at[k], pair_sems[k], partner).wait()

    @pl.when(alone)
    def _():
        given = ca.at[core, pl.ds(0, n_hi - 1), here_x]
        pltpu.make_async_copy(given, given, send.at[s_c]).wait()

    for whole, s_p in halves:
        pltpu.make_async_copy(whole, whole, send.at[s_p]).wait()
    for buf, n, s in sent[:-1]:
        wait_for(buf, n, send.at[s])
    arrived(fz, n_line - 1, s_l2)
    last = jnp.sum(fz[...], axis=0)
    a2 = rr / last[2:3, :1]
    w0 = a0 + a1 * (1.0 + b0) + a2 * (1.0 + b1 * (1.0 + b0))
    w1 = -a0 * (a1 + a2 * (1.0 + b1))
    w2 = -a1 * a2
    hyp = w0 * last[:1] + w1 * pltpu.roll(last, RANK, 1)[:1] + w2 * last[1:2]
    hyp_out[...] = -kappa * hyp[:, :RANK]
    sol_out[...] = w0 * pair_in[0] + w1 * pair_in[1] + w2 * pair_in[2]
    buf, n, s = sent[-1]
    wait_for(buf, n, send.at[s])


def solution(mesh, xc=8, z_lo=2):
    n_dp, n_fsdp = mesh.shape["dp"], mesh.shape["fsdp"]
    n_plane = (n_dp // z_lo) * xc
    n_line = (n_fsdp // xc) * z_lo
    n_chip = n_plane // 2
    n_sem = 48
    geo = (n_plane, n_line, xc, z_lo, n_sem)
    chunk = RANK // n_line
    two = 2 * RANK
    vm = pltpu.VMEM

    def sums(rows):
        return [vm((n_chip, rows, two), F32)] * 4

    def gather(rows):
        return [vm((rows, two), BF16), vm((n_plane, rows, two), BF16)]

    def line(*shape):
        return [vm((n_line, *shape), F32), vm((n_line, *shape), F32), vm(shape, F32), vm((n_line, *shape), F32)]

    late = vm((n_plane, HALF, two), BF16)
    scratch = [
        vm((n_plane, TOK, WIDE), BF16), vm((n_plane, TOK, WIDE), BF16), vm((2, n_chip // (xc // 2), xc // 2, WIDE, two), BF16),
        vm((n_plane, 8, two), F32), vm((TOK, n_plane * WIDE), BF16), vm((TOK, n_plane * WIDE), BF16),
        *gather(TOK), *line(chunk, WIDE), *line(2, chunk, WIDE),
        *sums(HALF), *gather(HALF), *line(chunk, 3 * two), late, late,
        *sums(HALF + 8), *gather(HALF), *line(chunk, 3 * two),
        *sums(HALF + 8),
        vm((8, two), F32), vm((n_plane, 8, two), F32), vm((8, two), F32), vm((n_line, 8, two), F32),
        vm((3, WIDE, two), F32), vm((3, WIDE, two), F32),
        pltpu.SemaphoreType.DMA((n_sem,)), pltpu.SemaphoreType.DMA((n_sem,)), pltpu.SemaphoreType.DMA((5,)),
    ]
    anywhere = pl.BlockSpec(memory_space=pl.ANY)
    inside = pl.BlockSpec(memory_space=pltpu.VMEM)

    def on_device(x, o, cat, coef, learn, held):
        sol, hyp = pl.pallas_call(
            functools.partial(kernel, geo),
            out_shape=(
                jax.ShapeDtypeStruct((WIDE, two), F32),
                jax.ShapeDtypeStruct((1, RANK), F32),
            ),
            in_specs=[anywhere, anywhere, inside, anywhere, inside, inside],
            out_specs=(inside, inside),
            scratch_shapes=scratch,
            compiler_params=pltpu.CompilerParams(
                collective_id=0, has_side_effects=True, vmem_limit_bytes=56 * 1024 * 1024
            ),
        )(x, o, cat.reshape(1, TOK), coef, learn.reshape(1, DOMAINS), held.reshape(1, DOMAINS))
        return sol, hyp.reshape(DOMAINS)

    placed = (P(("dp", "fsdp"), None), P(("dp", "fsdp"), None), P(("dp", "fsdp")), P("fsdp", None), P(), P())
    return jax.shard_map(
        on_device, mesh=mesh, in_specs=placed, out_specs=(P("fsdp", None), P()), check_vma=False
    )
```

```python
import functools

import jax
import jax.numpy as jnp
from jax import lax
from jax.experimental import pallas as pl
from jax.experimental.pallas import tpu as pltpu
from jax.sharding import PartitionSpec as P

MESH = pl.DeviceIdType.MESH
HIGH = lax.Precision.HIGHEST
RANK = 64
DOMAINS = 64
TOK = 64
HALF = 32
WIDE = 256
F32 = jnp.float32
BF16 = jnp.bfloat16
NN = (((1,), (0,)), ((), ()))
NT = (((1,), (1,)), ((), ()))
TN = (((0,), (0,)), ((), ()))


def mm(a, b, dims=NN):
    return lax.dot_general(a, b, dims, preferred_element_type=F32)


def exact(a, b, dims=NN):
    return lax.dot_general(a, b, dims, precision=HIGH, preferred_element_type=F32)


def split(v):
    hi = v.astype(BF16)
    return hi, (v - hi.astype(F32)).astype(BF16)


def mm2(a, v):
    both = mm(a, jnp.concatenate(split(v), axis=1))
    half = v.shape[1]
    return both[:, :half] + both[:, half:]


def total(v):
    return jnp.sum(v, axis=(0, 1), keepdims=True)


def kernel(geo, x, o, cat, coef, tl, th, sol_out, hyp_out, *scratch):
    n_plane, n_line, xc, z_lo, n_sem = geo
    (
        xs, os_, ca, wg, xr, orow, am1, ab1, zp1, zb1, zm1, zg1, zp1b, zb1b, zm1b, zg1b,
        po2, rb2, am2, ab2, zp2, zb2, zm2, zg2, pz, rz,
        po3, rb3, am3, ab3, zp3, zb3, zm3, zg3,
        po4, rb4, fm, fb, fq, fz, pair_out, pair_in, send, recv, local,
    ) = scratch
    n_chip = n_plane // 2
    nx = xc // 2
    width = n_plane * WIDE
    rows = n_plane * n_line * TOK
    sd = width ** (-0.5)
    sr = RANK ** (-0.5)
    sr2 = 1.0 / RANK
    kappa = DOMAINS / (rows * width)
    mu = 0.1 * DOMAINS / (width * RANK)
    tall = n_plane * HALF
    two = 2 * RANK
    chunk = RANK // n_line

    dp = lax.axis_index("dp")
    fs = lax.axis_index("fsdp")
    y = lax.div(dp, z_lo)
    low_z = lax.rem(dp, z_lo)
    z_hi = lax.div(fs, xc)
    col = lax.rem(fs, xc)
    core = lax.rem(col, 2)
    chip = y * nx + lax.div(col, 2)
    here_x = lax.div(col, 2)
    ny = n_chip // nx
    me = core * n_chip + chip
    z = z_hi * z_lo + low_z

    def at_chip(q, which):
        return (lax.div(q, nx) * z_lo + low_z, z_hi * xc + lax.rem(q, nx) * 2 + which)

    def in_plane(j):
        return at_chip(lax.rem(j, n_chip), lax.div(j, n_chip))

    def in_line(k):
        return (y * z_lo + lax.rem(k, z_lo), lax.div(k, z_lo) * xc + col)

    def shard(j):
        q = lax.rem(j, n_chip)
        return lax.div(q, nx) * xc + lax.rem(q, nx) * 2 + lax.div(j, n_chip)

    partner = (z_hi * z_lo + low_z, y * xc + col)
    paired = y != z_hi
    alone = jnp.logical_not(paired)

    used = [0]

    def fresh():
        used[0] += 1
        assert used[0] <= n_sem
        return used[0] - 1

    sent = []

    def columns(ref, j):
        return ref.at[:, pl.ds(pl.multiple_of(shard(j) * WIDE, WIDE), WIDE)]

    own_x = pltpu.make_async_copy(columns(x, me), xs.at[me], local.at[0])
    own_o = pltpu.make_async_copy(columns(o, me), os_.at[me], local.at[1])
    rows_x = pltpu.make_async_copy(x, xr, local.at[2])
    rows_o = pltpu.make_async_copy(o, orow, local.at[3])
    for copy in (rows_x, rows_o, own_x, own_o):
        copy.start()

    barrier = pltpu.get_barrier_semaphore()

    def greet(i, c):
        pl.semaphore_signal(barrier, inc=1, device_id=in_plane(lax.rem(me + i, n_plane)), device_id_type=MESH)
        return c

    def greet_line(i, c):
        pl.semaphore_signal(barrier, inc=1, device_id=in_line(lax.rem(z + i, n_line)), device_id_type=MESH)
        return c

    lax.fori_loop(1, n_plane, greet, 0)
    lax.fori_loop(1, n_line, greet_line, 0)

    sub = lax.broadcasted_iota(jnp.int32, (RANK, RANK), 0)
    lan = lax.broadcasted_iota(jnp.int32, (RANK, RANK), 1)
    eye = (sub == lan).astype(F32)
    sub2 = lax.broadcasted_iota(jnp.int32, (RANK, two), 0)
    lan2 = lax.broadcasted_iota(jnp.int32, (RANK, two), 1)
    put_l = (lan2 == sub2).astype(F32)
    put_r = (lan2 == sub2 + RANK).astype(F32)
    left_half = lan2 < RANK
    left32 = left_half[:HALF]
    sub8 = lax.broadcasted_iota(jnp.int32, (8, two), 0)
    hot_t = (cat[...] == sub).astype(F32)
    row_w = exact(exact(tl[...], hot_t), put_l) + exact(exact(th[...], hot_t), put_r)
    wg[me] = jnp.broadcast_to(row_w * kappa, (8, two))

    pl.semaphore_wait(barrier, n_plane + n_line - 2)

    def remote(src, dst, s, device):
        return pltpu.make_async_remote_copy(
            src_ref=src, dst_ref=dst, send_sem=send.at[s], recv_sem=recv.at[s], device_id=device, device_id_type=MESH
        )

    def plane_part(src_of, dst, s, first, stop):
        def body(i, c):
            j = lax.rem(me + i, n_plane)
            remote(src_of(j), dst.at[me], s, in_plane(j)).start()
            return c

        lax.fori_loop(first, stop, body, 0)

    def plane_send(src_of, dst, s):
        plane_part(src_of, dst, s, 1, n_plane)
        sent.append((dst, n_plane - 1, s))

    def chip_send(src_of, dst, slot, s):
        def body(i, c):
            q = lax.rem(chip + i, n_chip)
            remote(src_of(q), dst.at[slot], s, at_chip(q, core)).start()
            return c

        lax.fori_loop(1, n_chip, body, 0)
        sent.append((dst, n_chip - 1, s))

    def line_send(src_of, dst, s):
        def body(i, c):
            k = lax.rem(z + i, n_line)
            remote(src_of(k), dst.at[z], s, in_line(k)).start()
            return c

        lax.fori_loop(1, n_line, body, 0)
        sent.append((dst, n_line - 1, s))

    def sib_send(src, dst, s):
        remote(src, dst, s, at_chip(chip, 1 - core)).start()
        sent.append((dst, n_chip, s))

    def wait_for(buf, n, sem):
        part = buf.at[pl.ds(0, n)]
        pltpu.make_async_copy(part, part, sem).wait()

    def arrived(buf, n, s):
        wait_for(buf, n, recv.at[s])

    def sum_start(terms, po, rb):
        t = fresh()
        po[...] = terms
        rb[me] = po[me]
        plane_send(lambda j: po.at[j], rb, t)
        return t

    def sum_end(rb, t):
        arrived(rb, n_plane - 1, t)
        return jnp.sum(rb[...].astype(F32), axis=0)

    def line_start(zp, zb):
        s = fresh()
        zb[z] = zp[z]
        line_send(lambda k: zp.at[k], zb, s)
        return s

    def line_mid(zb, zm, zg, s):
        t = fresh()
        arrived(zb, n_line - 1, s)
        zm[...] = jnp.sum(zb[...], axis=0)
        zg[z] = zm[...]
        line_send(lambda k: zm, zg, t)
        return t

    s_c, s_w, s_x, s_o = fresh(), fresh(), fresh(), fresh()

    own_slot = ca.at[core, y, here_x]
    n_hi = n_line // z_lo
    own_c = pltpu.make_async_copy(coef, own_slot, local.at[4])

    @pl.when(alone)
    def _():
        def body(i, c):
            remote(coef, own_slot, s_c, (dp, lax.rem(z_hi + i, n_hi) * xc + col)).start()
            return c

        lax.fori_loop(1, n_hi, body, 0)
        own_c.start()

    plane_send(lambda j: wg.at[me], wg, s_w)
    plane_part(lambda j: columns(x, j), xs, s_x, 1, n_plane // 2)

    @pl.when(paired)
    def _():
        pltpu.make_async_copy(own_slot, own_slot, recv.at[s_c]).wait()

    @pl.when(alone)
    def _():
        own_c.wait()

    lower = pl.ds(0, WIDE // 2)
    upper = pl.ds(WIDE // 2, WIDE // 2)

    def along_y(ref, s):
        def body(i, c):
            remote(ref, ref, s, at_chip(lax.rem(y + i, ny) * nx + here_x, core)).start()
            return c

        lax.fori_loop(1, ny, body, 0)

    def along_x(ref, s):
        def body(i, c):
            remote(ref, ref, s, at_chip(y * nx + lax.rem(here_x + i, nx), core)).start()
            return c

        lax.fori_loop(1, nx, body, 0)

    def both_ends(part, s, n):
        for sem in (recv, send):
            for_all = part.at[pl.ds(0, n)]
            pltpu.make_async_copy(for_all, for_all, sem.at[s]).wait()

    g_a, g_b, g_a2, g_b2 = fresh(), fresh(), fresh(), fresh()
    along_y(ca.at[core, y, here_x, lower], g_a)
    along_x(ca.at[core, y, here_x, upper], g_b)

    n8 = HALF // 8
    deep = 8 * lax.broadcasted_iota(jnp.int32, (n8, 8, two), 0) + lax.broadcasted_iota(jnp.int32, (n8, 8, two), 1)
    wide = lax.broadcasted_iota(jnp.int32, (n8, 8, two), 2)
    big_l = lax.broadcasted_iota(jnp.int32, (two, two), 1) < RANK
    ones_l = big_l.astype(BF16)
    ones_r = jnp.logical_not(big_l).astype(BF16)

    def packed(v, base):
        n = v.shape[0]
        out = None
        for shift, ones in ((0, ones_l), (HALF, ones_r)):
            mask = (wide == deep + (base + shift)).astype(F32)
            picked = (v[:, None] * mask[None]).reshape(n * HALF, two)
            for part in split(picked):
                t = mm(part, ones)
                out = t if out is None else out + t
        return out

    own_wl = packed(wg[pl.ds(me, 1)], 0)

    arrived(wg, n_plane - 1, s_w)
    wlp = packed(wg[...], 0)
    whp = packed(wg[...], RANK)
    rows_x.wait()
    rows_o.wait()

    column_a = ca.at[core, :, here_x, lower]
    row_b = ca.at[core, y, :, upper]
    both_ends(column_a, g_a, ny - 1)
    along_x(column_a, g_a2)
    if nx > 1:
        both_ends(row_b, g_b, nx - 1)
    along_y(row_b, g_b2)
    plane_part(lambda j: columns(x, j), xs, s_x, n_plane // 2, n_plane)
    sent.append((xs, n_plane - 1, s_x))
    halves = []
    for span, s_p, n, kind in ((lower, g_a2, nx - 1, 0), (upper, g_b2, ny - 1, 1)):
        if n:
            rest = ca.at[core, :, pl.ds(0, n), span] if kind == 0 else ca.at[core, pl.ds(0, n), :, span]
            for sem in (recv, send):
                pltpu.make_async_copy(rest, rest, sem.at[s_p]).wait()
        whole = ca.at[core, :, :, span]
        s_p = fresh()
        remote(whole, whole, s_p, at_chip(chip, 1 - core)).start()
        halves.append((whole, s_p))
    both = None
    for piece, (whole, s_p) in enumerate(halves):
        pltpu.make_async_copy(whole, whole, recv.at[s_p]).wait()
        base = piece * (WIDE // 2)
        for j in range(n_plane):
            q = j % n_chip
            at = ((q // nx) * xc + (q % nx) * 2 + j // n_chip) * WIDE + base
            own_rows = jnp.concatenate(
                [xr[:, at : at + WIDE // 2], orow[:, at : at + WIDE // 2]], axis=0
            )
            t = mm(own_rows, ca[j // n_chip, q // nx, q % nx, base : base + WIDE // 2])
            both = t if both is None else both + t

    def spread(v, at):
        return jnp.broadcast_to(v[:, at : at + 1], (tall, two))

    f_own = jnp.where(left_half, (both[:TOK] * sd).astype(BF16).astype(F32), both[TOK:])
    am1[...] = f_own.astype(BF16)
    ab1[me] = am1[...]
    s_g, s_h2 = fresh(), fresh()
    chip_send(lambda q: am1, ab1, me, s_g)
    plane_send(lambda j: columns(o, j), os_, s_o)
    g_wide = None
    for j in range(n_plane):
        c = ca[j // n_chip, (j % n_chip) // nx, j % nx]
        t = mm(c, c, TN)
        g_wide = t if g_wide is None else g_wide + t
    g_wide = g_wide[RANK:]
    c_t = exact(put_r, ca[core, y, here_x].astype(F32), NT)
    nought = jnp.zeros_like(put_l)
    e_top = jnp.concatenate([put_l, nought], axis=0)
    e_top_r = jnp.concatenate([put_r, nought], axis=0)
    e_bot = jnp.concatenate([nought, put_l], axis=0)
    e_bot_r = jnp.concatenate([nought, put_r], axis=0)
    low_p = exact(f_own[:HALF], e_top) + exact(f_own[HALF:], e_top_r)
    ou_p = exact(f_own[:HALF], e_bot) + exact(f_own[HALF:], e_bot_r)
    hot = exact(hot_t, eye, TN)
    hot_l = exact(hot, put_l).astype(BF16)
    hot_r = exact(hot, put_r).astype(BF16)
    arrived(ab1, n_chip - 1, s_g)
    mine_half = ab1.at[pl.ds(core * n_chip, n_chip)]
    sib_send(mine_half, mine_half, s_h2)
    arrived(ab1, n_chip, s_h2)

    g_right = jnp.where(left_half, 0.0, g_wide)
    g_left = pltpu.roll(g_right, RANK, 1)
    g = g_left[:, :RANK]
    g_diag = jnp.concatenate([g_left, g_right], axis=0)
    f_a = ab1[:, :HALF].reshape(tall, two)
    f_b = ab1[:, HALF:].reshape(tall, two)
    k_l = jnp.concatenate([g_left * sr2, put_l * sr], axis=0)
    k_r = jnp.concatenate([g_right * sr2, put_r * sr], axis=0)
    f_ab = jnp.concatenate([f_a, f_b], axis=1)
    p0 = (whp * mm2(f_ab, jnp.concatenate([k_l, k_r], axis=0))).astype(BF16)
    def fold(v, a, b):
        return mm(v, a, TN)[:RANK] + mm(v, b, TN)[RANK:]

    own_x.wait()
    arrived(xs, n_plane - 1, s_x)
    x_a = xs[:, :HALF].reshape(tall, WIDE)
    x_b = xs[:, HALF:].reshape(tall, WIDE)
    zp1[...] = (fold(p0, x_a, x_b) * sd).reshape(n_line, chunk, WIDE)
    s_r = line_start(zp1, zb1)
    wfh_a = (f_a.astype(F32) * spread(whp, 0)).astype(BF16)
    wfh_b = (f_b.astype(F32) * spread(whp, RANK)).astype(BF16)
    wfl_a = (f_a.astype(F32) * spread(wlp, 0)).astype(BF16)
    wfl_b = (f_b.astype(F32) * spread(wlp, RANK)).astype(BF16)
    q_h = mm(f_a, wfh_a, TN)[:RANK] + mm(f_b, wfh_b, TN)[:RANK]
    q_l = mm(f_a, wfl_a, TN)[:RANK] + mm(f_b, wfl_b, TN)[:RANK]
    zp1b[:, 1] = jnp.concatenate([q_h, q_l], axis=1).reshape(n_line, chunk, WIDE)
    s_r = line_mid(zb1, zm1, zg1, s_r)
    own_o.wait()
    arrived(os_, n_plane - 1, s_o)
    o_a = os_[:, :HALF].reshape(tall, WIDE)
    o_b = os_[:, HALF:].reshape(tall, WIDE)
    zp1b[:, 0] = (mm(wfh_a, o_a, TN)[:RANK] + mm(wfh_b, o_b, TN)[:RANK]).reshape(n_line, chunk, WIDE)
    s_q = line_start(zp1b, zb1b)
    eu_p = ou_p + sr * exact(low_p, g_diag)
    arrived(zg1, n_line - 1, s_r)

    d_t = zg1[...].reshape(RANK, WIDE)
    nil = jnp.zeros((RANK, WIDE), BF16)

    def apply(v, a, b, both):
        parts = split(v) if both else (v.astype(BF16),)
        w_a = jnp.concatenate([w for part in parts for w in (part, nil)], axis=0)
        w_b = jnp.concatenate([w for part in parts for w in (nil, part)], axis=0)
        out = mm(a, w_a, NT) + mm(b, w_b, NT)
        if both:
            out = out[:, :two] + out[:, two:]
        return out.astype(BF16).reshape(n_plane, HALF, two)

    t2 = sum_start(apply(d_t, x_a, x_b, True), po2, rb2)
    s_q = line_mid(zb1b, zm1b, zg1b, s_q)

    pair_sems = [fresh(), fresh(), fresh()]

    def hand_over(k, both_halves):
        pair_out[k] = both_halves.T

        @pl.when(paired)
        def _():
            remote(pair_out.at[k], pair_in.at[k], pair_sems[k], partner).start()

        @pl.when(alone)
        def _():
            pair_in[k] = pair_out[k]

    d_l = sum_end(rb2, t2) * sd
    am2[...] = d_l.astype(BF16)
    ab2[me] = am2[...]
    s_a = fresh()
    plane_send(lambda j: am2, ab2, s_a)
    arrived(zg1b, n_line - 1, s_q)
    z_t = zg1b[:, 0].reshape(RANK, WIDE)
    stats = zg1b[:, 1].reshape(RANK, WIDE)
    s_h = stats[:, :RANK]
    zu = pltpu.roll(stats[:, :two], RANK, 1)[:, :RANK]
    s_l = stats[:, two : two + RANK]
    d_m = eye * sr
    d_n = s_h * sr2
    d_tu = exact(d_m, zu, TN) + exact(d_n, g, TN)

    def up_slice(m, n):
        return exact(m, z_t, TN) + exact(n, c_t, TN)

    d_t = jnp.concatenate([d_t, up_slice(d_m, d_n)], axis=0)
    arrived(ab2, n_plane - 1, s_a)
    gathered = ab2[...].reshape(tall, two)

    put_l16, put_r16 = put_l.astype(BF16), put_r.astype(BF16)

    def place(m, put, dims=NN):
        hi, lo = split(m)
        return mm(hi, put, dims) + mm(lo, put, dims)

    def near(a, b):
        a_hi, a_lo = split(a)
        b_hi, b_lo = split(b)
        return mm(a_hi, b_hi) + (mm(a_hi, b_lo) + mm(a_lo, b_hi))

    def image_part(l_p, tu, zp):
        tu_l = jnp.concatenate([place(tu, put_l16), nought], axis=0)
        tu_r = jnp.concatenate([place(tu, put_r16), nought], axis=0)
        inner = mm2(f_ab, jnp.concatenate([tu_l, tu_r], axis=0)) + mm2(l_p, g_diag)
        y_p = (wlp * sr2 * inner).astype(BF16)
        down = fold(y_p, x_a, x_b) * sd
        cross = fold(l_p, wfl_a, wfl_b)
        zp[...] = jnp.concatenate([down, cross], axis=1).reshape(n_line, chunk, 3 * two)

    def diag(m):
        return jnp.concatenate([place(m, put_l16), place(m, put_r16)], axis=0)

    def diag_t(m):
        return jnp.concatenate([place(m, put_l16, TN), place(m, put_r16, TN)], axis=0)

    def up_rows(m, n, tu):
        return low_p * (near(oz_p, diag(m)) + late_rows(n, tu))

    def late_rows(n, tu):
        return near(ou_p, diag(n)) + sr * near(low_p, diag_t(tu))

    def by_domain(q, to):
        q_left = jnp.where(left32, q, 0.0)
        q_right = jnp.where(left32, 0.0, q)
        by = place(q_left, to[:HALF], TN) + place(q_right, to[HALF:], TN)
        return sr * jnp.sum(by, axis=0, keepdims=True)

    r_t, r_m, r_n, r_l, r_tu = d_t, d_m, d_n, d_l, d_tu
    first_l, first_m, first_n, first_tu = d_l, d_m, d_n, d_tu
    rounds = (
        (zp2, zb2, zm2, zg2, po3, rb3), (zp3, zb3, zm3, zg3, po4, rb4),
    )
    steps = []
    for turn, (zp, zb, zm, zg, po, rb) in enumerate(rounds):
        image_part(gathered, d_tu, zp)
        s_z = line_start(zp, zb)
        i_m = sr2 * exact(d_m, s_l) + mu * d_m
        i_n = sr2 * exact(d_n, s_l) + mu * d_n
        i_tu = exact(i_m, zu, TN) + exact(i_n, g, TN)
        i_up = up_slice(i_m, i_n)
        if turn == 0:
            pz[...] = apply(z_t, o_a, o_b, False)
            s_pz = fresh()
            rz[me] = pz[me]
            plane_send(lambda j: pz.at[j], rz, s_pz)
        else:
            r_lt = near(low_p, diag(r_tu))
            d_lt = near(low_p, diag(d_tu))
        s_z = line_mid(zb, zm, zg, s_z)
        if turn == 0:
            hand_over(0, d_t)
        else:
            third_up = up_rows(i_m, i_n, i_tu)
            d_sv = exact(s_l, d_t[RANK:], TN)
            r_sv = exact(s_l, r_t[RANK:], TN)
        arrived(zg, n_line - 1, s_z)
        full = zg[...].reshape(RANK, 3 * two)
        cross = sr2 * full[:, WIDE : WIDE + RANK]
        i_t = jnp.concatenate(
            [full[:, :WIDE] + mu * d_t[:RANK], i_up + exact(cross, c_t, TN)], axis=0
        )
        note = jnp.zeros((8, two), F32)
        for at, value in enumerate((total(d_t * i_t), total(r_t * i_t), total(i_t * i_t), total(r_t * r_t))):
            note = jnp.where(sub8 == at, value, note)

        note = jnp.concatenate([part.astype(F32) for part in split(note)], axis=0).astype(BF16)
        terms = jnp.concatenate(
            [apply(i_t[:RANK], x_a, x_b, True), jnp.broadcast_to(note[None], (n_plane, 16, two))], axis=1
        )
        t3 = sum_start(terms, po, rb)
        cross_tu = exact(cross, g, TN)
        i_n = i_n + cross
        i_tu = i_tu + cross_tu
        if turn == 1:
            third_up = third_up + low_p * late_rows(cross, cross_tu)
            i_lt = near(low_p, diag(i_tu))
            i_sv = exact(s_l, i_t[RANK:], TN)
        s = sum_end(rb, t3)
        i_l = s[:HALF] * sd
        sums = s[HALF : HALF + 8] + s[HALF + 8 :]
        di, ri, ii, r_r = [sums[at : at + 1, :1] for at in range(4)]
        alpha = r_r / di
        rr = r_r - 2.0 * alpha * ri + alpha * alpha * ii
        beta = rr / r_r
        steps.append((alpha, beta))
        r_l = r_l - alpha * i_l
        d_l = r_l + beta * d_l
        if turn == 0:
            am3[...] = d_l.astype(BF16)
            ab3[me] = am3[...]
            s_a = fresh()
            plane_send(lambda j: am3, ab3, s_a)
            r_tu = r_tu - alpha * i_tu
            d_tu = r_tu + beta * d_tu
            hand_over(1, i_t)
            arrived(rz, n_plane - 1, s_pz)
            oz_p = jnp.sum(rz[...].astype(F32), axis=0)
            second_by = by_domain(i_l * eu_p + up_rows(i_m, i_n, i_tu), hot_r)
            first_by = by_domain(first_l * eu_p + up_rows(first_m, first_n, first_tu), hot_l)
        else:
            d_lt = r_lt - alpha * i_lt + beta * d_lt
            d_sv = r_sv - alpha * i_sv + beta * d_sv
            third_by = by_domain(i_l * eu_p + third_up, hot_l)
        r_t, r_m, r_n = r_t - alpha * i_t, r_m - alpha * i_m, r_n - alpha * i_n
        d_t, d_m, d_n = r_t + beta * d_t, r_m + beta * d_m, r_n + beta * d_n
        if turn == 0:
            arrived(ab3, n_plane - 1, s_a)
            gathered = ab3[...].reshape(tall, two)

    d_lb = d_l.astype(BF16)
    quad = sr2 * own_wl * d_lb.astype(F32) * (mm2(d_lb, g_diag) + 2.0 * d_lt)
    slices = mu * total(d_t * d_t) + sr2 * total(d_sv * d_t[RANK:])
    curve = total(quad) + slices * (1.0 / n_line)
    s_f, s_l2 = fresh(), fresh()
    fm[...] = jnp.where(
        sub8 == 0, first_by + second_by, jnp.where(sub8 == 1, third_by, jnp.where(sub8 == 2, curve, 0.0))
    )
    fb[me] = fm[...]
    plane_send(lambda j: fm, fb, s_f)
    hand_over(2, i_t)
    arrived(fb, n_plane - 1, s_f)
    fq[...] = jnp.sum(fb[...], axis=0)
    fz[z] = fq[...]
    line_send(lambda k: fq, fz, s_l2)
    (a0, b0), (a1, b1) = steps
    for k in range(3):
        @pl.when(paired)
        def _(k=k):
            remote(pair_out.at[k], pair_in.at[k], pair_sems[k], partner).wait()

    @pl.when(alone)
    def _():
        given = ca.at[core, pl.ds(0, n_hi - 1), here_x]
        pltpu.make_async_copy(given, given, send.at[s_c]).wait()

    for whole, s_p in halves:
        pltpu.make_async_copy(whole, whole, send.at[s_p]).wait()
    for buf, n, s in sent[:-1]:
        wait_for(buf, n, send.at[s])
    arrived(fz, n_line - 1, s_l2)
    last = jnp.sum(fz[...], axis=0)
    a2 = rr / last[2:3, :1]
    w0 = a0 + a1 * (1.0 + b0) + a2 * (1.0 + b1 * (1.0 + b0))
    w1 = -a0 * (a1 + a2 * (1.0 + b1))
    w2 = -a1 * a2
    hyp = w0 * last[:1] + w1 * pltpu.roll(last, RANK, 1)[:1] + w2 * last[1:2]
    hyp_out[...] = -kappa * hyp[:, :RANK]
    sol_out[...] = w0 * pair_in[0] + w1 * pair_in[1] + w2 * pair_in[2]
    buf, n, s = sent[-1]
    wait_for(buf, n, send.at[s])


def solution(mesh, xc=8, z_lo=2):
    n_dp, n_fsdp = mesh.shape["dp"], mesh.shape["fsdp"]
    n_plane = (n_dp // z_lo) * xc
    n_line = (n_fsdp // xc) * z_lo
    n_chip = n_plane // 2
    n_sem = 48
    geo = (n_plane, n_line, xc, z_lo, n_sem)
    chunk = RANK // n_line
    two = 2 * RANK
    vm = pltpu.VMEM

    def sums(rows):
        return [vm((n_plane, rows, two), BF16)] * 2

    def gather(rows):
        return [vm((rows, two), BF16), vm((n_plane, rows, two), BF16)]

    def line(*shape):
        return [vm((n_line, *shape), F32), vm((n_line, *shape), F32), vm(shape, F32), vm((n_line, *shape), F32)]

    late = vm((n_plane, HALF, two), BF16)
    scratch = [
        vm((n_plane, TOK, WIDE), BF16), vm((n_plane, TOK, WIDE), BF16), vm((2, n_chip // (xc // 2), xc // 2, WIDE, two), BF16),
        vm((n_plane, 8, two), F32), vm((TOK, n_plane * WIDE), BF16), vm((TOK, n_plane * WIDE), BF16),
        *gather(TOK), *line(chunk, WIDE), *line(2, chunk, WIDE),
        *sums(HALF), *gather(HALF), *line(chunk, 3 * two), late, late,
        *sums(HALF + 16), *gather(HALF), *line(chunk, 3 * two),
        *sums(HALF + 16),
        vm((8, two), F32), vm((n_plane, 8, two), F32), vm((8, two), F32), vm((n_line, 8, two), F32),
        vm((3, WIDE, two), F32), vm((3, WIDE, two), F32),
        pltpu.SemaphoreType.DMA((n_sem,)), pltpu.SemaphoreType.DMA((n_sem,)), pltpu.SemaphoreType.DMA((5,)),
    ]
    anywhere = pl.BlockSpec(memory_space=pl.ANY)
    inside = pl.BlockSpec(memory_space=pltpu.VMEM)

    def on_device(x, o, cat, coef, learn, held):
        sol, hyp = pl.pallas_call(
            functools.partial(kernel, geo),
            out_shape=(
                jax.ShapeDtypeStruct((WIDE, two), F32),
                jax.ShapeDtypeStruct((1, RANK), F32),
            ),
            in_specs=[anywhere, anywhere, inside, anywhere, inside, inside],
            out_specs=(inside, inside),
            scratch_shapes=scratch,
            compiler_params=pltpu.CompilerParams(
                collective_id=0, has_side_effects=True, vmem_limit_bytes=56 * 1024 * 1024
            ),
        )(x, o, cat.reshape(1, TOK), coef, learn.reshape(1, DOMAINS), held.reshape(1, DOMAINS))
        return sol, hyp.reshape(DOMAINS)

    placed = (P(("dp", "fsdp"), None), P(("dp", "fsdp"), None), P(("dp", "fsdp")), P("fsdp", None), P(), P())
    return jax.shard_map(
        on_device, mesh=mesh, in_specs=placed, out_specs=(P("fsdp", None), P()), check_vma=False
    )
```

```python
import functools

import jax
import jax.numpy as jnp
from jax import lax
from jax.experimental import pallas as pl
from jax.experimental.pallas import tpu as pltpu
from jax.sharding import PartitionSpec as P

MESH = pl.DeviceIdType.MESH
HIGH = lax.Precision.HIGHEST
RANK = 64
DOMAINS = 64
TOK = 64
HALF = 32
WIDE = 256
F32 = jnp.float32
BF16 = jnp.bfloat16
NN = (((1,), (0,)), ((), ()))
NT = (((1,), (1,)), ((), ()))
TN = (((0,), (0,)), ((), ()))


def mm(a, b, dims=NN):
    return lax.dot_general(a, b, dims, preferred_element_type=F32)


def exact(a, b, dims=NN):
    return lax.dot_general(a, b, dims, precision=HIGH, preferred_element_type=F32)


def split(v):
    hi = v.astype(BF16)
    return hi, (v - hi.astype(F32)).astype(BF16)


def mm2(a, v):
    both = mm(a, jnp.concatenate(split(v), axis=1))
    half = v.shape[1]
    return both[:, :half] + both[:, half:]


def total(v):
    return jnp.sum(v, axis=(0, 1), keepdims=True)


def kernel(geo, x, o, cat, coef, tl, th, sol_out, hyp_out, *scratch):
    n_plane, n_line, xc, z_lo, n_sem = geo
    (
        xs, os_, ca, wg, xr, orow, am1, ab1, zp1, zb1, zm1, zg1, zp1b, zb1b, zm1b, zg1b,
        po2, rb2, am2, ab2, zp2, zb2, pz, rz,
        po3, rb3, am3, ab3, zp3, zb3,
        po4, rb4, fm, fb, fq, fz, pair_out, pair_in, send, recv, local,
    ) = scratch
    n_chip = n_plane // 2
    nx = xc // 2
    width = n_plane * WIDE
    rows = n_plane * n_line * TOK
    sd = width ** (-0.5)
    sr = RANK ** (-0.5)
    sr2 = 1.0 / RANK
    kappa = DOMAINS / (rows * width)
    mu = 0.1 * DOMAINS / (width * RANK)
    tall = n_plane * HALF
    two = 2 * RANK
    chunk = RANK // n_line

    dp = lax.axis_index("dp")
    fs = lax.axis_index("fsdp")
    y = lax.div(dp, z_lo)
    low_z = lax.rem(dp, z_lo)
    z_hi = lax.div(fs, xc)
    col = lax.rem(fs, xc)
    core = lax.rem(col, 2)
    chip = y * nx + lax.div(col, 2)
    here_x = lax.div(col, 2)
    ny = n_chip // nx
    me = core * n_chip + chip
    z = z_hi * z_lo + low_z

    def at_chip(q, which):
        return (lax.div(q, nx) * z_lo + low_z, z_hi * xc + lax.rem(q, nx) * 2 + which)

    def in_plane(j):
        return at_chip(lax.rem(j, n_chip), lax.div(j, n_chip))

    def in_line(k):
        return (y * z_lo + lax.rem(k, z_lo), lax.div(k, z_lo) * xc + col)

    def shard(j):
        q = lax.rem(j, n_chip)
        return lax.div(q, nx) * xc + lax.rem(q, nx) * 2 + lax.div(j, n_chip)

    partner = (z_hi * z_lo + low_z, y * xc + col)
    paired = y != z_hi
    alone = jnp.logical_not(paired)

    used = [0]

    def fresh():
        used[0] += 1
        assert used[0] <= n_sem
        return used[0] - 1

    sent = []

    def columns(ref, j):
        return ref.at[:, pl.ds(pl.multiple_of(shard(j) * WIDE, WIDE), WIDE)]

    own_x = pltpu.make_async_copy(columns(x, me), xs.at[me], local.at[0])
    own_o = pltpu.make_async_copy(columns(o, me), os_.at[me], local.at[1])
    rows_x = pltpu.make_async_copy(x, xr, local.at[2])
    rows_o = pltpu.make_async_copy(o, orow, local.at[3])
    for copy in (rows_x, rows_o, own_x, own_o):
        copy.start()

    by_far = sorted(range(nx), key=lambda d: -min(d, nx - d))

    def over_plane(go, cores):
        def at_row(yy, steps):
            for d in steps:
                xx = lax.rem(here_x + d, nx)
                for e in range(cores):
                    which = lax.rem(core + e, 2)
                    go(which * n_chip + yy * nx + xx, (yy * z_lo + low_z, z_hi * xc + xx * 2 + which))

        def far(t, c):
            d = ny // 2 - t + (ny - 1) * lax.div(t, ny // 2)
            at_row(lax.rem(y + d, ny), by_far)
            return c

        lax.fori_loop(0, ny - 1, far, 0)
        at_row(y, [d for d in by_far if d])
        if cores == 2:
            go((1 - core) * n_chip + chip, at_chip(chip, 1 - core))

    barrier = pltpu.get_barrier_semaphore()

    def greet_line(i, c):
        pl.semaphore_signal(barrier, inc=1, device_id=in_line(lax.rem(z + i, n_line)), device_id_type=MESH)
        return c

    lax.fori_loop(1, n_line, greet_line, 0)
    over_plane(
        lambda j, device: pl.semaphore_signal(barrier, inc=1, device_id=device, device_id_type=MESH), 2
    )

    sub = lax.broadcasted_iota(jnp.int32, (RANK, RANK), 0)
    lan = lax.broadcasted_iota(jnp.int32, (RANK, RANK), 1)
    eye = (sub == lan).astype(F32)
    sub2 = lax.broadcasted_iota(jnp.int32, (RANK, two), 0)
    lan2 = lax.broadcasted_iota(jnp.int32, (RANK, two), 1)
    put_l = (lan2 == sub2).astype(F32)
    put_r = (lan2 == sub2 + RANK).astype(F32)
    left_half = lan2 < RANK
    left32 = left_half[:HALF]
    sub8 = lax.broadcasted_iota(jnp.int32, (8, two), 0)
    hot_t = (cat[...] == sub).astype(F32)
    row_w = exact(exact(tl[...], hot_t), put_l) + exact(exact(th[...], hot_t), put_r)
    wg[me] = jnp.broadcast_to(row_w * kappa, (8, two))

    pl.semaphore_wait(barrier, n_plane + n_line - 2)

    def remote(src, dst, s, device):
        return pltpu.make_async_remote_copy(
            src_ref=src, dst_ref=dst, send_sem=send.at[s], recv_sem=recv.at[s], device_id=device, device_id_type=MESH
        )

    def plane_part(src_of, dst, s, first, stop):
        def body(i, c):
            j = lax.rem(me + i, n_plane)
            remote(src_of(j), dst.at[me], s, in_plane(j)).start()
            return c

        lax.fori_loop(first, stop, body, 0)

    def plane_send(src_of, dst, s):
        over_plane(lambda j, device: remote(src_of(j), dst.at[me], s, device).start(), 2)
        sent.append((dst, n_plane - 1, s))

    def chip_send(src_of, dst, slot, s):
        over_plane(lambda j, device: remote(src_of(j), dst.at[slot], s, device).start(), 1)
        sent.append((dst, n_chip - 1, s))

    def line_send(src_of, dst, s):
        def body(i, c):
            k = lax.rem(z + i, n_line)
            remote(src_of(k), dst.at[z], s, in_line(k)).start()
            return c

        lax.fori_loop(1, n_line, body, 0)
        sent.append((dst, n_line - 1, s))

    def sib_send(src, dst, s):
        remote(src, dst, s, at_chip(chip, 1 - core)).start()
        sent.append((dst, n_chip, s))

    def wait_for(buf, n, sem):
        part = buf.at[pl.ds(0, n)]
        pltpu.make_async_copy(part, part, sem).wait()

    def arrived(buf, n, s):
        wait_for(buf, n, recv.at[s])

    def sum_start(terms, po, rb):
        t = fresh()
        po[...] = terms
        rb[me] = po[me]
        plane_send(lambda j: po.at[j], rb, t)
        return t

    def sum_end(rb, t):
        arrived(rb, n_plane - 1, t)
        return jnp.sum(rb[...].astype(F32), axis=0)

    def line_start(zp, zb):
        s = fresh()
        zb[z] = zp[z]
        line_send(lambda k: zp.at[k], zb, s)
        return s

    def line_mid(zb, zm, zg, s):
        t = fresh()
        arrived(zb, n_line - 1, s)
        zm[...] = jnp.sum(zb[...], axis=0)
        zg[z] = zm[...]
        line_send(lambda k: zm, zg, t)
        return t

    s_c, s_w, s_x, s_o = fresh(), fresh(), fresh(), fresh()

    own_slot = ca.at[core, y, here_x]
    n_hi = n_line // z_lo
    own_c = pltpu.make_async_copy(coef, own_slot, local.at[4])

    @pl.when(alone)
    def _():
        def body(i, c):
            remote(coef, own_slot, s_c, (dp, lax.rem(z_hi + i, n_hi) * xc + col)).start()
            return c

        lax.fori_loop(1, n_hi, body, 0)
        own_c.start()

    plane_send(lambda j: wg.at[me], wg, s_w)
    plane_part(lambda j: columns(x, j), xs, s_x, 1, n_plane // 2)

    @pl.when(paired)
    def _():
        pltpu.make_async_copy(own_slot, own_slot, recv.at[s_c]).wait()

    @pl.when(alone)
    def _():
        own_c.wait()

    lower = pl.ds(0, WIDE // 2)
    upper = pl.ds(WIDE // 2, WIDE // 2)

    def along_y(ref, s):
        def body(i, c):
            remote(ref, ref, s, at_chip(lax.rem(y + i, ny) * nx + here_x, core)).start()
            return c

        lax.fori_loop(1, ny, body, 0)

    def along_x(ref, s):
        def body(i, c):
            remote(ref, ref, s, at_chip(y * nx + lax.rem(here_x + i, nx), core)).start()
            return c

        lax.fori_loop(1, nx, body, 0)

    def both_ends(part, s, n):
        for sem in (recv, send):
            for_all = part.at[pl.ds(0, n)]
            pltpu.make_async_copy(for_all, for_all, sem.at[s]).wait()

    g_a, g_b, g_a2, g_b2 = fresh(), fresh(), fresh(), fresh()
    along_y(ca.at[core, y, here_x, lower], g_a)
    along_x(ca.at[core, y, here_x, upper], g_b)

    n8 = HALF // 8
    deep = 8 * lax.broadcasted_iota(jnp.int32, (n8, 8, two), 0) + lax.broadcasted_iota(jnp.int32, (n8, 8, two), 1)
    wide = lax.broadcasted_iota(jnp.int32, (n8, 8, two), 2)
    big_l = lax.broadcasted_iota(jnp.int32, (two, two), 1) < RANK
    ones_l = big_l.astype(BF16)
    ones_r = jnp.logical_not(big_l).astype(BF16)

    def packed(v, base):
        n = v.shape[0]
        out = None
        for shift, ones in ((0, ones_l), (HALF, ones_r)):
            mask = (wide == deep + (base + shift)).astype(F32)
            picked = (v[:, None] * mask[None]).reshape(n * HALF, two)
            for part in split(picked):
                t = mm(part, ones)
                out = t if out is None else out + t
        return out

    own_wl = packed(wg[pl.ds(me, 1)], 0)

    arrived(wg, n_plane - 1, s_w)
    wlp = packed(wg[...], 0)
    whp = packed(wg[...], RANK)
    rows_x.wait()
    rows_o.wait()

    column_a = ca.at[core, :, here_x, lower]
    row_b = ca.at[core, y, :, upper]
    both_ends(column_a, g_a, ny - 1)
    along_x(column_a, g_a2)
    if nx > 1:
        both_ends(row_b, g_b, nx - 1)
    along_y(row_b, g_b2)
    plane_part(lambda j: columns(x, j), xs, s_x, n_plane // 2, n_plane)
    sent.append((xs, n_plane - 1, s_x))
    halves = []
    for span, s_p, n, kind in ((lower, g_a2, nx - 1, 0), (upper, g_b2, ny - 1, 1)):
        if n:
            rest = ca.at[core, :, pl.ds(0, n), span] if kind == 0 else ca.at[core, pl.ds(0, n), :, span]
            for sem in (recv, send):
                pltpu.make_async_copy(rest, rest, sem.at[s_p]).wait()
        whole = ca.at[core, :, :, span]
        s_p = fresh()
        remote(whole, whole, s_p, at_chip(chip, 1 - core)).start()
        halves.append((whole, s_p))
    both = None
    for piece, (whole, s_p) in enumerate(halves):
        pltpu.make_async_copy(whole, whole, recv.at[s_p]).wait()
        base = piece * (WIDE // 2)
        for j in range(n_plane):
            q = j % n_chip
            at = ((q // nx) * xc + (q % nx) * 2 + j // n_chip) * WIDE + base
            own_rows = jnp.concatenate(
                [xr[:, at : at + WIDE // 2], orow[:, at : at + WIDE // 2]], axis=0
            )
            t = mm(own_rows, ca[j // n_chip, q // nx, q % nx, base : base + WIDE // 2])
            both = t if both is None else both + t

    def spread(v, at):
        return jnp.broadcast_to(v[:, at : at + 1], (tall, two))

    f_own = jnp.where(left_half, (both[:TOK] * sd).astype(BF16).astype(F32), both[TOK:])
    am1[...] = f_own.astype(BF16)
    ab1[me] = am1[...]
    s_g, s_h2 = fresh(), fresh()
    chip_send(lambda q: am1, ab1, me, s_g)
    plane_part(lambda j: columns(o, j), os_, s_o, 1, n_plane)
    sent.append((os_, n_plane - 1, s_o))
    g_wide = None
    for j in range(n_plane):
        c = ca[j // n_chip, (j % n_chip) // nx, j % nx]
        t = mm(c, c, TN)
        g_wide = t if g_wide is None else g_wide + t
    g_wide = g_wide[RANK:]
    c_t = exact(put_r, ca[core, y, here_x].astype(F32), NT)
    nought = jnp.zeros_like(put_l)
    e_top = jnp.concatenate([put_l, nought], axis=0)
    e_top_r = jnp.concatenate([put_r, nought], axis=0)
    e_bot = jnp.concatenate([nought, put_l], axis=0)
    e_bot_r = jnp.concatenate([nought, put_r], axis=0)
    low_p = exact(f_own[:HALF], e_top) + exact(f_own[HALF:], e_top_r)
    ou_p = exact(f_own[:HALF], e_bot) + exact(f_own[HALF:], e_bot_r)
    hot = exact(hot_t, eye, TN)
    hot_l = exact(hot, put_l).astype(BF16)
    hot_r = exact(hot, put_r).astype(BF16)
    arrived(ab1, n_chip - 1, s_g)
    mine_half = ab1.at[pl.ds(core * n_chip, n_chip)]
    sib_send(mine_half, mine_half, s_h2)
    arrived(ab1, n_chip, s_h2)

    g_right = jnp.where(left_half, 0.0, g_wide)
    g_left = pltpu.roll(g_right, RANK, 1)
    g = g_left[:, :RANK]
    g_diag = jnp.concatenate([g_left, g_right], axis=0)
    f_a = ab1[:, :HALF].reshape(tall, two)
    f_b = ab1[:, HALF:].reshape(tall, two)
    k_l = jnp.concatenate([g_left * sr2, put_l * sr], axis=0)
    k_r = jnp.concatenate([g_right * sr2, put_r * sr], axis=0)
    f_ab = jnp.concatenate([f_a, f_b], axis=1)
    p0 = (whp * mm2(f_ab, jnp.concatenate([k_l, k_r], axis=0))).astype(BF16)
    def fold(v, a, b):
        return mm(v, a, TN)[:RANK] + mm(v, b, TN)[RANK:]

    own_x.wait()
    arrived(xs, n_plane - 1, s_x)
    x_a = xs[:, :HALF].reshape(tall, WIDE)
    x_b = xs[:, HALF:].reshape(tall, WIDE)
    zp1[...] = (fold(p0, x_a, x_b) * sd).reshape(n_line, chunk, WIDE)
    s_r = line_start(zp1, zb1)
    wfh_a = (f_a.astype(F32) * spread(whp, 0)).astype(BF16)
    wfh_b = (f_b.astype(F32) * spread(whp, RANK)).astype(BF16)
    wfl_a = (f_a.astype(F32) * spread(wlp, 0)).astype(BF16)
    wfl_b = (f_b.astype(F32) * spread(wlp, RANK)).astype(BF16)
    q_h = mm(f_a, wfh_a, TN)[:RANK] + mm(f_b, wfh_b, TN)[:RANK]
    q_l = mm(f_a, wfl_a, TN)[:RANK] + mm(f_b, wfl_b, TN)[:RANK]
    zp1b[:, 1] = jnp.concatenate([q_h, q_l], axis=1).reshape(n_line, chunk, WIDE)
    s_r = line_mid(zb1, zm1, zg1, s_r)
    own_o.wait()
    arrived(os_, n_plane - 1, s_o)
    o_a = os_[:, :HALF].reshape(tall, WIDE)
    o_b = os_[:, HALF:].reshape(tall, WIDE)
    zp1b[:, 0] = (mm(wfh_a, o_a, TN)[:RANK] + mm(wfh_b, o_b, TN)[:RANK]).reshape(n_line, chunk, WIDE)
    s_q = line_start(zp1b, zb1b)
    eu_p = ou_p + sr * exact(low_p, g_diag)
    arrived(zg1, n_line - 1, s_r)

    d_t = zg1[...].reshape(RANK, WIDE)
    nil = jnp.zeros((RANK, WIDE), BF16)

    def apply(v, a, b, both):
        parts = split(v) if both else (v.astype(BF16),)
        w_a = jnp.concatenate([w for part in parts for w in (part, nil)], axis=0)
        w_b = jnp.concatenate([w for part in parts for w in (nil, part)], axis=0)
        out = mm(a, w_a, NT) + mm(b, w_b, NT)
        if both:
            out = out[:, :two] + out[:, two:]
        return out.astype(BF16).reshape(n_plane, HALF, two)

    t2 = sum_start(apply(d_t, x_a, x_b, True), po2, rb2)
    s_q = line_mid(zb1b, zm1b, zg1b, s_q)

    pair_sems = [fresh(), fresh(), fresh()]

    def hand_over(k, both_halves):
        pair_out[k] = both_halves.T

        @pl.when(paired)
        def _():
            remote(pair_out.at[k], pair_in.at[k], pair_sems[k], partner).start()

        @pl.when(alone)
        def _():
            pair_in[k] = pair_out[k]

    d_l = sum_end(rb2, t2) * sd
    am2[...] = d_l.astype(BF16)
    ab2[me] = am2[...]
    s_a = fresh()
    plane_send(lambda j: am2, ab2, s_a)
    arrived(zg1b, n_line - 1, s_q)
    z_t = zg1b[:, 0].reshape(RANK, WIDE)
    stats = zg1b[:, 1].reshape(RANK, WIDE)
    s_h = stats[:, :RANK]
    zu = pltpu.roll(stats[:, :two], RANK, 1)[:, :RANK]
    s_l = stats[:, two : two + RANK]
    d_m = eye * sr
    d_n = s_h * sr2
    d_tu = exact(d_m, zu, TN) + exact(d_n, g, TN)

    def up_slice(m, n):
        return exact(m, z_t, TN) + exact(n, c_t, TN)

    d_t = jnp.concatenate([d_t, up_slice(d_m, d_n)], axis=0)

    put_l16, put_r16 = put_l.astype(BF16), put_r.astype(BF16)

    def place(m, put, dims=NN):
        hi, lo = split(m)
        return mm(hi, put, dims) + mm(lo, put, dims)

    def near(a, b):
        a_hi, a_lo = split(a)
        b_hi, b_lo = split(b)
        return mm(a_hi, b_hi) + (mm(a_hi, b_lo) + mm(a_lo, b_hi))

    def with_low(tu):
        tu_l = jnp.concatenate([place(tu, put_l16), nought], axis=0)
        tu_r = jnp.concatenate([place(tu, put_r16), nought], axis=0)
        return mm2(f_ab, jnp.concatenate([tu_l, tu_r], axis=0))

    def image_part(l_p, inner, zp):
        y_p = (wlp * sr2 * (inner + mm2(l_p, g_diag))).astype(BF16)
        down = fold(y_p, x_a, x_b) * sd
        cross = fold(l_p, wfl_a, wfl_b)
        cross = jnp.where(left32, cross[:HALF], pltpu.roll(cross[HALF:], RANK, 1))
        zp[...] = jnp.concatenate([down[:, :two], down[:, two:], cross], axis=0).astype(BF16)

    inner = with_low(d_tu)
    arrived(ab2, n_plane - 1, s_a)
    gathered = ab2[...].reshape(tall, two)

    def diag(m):
        return jnp.concatenate([place(m, put_l16), place(m, put_r16)], axis=0)

    def diag_t(m):
        return jnp.concatenate([place(m, put_l16, TN), place(m, put_r16, TN)], axis=0)

    def up_rows(m, n, tu):
        return low_p * (near(oz_p, diag(m)) + late_rows(n, tu))

    def late_rows(n, tu):
        return near(ou_p, diag(n)) + sr * near(low_p, diag_t(tu))

    def by_domain(q, to):
        q_left = jnp.where(left32, q, 0.0)
        q_right = jnp.where(left32, 0.0, q)
        by = place(q_left, to[:HALF], TN) + place(q_right, to[HALF:], TN)
        return sr * jnp.sum(by, axis=0, keepdims=True)

    r_t, r_m, r_n, r_l, r_tu = d_t, d_m, d_n, d_l, d_tu
    first_l, first_m, first_n, first_tu = d_l, d_m, d_n, d_tu
    rounds = (
        (zp2, zb2, po3, rb3), (zp3, zb3, po4, rb4),
    )
    steps = []
    for turn, (zp, zb, po, rb) in enumerate(rounds):
        image_part(gathered, inner, zp)
        s_z = fresh()
        zb[z] = zp[...]
        line_send(lambda k: zp, zb, s_z)
        i_m = sr2 * exact(d_m, s_l) + mu * d_m
        i_n = sr2 * exact(d_n, s_l) + mu * d_n
        i_tu = exact(i_m, zu, TN) + exact(i_n, g, TN)
        i_up = up_slice(i_m, i_n)
        if turn == 0:
            pz[...] = apply(z_t, o_a, o_b, False)
            s_pz = fresh()
            rz[me] = pz[me]
            plane_send(lambda j: pz.at[j], rz, s_pz)
        else:
            r_lt = near(low_p, diag(r_tu))
            d_lt = near(low_p, diag(d_tu))
        r_r_part = total(r_t * r_t)
        if turn == 0:
            hand_over(0, d_t)
        else:
            third_up = up_rows(i_m, i_n, i_tu)
            d_sv = exact(s_l, d_t[RANK:], TN)
            r_sv = exact(s_l, r_t[RANK:], TN)
        arrived(zb, n_line - 1, s_z)
        full = jnp.sum(zb[...].astype(F32), axis=0)
        down = jnp.concatenate([full[:RANK], full[RANK:two]], axis=1)
        cross = full[two:]
        cross = sr2 * jnp.concatenate([cross, pltpu.roll(cross, RANK, 1)], axis=0)[:, :RANK]
        i_t = jnp.concatenate(
            [down + mu * d_t[:RANK], i_up + exact(cross, c_t, TN)], axis=0
        )
        note = jnp.zeros((8, two), F32)
        for at, value in enumerate((total(d_t * i_t), total(r_t * i_t), total(i_t * i_t), r_r_part)):
            note = jnp.where(sub8 == at, value, note)

        note = jnp.concatenate([part.astype(F32)[:4] for part in split(note)], axis=0).astype(BF16)
        terms = jnp.concatenate(
            [apply(i_t[:RANK], x_a, x_b, True), jnp.broadcast_to(note[None], (n_plane, 8, two))], axis=1
        )
        t3 = sum_start(terms, po, rb)
        cross_tu = exact(cross, g, TN)
        i_n = i_n + cross
        i_tu = i_tu + cross_tu
        if turn == 1:
            third_up = third_up + low_p * late_rows(cross, cross_tu)
            i_lt = near(low_p, diag(i_tu))
            i_sv = exact(s_l, i_t[RANK:], TN)
        s = sum_end(rb, t3)
        i_l = s[:HALF] * sd
        sums = s[HALF : HALF + 4] + s[HALF + 4 :]
        di, ri, ii, r_r = [sums[at : at + 1, :1] for at in range(4)]
        alpha = r_r / di
        rr = r_r - 2.0 * alpha * ri + alpha * alpha * ii
        beta = rr / r_r
        steps.append((alpha, beta))
        r_l = r_l - alpha * i_l
        d_l = r_l + beta * d_l
        if turn == 0:
            am3[...] = d_l.astype(BF16)
            ab3[me] = am3[...]
            s_a = fresh()
            plane_send(lambda j: am3, ab3, s_a)
            r_tu = r_tu - alpha * i_tu
            d_tu = r_tu + beta * d_tu
            inner = with_low(d_tu)
            hand_over(1, i_t)
            arrived(rz, n_plane - 1, s_pz)
            oz_p = jnp.sum(rz[...].astype(F32), axis=0)
            second_by = by_domain(i_l * eu_p + up_rows(i_m, i_n, i_tu), hot_r)
            first_by = by_domain(first_l * eu_p + up_rows(first_m, first_n, first_tu), hot_l)
        else:
            d_lt = r_lt - alpha * i_lt + beta * d_lt
            d_sv = r_sv - alpha * i_sv + beta * d_sv
            third_by = by_domain(i_l * eu_p + third_up, hot_l)
        r_t, r_m, r_n = r_t - alpha * i_t, r_m - alpha * i_m, r_n - alpha * i_n
        d_t, d_m, d_n = r_t + beta * d_t, r_m + beta * d_m, r_n + beta * d_n
        if turn == 0:
            arrived(ab3, n_plane - 1, s_a)
            gathered = ab3[...].reshape(tall, two)

    d_lb = d_l.astype(BF16)
    quad = sr2 * own_wl * d_lb.astype(F32) * (mm2(d_lb, g_diag) + 2.0 * d_lt)
    slices = mu * total(d_t * d_t) + sr2 * total(d_sv * d_t[RANK:])
    curve = total(quad) + slices * (1.0 / n_line)
    s_f, s_l2 = fresh(), fresh()
    fm[...] = jnp.where(
        sub8 == 0, first_by + second_by, jnp.where(sub8 == 1, third_by, jnp.where(sub8 == 2, curve, 0.0))
    )[:4]
    fb[me] = fm[...]
    plane_send(lambda j: fm, fb, s_f)
    hand_over(2, i_t)
    arrived(fb, n_plane - 1, s_f)
    fq[...] = jnp.sum(fb[...], axis=0)
    fz[z] = fq[...]
    line_send(lambda k: fq, fz, s_l2)
    (a0, b0), (a1, b1) = steps
    for k in range(3):
        @pl.when(paired)
        def _(k=k):
            remote(pair_out.at[k], pair_in.at[k], pair_sems[k], partner).wait()

    @pl.when(alone)
    def _():
        given = ca.at[core, pl.ds(0, n_hi - 1), here_x]
        pltpu.make_async_copy(given, given, send.at[s_c]).wait()

    for whole, s_p in halves:
        pltpu.make_async_copy(whole, whole, send.at[s_p]).wait()
    for buf, n, s in sent[:-1]:
        wait_for(buf, n, send.at[s])
    arrived(fz, n_line - 1, s_l2)
    last = jnp.sum(fz[...], axis=0)
    a2 = rr / last[2:3, :1]
    w0 = a0 + a1 * (1.0 + b0) + a2 * (1.0 + b1 * (1.0 + b0))
    w1 = -a0 * (a1 + a2 * (1.0 + b1))
    w2 = -a1 * a2
    hyp = w0 * last[:1] + w1 * pltpu.roll(last, RANK, 1)[:1] + w2 * last[1:2]
    hyp_out[...] = -kappa * hyp[:, :RANK]
    sol_out[...] = w0 * pair_in[0] + w1 * pair_in[1] + w2 * pair_in[2]
    buf, n, s = sent[-1]
    wait_for(buf, n, send.at[s])


def solution(mesh, xc=8, z_lo=2):
    n_dp, n_fsdp = mesh.shape["dp"], mesh.shape["fsdp"]
    n_plane = (n_dp // z_lo) * xc
    n_line = (n_fsdp // xc) * z_lo
    n_chip = n_plane // 2
    n_sem = 48
    geo = (n_plane, n_line, xc, z_lo, n_sem)
    chunk = RANK // n_line
    two = 2 * RANK
    vm = pltpu.VMEM

    def sums(rows):
        return [vm((n_plane, rows, two), BF16)] * 2

    def gather(rows):
        return [vm((rows, two), BF16), vm((n_plane, rows, two), BF16)]

    def line(*shape):
        return [vm((n_line, *shape), F32), vm((n_line, *shape), F32), vm(shape, F32), vm((n_line, *shape), F32)]

    terms = [vm((two + HALF, two), BF16), vm((n_line, two + HALF, two), BF16)]
    late = vm((n_plane, HALF, two), BF16)
    scratch = [
        vm((n_plane, TOK, WIDE), BF16), vm((n_plane, TOK, WIDE), BF16), vm((2, n_chip // (xc // 2), xc // 2, WIDE, two), BF16),
        vm((n_plane, 8, two), F32), vm((TOK, n_plane * WIDE), BF16), vm((TOK, n_plane * WIDE), BF16),
        *gather(TOK), *line(chunk, WIDE), *line(2, chunk, WIDE),
        *sums(HALF), *gather(HALF), *terms, late, late,
        *sums(HALF + 8), *gather(HALF), *terms,
        *sums(HALF + 8),
        vm((4, two), F32), vm((n_plane, 4, two), F32), vm((4, two), F32), vm((n_line, 4, two), F32),
        vm((3, WIDE, two), F32), vm((3, WIDE, two), F32),
        pltpu.SemaphoreType.DMA((n_sem,)), pltpu.SemaphoreType.DMA((n_sem,)), pltpu.SemaphoreType.DMA((5,)),
    ]
    anywhere = pl.BlockSpec(memory_space=pl.ANY)
    inside = pl.BlockSpec(memory_space=pltpu.VMEM)

    def on_device(x, o, cat, coef, learn, held):
        sol, hyp = pl.pallas_call(
            functools.partial(kernel, geo),
            out_shape=(
                jax.ShapeDtypeStruct((WIDE, two), F32),
                jax.ShapeDtypeStruct((1, RANK), F32),
            ),
            in_specs=[anywhere, anywhere, inside, anywhere, inside, inside],
            out_specs=(inside, inside),
            scratch_shapes=scratch,
            compiler_params=pltpu.CompilerParams(
                collective_id=0, has_side_effects=True, vmem_limit_bytes=56 * 1024 * 1024
            ),
        )(x, o, cat.reshape(1, TOK), coef, learn.reshape(1, DOMAINS), held.reshape(1, DOMAINS))
        return sol, hyp.reshape(DOMAINS)

    placed = (P(("dp", "fsdp"), None), P(("dp", "fsdp"), None), P(("dp", "fsdp")), P("fsdp", None), P(), P())
    return jax.shard_map(
        on_device, mesh=mesh, in_specs=placed, out_specs=(P("fsdp", None), P()), check_vma=False
    )
```

```python
import functools

import jax
import jax.numpy as jnp
from jax import lax
from jax.experimental import pallas as pl
from jax.experimental.pallas import tpu as pltpu
from jax.sharding import PartitionSpec as P

MESH = pl.DeviceIdType.MESH
HIGH = lax.Precision.HIGHEST
RANK = 64
DOMAINS = 64
TOK = 64
HALF = 32
WIDE = 256
F32 = jnp.float32
BF16 = jnp.bfloat16
NN = (((1,), (0,)), ((), ()))
NT = (((1,), (1,)), ((), ()))
TN = (((0,), (0,)), ((), ()))


def mm(a, b, dims=NN):
    return lax.dot_general(a, b, dims, preferred_element_type=F32)


def exact(a, b, dims=NN):
    return lax.dot_general(a, b, dims, precision=HIGH, preferred_element_type=F32)


def split(v):
    hi = v.astype(BF16)
    return hi, (v - hi.astype(F32)).astype(BF16)


def mm2(a, v):
    both = mm(a, jnp.concatenate(split(v), axis=1))
    half = v.shape[1]
    return both[:, :half] + both[:, half:]


def total(v):
    return jnp.sum(v, axis=(0, 1), keepdims=True)


def kernel(geo, x, o, cat, coef, tl, th, sol_out, hyp_out, *scratch):
    n_plane, n_line, xc, z_lo, n_sem = geo
    (
        xs, os_, ca, wg, xr, orow, am1, ab1, zp1, zb1, zm1, zg1, zp1b, zb1b, zm1b, zg1b,
        zp1z, zb1z, zm1z, zg1z,
        po2, rb2, am2, ab2, zp2, zb2, pz, rz,
        po3, rb3, am3, ab3, zp3, zb3,
        po4, rb4, fm, fb, fq, fz, pair_out, pair_in, send, recv, local,
    ) = scratch
    n_chip = n_plane // 2
    nx = xc // 2
    width = n_plane * WIDE
    rows = n_plane * n_line * TOK
    sd = width ** (-0.5)
    sr = RANK ** (-0.5)
    sr2 = 1.0 / RANK
    kappa = DOMAINS / (rows * width)
    mu = 0.1 * DOMAINS / (width * RANK)
    tall = n_plane * HALF
    two = 2 * RANK
    chunk = RANK // n_line

    dp = lax.axis_index("dp")
    fs = lax.axis_index("fsdp")
    y = lax.div(dp, z_lo)
    low_z = lax.rem(dp, z_lo)
    z_hi = lax.div(fs, xc)
    col = lax.rem(fs, xc)
    core = lax.rem(col, 2)
    chip = y * nx + lax.div(col, 2)
    here_x = lax.div(col, 2)
    ny = n_chip // nx
    me = core * n_chip + chip
    z = z_hi * z_lo + low_z

    def at_chip(q, which):
        return (lax.div(q, nx) * z_lo + low_z, z_hi * xc + lax.rem(q, nx) * 2 + which)

    def in_plane(j):
        return at_chip(lax.rem(j, n_chip), lax.div(j, n_chip))

    def in_line(k):
        return (y * z_lo + lax.rem(k, z_lo), lax.div(k, z_lo) * xc + col)

    def shard(j):
        q = lax.rem(j, n_chip)
        return lax.div(q, nx) * xc + lax.rem(q, nx) * 2 + lax.div(j, n_chip)

    partner = (z_hi * z_lo + low_z, y * xc + col)
    paired = y != z_hi
    alone = jnp.logical_not(paired)

    used = [0]

    def fresh():
        used[0] += 1
        assert used[0] <= n_sem
        return used[0] - 1

    sent = []

    def columns(ref, j):
        return ref.at[:, pl.ds(pl.multiple_of(shard(j) * WIDE, WIDE), WIDE)]

    own_x = pltpu.make_async_copy(columns(x, me), xs.at[me], local.at[0])
    own_o = pltpu.make_async_copy(columns(o, me), os_.at[me], local.at[1])
    rows_x = pltpu.make_async_copy(x, xr, local.at[2])
    rows_o = pltpu.make_async_copy(o, orow, local.at[3])
    for copy in (rows_x, rows_o, own_x, own_o):
        copy.start()

    by_far = sorted(range(nx), key=lambda d: -min(d, nx - d))

    def over_plane(go, cores):
        def at_row(yy, steps):
            for d in steps:
                xx = lax.rem(here_x + d, nx)
                for e in range(cores):
                    which = lax.rem(core + e, 2)
                    go(which * n_chip + yy * nx + xx, (yy * z_lo + low_z, z_hi * xc + xx * 2 + which))

        def far(t, c):
            d = ny // 2 - t + (ny - 1) * lax.div(t, ny // 2)
            at_row(lax.rem(y + d, ny), by_far)
            return c

        lax.fori_loop(0, ny - 1, far, 0)
        at_row(y, [d for d in by_far if d])
        if cores == 2:
            go((1 - core) * n_chip + chip, at_chip(chip, 1 - core))

    barrier = pltpu.get_barrier_semaphore()

    def greet_line(i, c):
        pl.semaphore_signal(barrier, inc=1, device_id=in_line(lax.rem(z + i, n_line)), device_id_type=MESH)
        return c

    lax.fori_loop(1, n_line, greet_line, 0)
    over_plane(
        lambda j, device: pl.semaphore_signal(barrier, inc=1, device_id=device, device_id_type=MESH), 2
    )

    sub = lax.broadcasted_iota(jnp.int32, (RANK, RANK), 0)
    lan = lax.broadcasted_iota(jnp.int32, (RANK, RANK), 1)
    eye = (sub == lan).astype(F32)
    sub2 = lax.broadcasted_iota(jnp.int32, (RANK, two), 0)
    lan2 = lax.broadcasted_iota(jnp.int32, (RANK, two), 1)
    put_l = (lan2 == sub2).astype(F32)
    put_r = (lan2 == sub2 + RANK).astype(F32)
    left_half = lan2 < RANK
    left32 = left_half[:HALF]
    sub8 = lax.broadcasted_iota(jnp.int32, (8, two), 0)
    hot_t = (cat[...] == sub).astype(F32)
    row_w = exact(exact(tl[...], hot_t), put_l) + exact(exact(th[...], hot_t), put_r)
    wg[me] = jnp.broadcast_to(row_w * kappa, (8, two))

    pl.semaphore_wait(barrier, n_plane + n_line - 2)

    def remote(src, dst, s, device):
        return pltpu.make_async_remote_copy(
            src_ref=src, dst_ref=dst, send_sem=send.at[s], recv_sem=recv.at[s], device_id=device, device_id_type=MESH
        )

    def plane_part(src_of, dst, s, first, stop):
        def body(i, c):
            j = lax.rem(me + i, n_plane)
            remote(src_of(j), dst.at[me], s, in_plane(j)).start()
            return c

        lax.fori_loop(first, stop, body, 0)

    def plane_send(src_of, dst, s):
        over_plane(lambda j, device: remote(src_of(j), dst.at[me], s, device).start(), 2)
        sent.append((dst, n_plane - 1, s))

    def chip_send(src_of, dst, slot, s):
        over_plane(lambda j, device: remote(src_of(j), dst.at[slot], s, device).start(), 1)
        sent.append((dst, n_chip - 1, s))

    def line_send(src_of, dst, s):
        def body(i, c):
            k = lax.rem(z + i, n_line)
            remote(src_of(k), dst.at[z], s, in_line(k)).start()
            return c

        lax.fori_loop(1, n_line, body, 0)
        sent.append((dst, n_line - 1, s))

    def sib_send(src, dst, s):
        remote(src, dst, s, at_chip(chip, 1 - core)).start()
        sent.append((dst, n_chip, s))

    def wait_for(buf, n, sem):
        part = buf.at[pl.ds(0, n)]
        pltpu.make_async_copy(part, part, sem).wait()

    def arrived(buf, n, s):
        wait_for(buf, n, recv.at[s])

    def sum_start(terms, po, rb):
        t = fresh()
        po[...] = terms
        rb[me] = po[me]
        plane_send(lambda j: po.at[j], rb, t)
        return t

    def sum_end(rb, t):
        arrived(rb, n_plane - 1, t)
        return jnp.sum(rb[...].astype(F32), axis=0)

    def line_start(zp, zb):
        s = fresh()
        zb[z] = zp[z]
        line_send(lambda k: zp.at[k], zb, s)
        return s

    def line_mid(zb, zm, zg, s):
        t = fresh()
        arrived(zb, n_line - 1, s)
        zm[...] = jnp.sum(zb[...], axis=0)
        zg[z] = zm[...]
        line_send(lambda k: zm, zg, t)
        return t

    s_c, s_w, s_x, s_o = fresh(), fresh(), fresh(), fresh()

    own_slot = ca.at[core, y, here_x]
    n_hi = n_line // z_lo
    own_c = pltpu.make_async_copy(coef, own_slot, local.at[4])

    @pl.when(alone)
    def _():
        def body(i, c):
            remote(coef, own_slot, s_c, (dp, lax.rem(z_hi + i, n_hi) * xc + col)).start()
            return c

        lax.fori_loop(1, n_hi, body, 0)
        own_c.start()

    plane_send(lambda j: wg.at[me], wg, s_w)
    plane_part(lambda j: columns(x, j), xs, s_x, 1, 3 * n_plane // 4)

    @pl.when(paired)
    def _():
        pltpu.make_async_copy(own_slot, own_slot, recv.at[s_c]).wait()

    @pl.when(alone)
    def _():
        own_c.wait()

    lower = pl.ds(0, WIDE // 2)
    upper = pl.ds(WIDE // 2, WIDE // 2)

    def along_y(ref, s):
        def body(i, c):
            remote(ref, ref, s, at_chip(lax.rem(y + i, ny) * nx + here_x, core)).start()
            return c

        lax.fori_loop(1, ny, body, 0)

    def along_x(ref, s):
        def body(i, c):
            remote(ref, ref, s, at_chip(y * nx + lax.rem(here_x + i, nx), core)).start()
            return c

        lax.fori_loop(1, nx, body, 0)

    def both_ends(part, s, n):
        for sem in (recv, send):
            for_all = part.at[pl.ds(0, n)]
            pltpu.make_async_copy(for_all, for_all, sem.at[s]).wait()

    g_a, g_b, g_a2, g_b2 = fresh(), fresh(), fresh(), fresh()
    along_y(ca.at[core, y, here_x, lower], g_a)
    along_x(ca.at[core, y, here_x, upper], g_b)

    n8 = HALF // 8
    deep = 8 * lax.broadcasted_iota(jnp.int32, (n8, 8, two), 0) + lax.broadcasted_iota(jnp.int32, (n8, 8, two), 1)
    wide = lax.broadcasted_iota(jnp.int32, (n8, 8, two), 2)
    big_l = lax.broadcasted_iota(jnp.int32, (two, two), 1) < RANK
    ones_l = big_l.astype(BF16)
    ones_r = jnp.logical_not(big_l).astype(BF16)

    def packed(v, base):
        n = v.shape[0]
        out = None
        for shift, ones in ((0, ones_l), (HALF, ones_r)):
            mask = (wide == deep + (base + shift)).astype(F32)
            picked = (v[:, None] * mask[None]).reshape(n * HALF, two)
            for part in split(picked):
                t = mm(part, ones)
                out = t if out is None else out + t
        return out

    own_wl = packed(wg[pl.ds(me, 1)], 0)

    arrived(wg, n_plane - 1, s_w)
    wlp = packed(wg[...], 0)
    whp = packed(wg[...], RANK)
    rows_x.wait()
    rows_o.wait()

    column_a = ca.at[core, :, here_x, lower]
    row_b = ca.at[core, y, :, upper]
    both_ends(column_a, g_a, ny - 1)
    along_x(column_a, g_a2)
    if nx > 1:
        both_ends(row_b, g_b, nx - 1)
    along_y(row_b, g_b2)
    plane_part(lambda j: columns(x, j), xs, s_x, 3 * n_plane // 4, n_plane)
    sent.append((xs, n_plane - 1, s_x))
    halves = []
    for span, s_p, n, kind in ((lower, g_a2, nx - 1, 0), (upper, g_b2, ny - 1, 1)):
        if n:
            rest = ca.at[core, :, pl.ds(0, n), span] if kind == 0 else ca.at[core, pl.ds(0, n), :, span]
            for sem in (recv, send):
                pltpu.make_async_copy(rest, rest, sem.at[s_p]).wait()
        whole = ca.at[core, :, :, span]
        s_p = fresh()
        remote(whole, whole, s_p, at_chip(chip, 1 - core)).start()
        halves.append((whole, s_p))
    both = None
    for piece, (whole, s_p) in enumerate(halves):
        pltpu.make_async_copy(whole, whole, recv.at[s_p]).wait()
        base = piece * (WIDE // 2)
        for j in range(n_plane):
            q = j % n_chip
            at = ((q // nx) * xc + (q % nx) * 2 + j // n_chip) * WIDE + base
            own_rows = jnp.concatenate(
                [xr[:, at : at + WIDE // 2], orow[:, at : at + WIDE // 2]], axis=0
            )
            t = mm(own_rows, ca[j // n_chip, q // nx, q % nx, base : base + WIDE // 2])
            both = t if both is None else both + t

    def spread(v, at):
        return jnp.broadcast_to(v[:, at : at + 1], (tall, two))

    f_own = jnp.where(left_half, (both[:TOK] * sd).astype(BF16).astype(F32), both[TOK:])
    am1[...] = f_own.astype(BF16)
    ab1[me] = am1[...]
    s_g, s_h2 = fresh(), fresh()
    chip_send(lambda q: am1, ab1, me, s_g)
    g_wide = None
    for j in range(n_plane):
        c = ca[j // n_chip, (j % n_chip) // nx, j % nx]
        t = mm(c, c, TN)
        g_wide = t if g_wide is None else g_wide + t
    g_wide = g_wide[RANK:]
    c_t = exact(put_r, ca[core, y, here_x].astype(F32), NT)
    nought = jnp.zeros_like(put_l)
    e_top = jnp.concatenate([put_l, nought], axis=0)
    e_top_r = jnp.concatenate([put_r, nought], axis=0)
    e_bot = jnp.concatenate([nought, put_l], axis=0)
    e_bot_r = jnp.concatenate([nought, put_r], axis=0)
    low_p = exact(f_own[:HALF], e_top) + exact(f_own[HALF:], e_top_r)
    ou_p = exact(f_own[:HALF], e_bot) + exact(f_own[HALF:], e_bot_r)
    hot = exact(hot_t, eye, TN)
    hot_l = exact(hot, put_l).astype(BF16)
    hot_r = exact(hot, put_r).astype(BF16)
    arrived(ab1, n_chip - 1, s_g)
    mine_half = ab1.at[pl.ds(core * n_chip, n_chip)]
    sib_send(mine_half, mine_half, s_h2)
    arrived(ab1, n_chip, s_h2)
    plane_part(lambda j: columns(o, j), os_, s_o, 1, n_plane)
    sent.append((os_, n_plane - 1, s_o))

    g_right = jnp.where(left_half, 0.0, g_wide)
    g_left = pltpu.roll(g_right, RANK, 1)
    g = g_left[:, :RANK]
    g_diag = jnp.concatenate([g_left, g_right], axis=0)
    f_a = ab1[:, :HALF].reshape(tall, two)
    f_b = ab1[:, HALF:].reshape(tall, two)
    k_l = jnp.concatenate([g_left * sr2, put_l * sr], axis=0)
    k_r = jnp.concatenate([g_right * sr2, put_r * sr], axis=0)
    f_ab = jnp.concatenate([f_a, f_b], axis=1)
    p0 = (whp * mm2(f_ab, jnp.concatenate([k_l, k_r], axis=0))).astype(BF16)
    def fold(v, a, b):
        return mm(v, a, TN)[:RANK] + mm(v, b, TN)[RANK:]

    own_x.wait()
    arrived(xs, n_plane - 1, s_x)
    x_a = xs[:, :HALF].reshape(tall, WIDE)
    x_b = xs[:, HALF:].reshape(tall, WIDE)
    zp1[...] = (fold(p0, x_a, x_b) * sd).reshape(n_line, chunk, WIDE)
    s_r = line_start(zp1, zb1)
    wfh_a = (f_a.astype(F32) * spread(whp, 0)).astype(BF16)
    wfh_b = (f_b.astype(F32) * spread(whp, RANK)).astype(BF16)
    wfl_a = (f_a.astype(F32) * spread(wlp, 0)).astype(BF16)
    wfl_b = (f_b.astype(F32) * spread(wlp, RANK)).astype(BF16)
    q_h = mm(f_a, wfh_a, TN)[:RANK] + mm(f_b, wfh_b, TN)[:RANK]
    q_l = mm(f_a, wfl_a, TN)[:RANK] + mm(f_b, wfl_b, TN)[:RANK]
    zp1b[...] = jnp.concatenate([q_h, q_l], axis=1).reshape(n_line, chunk, WIDE)
    s_q = line_start(zp1b, zb1b)
    s_r = line_mid(zb1, zm1, zg1, s_r)
    s_q = line_mid(zb1b, zm1b, zg1b, s_q)
    eu_p = ou_p + sr * exact(low_p, g_diag)
    arrived(zg1, n_line - 1, s_r)

    d_t = zg1[...].reshape(RANK, WIDE)
    nil = jnp.zeros((RANK, WIDE), BF16)

    def apply(v, a, b, both):
        parts = split(v) if both else (v.astype(BF16),)
        w_a = jnp.concatenate([w for part in parts for w in (part, nil)], axis=0)
        w_b = jnp.concatenate([w for part in parts for w in (nil, part)], axis=0)
        out = mm(a, w_a, NT) + mm(b, w_b, NT)
        if both:
            out = out[:, :two] + out[:, two:]
        return out.astype(BF16).reshape(n_plane, HALF, two)

    t2 = sum_start(apply(d_t, x_a, x_b, True), po2, rb2)
    own_o.wait()
    arrived(os_, n_plane - 1, s_o)
    o_a = os_[:, :HALF].reshape(tall, WIDE)
    o_b = os_[:, HALF:].reshape(tall, WIDE)
    zp1z[...] = (mm(wfh_a, o_a, TN)[:RANK] + mm(wfh_b, o_b, TN)[:RANK]).reshape(n_line, chunk, WIDE)
    s_zz = line_start(zp1z, zb1z)

    pair_sems = [fresh(), fresh(), fresh()]

    def hand_over(k, both_halves):
        pair_out[k] = both_halves.T

        @pl.when(paired)
        def _():
            remote(pair_out.at[k], pair_in.at[k], pair_sems[k], partner).start()

        @pl.when(alone)
        def _():
            pair_in[k] = pair_out[k]

    d_l = sum_end(rb2, t2) * sd
    am2[...] = d_l.astype(BF16)
    ab2[me] = am2[...]
    s_a = fresh()
    plane_send(lambda j: am2, ab2, s_a)
    s_zz = line_mid(zb1z, zm1z, zg1z, s_zz)
    arrived(zg1b, n_line - 1, s_q)
    stats = zg1b[...].reshape(RANK, WIDE)
    s_h = stats[:, :RANK]
    zu = pltpu.roll(stats[:, :two], RANK, 1)[:, :RANK]
    s_l = stats[:, two : two + RANK]
    d_m = eye * sr
    d_n = s_h * sr2
    d_tu = exact(d_m, zu, TN) + exact(d_n, g, TN)

    def up_slice(m, n):
        return exact(m, z_t, TN) + exact(n, c_t, TN)


    put_l16, put_r16 = put_l.astype(BF16), put_r.astype(BF16)

    def place(m, put, dims=NN):
        hi, lo = split(m)
        return mm(hi, put, dims) + mm(lo, put, dims)

    def near(a, b):
        a_hi, a_lo = split(a)
        b_hi, b_lo = split(b)
        return mm(a_hi, b_hi) + (mm(a_hi, b_lo) + mm(a_lo, b_hi))

    def with_low(tu):
        tu_l = jnp.concatenate([place(tu, put_l16), nought], axis=0)
        tu_r = jnp.concatenate([place(tu, put_r16), nought], axis=0)
        return mm2(f_ab, jnp.concatenate([tu_l, tu_r], axis=0))

    def image_part(l_p, inner, zp):
        y_p = (wlp * sr2 * (inner + mm2(l_p, g_diag))).astype(BF16)
        down = fold(y_p, x_a, x_b) * sd
        cross = fold(l_p, wfl_a, wfl_b)
        cross = jnp.where(left32, cross[:HALF], pltpu.roll(cross[HALF:], RANK, 1))
        zp[...] = jnp.concatenate([down[:, :two], down[:, two:], cross], axis=0).astype(BF16)

    inner = with_low(d_tu)
    arrived(ab2, n_plane - 1, s_a)
    gathered = ab2[...].reshape(tall, two)

    def diag(m):
        return jnp.concatenate([place(m, put_l16), place(m, put_r16)], axis=0)

    def diag_t(m):
        return jnp.concatenate([place(m, put_l16, TN), place(m, put_r16, TN)], axis=0)

    def up_rows(m, n, tu):
        return low_p * (near(oz_p, diag(m)) + late_rows(n, tu))

    def late_rows(n, tu):
        return near(ou_p, diag(n)) + sr * near(low_p, diag_t(tu))

    def by_domain(q, to):
        q_left = jnp.where(left32, q, 0.0)
        q_right = jnp.where(left32, 0.0, q)
        by = place(q_left, to[:HALF], TN) + place(q_right, to[HALF:], TN)
        return sr * jnp.sum(by, axis=0, keepdims=True)

    r_t, r_m, r_n, r_l, r_tu = d_t, d_m, d_n, d_l, d_tu
    first_l, first_m, first_n, first_tu = d_l, d_m, d_n, d_tu
    rounds = (
        (zp2, zb2, po3, rb3), (zp3, zb3, po4, rb4),
    )
    steps = []
    for turn, (zp, zb, po, rb) in enumerate(rounds):
        image_part(gathered, inner, zp)
        s_z = fresh()
        zb[z] = zp[...]
        line_send(lambda k: zp, zb, s_z)
        i_m = sr2 * exact(d_m, s_l) + mu * d_m
        i_n = sr2 * exact(d_n, s_l) + mu * d_n
        i_tu = exact(i_m, zu, TN) + exact(i_n, g, TN)
        if turn == 0:
            arrived(zg1z, n_line - 1, s_zz)
            z_t = zg1z[...].reshape(RANK, WIDE)
            d_t = jnp.concatenate([d_t, up_slice(d_m, d_n)], axis=0)
            r_t = d_t
        i_up = up_slice(i_m, i_n)
        if turn == 0:
            pz[...] = apply(z_t, o_a, o_b, False)
            s_pz = fresh()
            rz[me] = pz[me]
            plane_send(lambda j: pz.at[j], rz, s_pz)
        else:
            r_lt = near(low_p, diag(r_tu))
            d_lt = near(low_p, diag(d_tu))
        r_r_part = total(r_t * r_t)
        if turn == 0:
            hand_over(0, d_t)
        else:
            third_up = up_rows(i_m, i_n, i_tu)
            d_sv = exact(s_l, d_t[RANK:], TN)
            r_sv = exact(s_l, r_t[RANK:], TN)
        arrived(zb, n_line - 1, s_z)
        full = jnp.sum(zb[...].astype(F32), axis=0)
        down = jnp.concatenate([full[:RANK], full[RANK:two]], axis=1)
        cross = full[two:]
        cross = sr2 * jnp.concatenate([cross, pltpu.roll(cross, RANK, 1)], axis=0)[:, :RANK]
        i_t = jnp.concatenate(
            [down + mu * d_t[:RANK], i_up + exact(cross, c_t, TN)], axis=0
        )
        note = jnp.zeros((8, two), F32)
        for at, value in enumerate((total(d_t * i_t), total(r_t * i_t), total(i_t * i_t), r_r_part)):
            note = jnp.where(sub8 == at, value, note)

        note = jnp.concatenate([part.astype(F32)[:4] for part in split(note)], axis=0).astype(BF16)
        terms = jnp.concatenate(
            [apply(i_t[:RANK], x_a, x_b, True), jnp.broadcast_to(note[None], (n_plane, 8, two))], axis=1
        )
        t3 = sum_start(terms, po, rb)
        cross_tu = exact(cross, g, TN)
        i_n = i_n + cross
        i_tu = i_tu + cross_tu
        if turn == 1:
            third_up = third_up + low_p * late_rows(cross, cross_tu)
            i_lt = near(low_p, diag(i_tu))
            i_sv = exact(s_l, i_t[RANK:], TN)
        s = sum_end(rb, t3)
        i_l = s[:HALF] * sd
        sums = s[HALF : HALF + 4] + s[HALF + 4 :]
        di, ri, ii, r_r = [sums[at : at + 1, :1] for at in range(4)]
        alpha = r_r / di
        rr = r_r - 2.0 * alpha * ri + alpha * alpha * ii
        beta = rr / r_r
        steps.append((alpha, beta))
        r_l = r_l - alpha * i_l
        d_l = r_l + beta * d_l
        if turn == 0:
            am3[...] = d_l.astype(BF16)
            ab3[me] = am3[...]
            s_a = fresh()
            plane_send(lambda j: am3, ab3, s_a)
            r_tu = r_tu - alpha * i_tu
            d_tu = r_tu + beta * d_tu
            inner = with_low(d_tu)
            hand_over(1, i_t)
            arrived(rz, n_plane - 1, s_pz)
            oz_p = jnp.sum(rz[...].astype(F32), axis=0)
            second_by = by_domain(i_l * eu_p + up_rows(i_m, i_n, i_tu), hot_r)
            first_by = by_domain(first_l * eu_p + up_rows(first_m, first_n, first_tu), hot_l)
        else:
            d_lt = r_lt - alpha * i_lt + beta * d_lt
            d_sv = r_sv - alpha * i_sv + beta * d_sv
            third_by = by_domain(i_l * eu_p + third_up, hot_l)
        r_t, r_m, r_n = r_t - alpha * i_t, r_m - alpha * i_m, r_n - alpha * i_n
        d_t, d_m, d_n = r_t + beta * d_t, r_m + beta * d_m, r_n + beta * d_n
        if turn == 0:
            arrived(ab3, n_plane - 1, s_a)
            gathered = ab3[...].reshape(tall, two)

    d_lb = d_l.astype(BF16)
    quad = sr2 * own_wl * d_lb.astype(F32) * (mm2(d_lb, g_diag) + 2.0 * d_lt)
    slices = mu * total(d_t * d_t) + sr2 * total(d_sv * d_t[RANK:])
    curve = total(quad) + slices * (1.0 / n_line)
    s_f, s_l2 = fresh(), fresh()
    fm[...] = jnp.where(
        sub8 == 0, first_by + second_by, jnp.where(sub8 == 1, third_by, jnp.where(sub8 == 2, curve, 0.0))
    )[:4]
    fb[me] = fm[...]
    plane_send(lambda j: fm, fb, s_f)
    hand_over(2, i_t)
    arrived(fb, n_plane - 1, s_f)
    fq[...] = jnp.sum(fb[...], axis=0)
    fz[z] = fq[...]
    line_send(lambda k: fq, fz, s_l2)
    (a0, b0), (a1, b1) = steps
    for k in range(3):
        @pl.when(paired)
        def _(k=k):
            remote(pair_out.at[k], pair_in.at[k], pair_sems[k], partner).wait()

    @pl.when(alone)
    def _():
        given = ca.at[core, pl.ds(0, n_hi - 1), here_x]
        pltpu.make_async_copy(given, given, send.at[s_c]).wait()

    for whole, s_p in halves:
        pltpu.make_async_copy(whole, whole, send.at[s_p]).wait()
    for buf, n, s in sent[:-1]:
        wait_for(buf, n, send.at[s])
    arrived(fz, n_line - 1, s_l2)
    last = jnp.sum(fz[...], axis=0)
    a2 = rr / last[2:3, :1]
    w0 = a0 + a1 * (1.0 + b0) + a2 * (1.0 + b1 * (1.0 + b0))
    w1 = -a0 * (a1 + a2 * (1.0 + b1))
    w2 = -a1 * a2
    hyp = w0 * last[:1] + w1 * pltpu.roll(last, RANK, 1)[:1] + w2 * last[1:2]
    hyp_out[...] = -kappa * hyp[:, :RANK]
    sol_out[...] = w0 * pair_in[0] + w1 * pair_in[1] + w2 * pair_in[2]
    buf, n, s = sent[-1]
    wait_for(buf, n, send.at[s])


def solution(mesh, xc=8, z_lo=2):
    n_dp, n_fsdp = mesh.shape["dp"], mesh.shape["fsdp"]
    n_plane = (n_dp // z_lo) * xc
    n_line = (n_fsdp // xc) * z_lo
    n_chip = n_plane // 2
    n_sem = 48
    geo = (n_plane, n_line, xc, z_lo, n_sem)
    chunk = RANK // n_line
    two = 2 * RANK
    vm = pltpu.VMEM

    def sums(rows):
        return [vm((n_plane, rows, two), BF16)] * 2

    def gather(rows):
        return [vm((rows, two), BF16), vm((n_plane, rows, two), BF16)]

    def line(*shape):
        return [vm((n_line, *shape), F32), vm((n_line, *shape), F32), vm(shape, F32), vm((n_line, *shape), F32)]

    terms = [vm((two + HALF, two), BF16), vm((n_line, two + HALF, two), BF16)]
    late = vm((n_plane, HALF, two), BF16)
    scratch = [
        vm((n_plane, TOK, WIDE), BF16), vm((n_plane, TOK, WIDE), BF16), vm((2, n_chip // (xc // 2), xc // 2, WIDE, two), BF16),
        vm((n_plane, 8, two), F32), vm((TOK, n_plane * WIDE), BF16), vm((TOK, n_plane * WIDE), BF16),
        *gather(TOK), *line(chunk, WIDE), *line(chunk, WIDE), *line(chunk, WIDE),
        *sums(HALF), *gather(HALF), *terms, late, late,
        *sums(HALF + 8), *gather(HALF), *terms,
        *sums(HALF + 8),
        vm((4, two), F32), vm((n_plane, 4, two), F32), vm((4, two), F32), vm((n_line, 4, two), F32),
        vm((3, WIDE, two), F32), vm((3, WIDE, two), F32),
        pltpu.SemaphoreType.DMA((n_sem,)), pltpu.SemaphoreType.DMA((n_sem,)), pltpu.SemaphoreType.DMA((5,)),
    ]
    anywhere = pl.BlockSpec(memory_space=pl.ANY)
    inside = pl.BlockSpec(memory_space=pltpu.VMEM)

    def on_device(x, o, cat, coef, learn, held):
        sol, hyp = pl.pallas_call(
            functools.partial(kernel, geo),
            out_shape=(
                jax.ShapeDtypeStruct((WIDE, two), F32),
                jax.ShapeDtypeStruct((1, RANK), F32),
            ),
            in_specs=[anywhere, anywhere, inside, anywhere, inside, inside],
            out_specs=(inside, inside),
            scratch_shapes=scratch,
            compiler_params=pltpu.CompilerParams(
                collective_id=0, has_side_effects=True, vmem_limit_bytes=56 * 1024 * 1024
            ),
        )(x, o, cat.reshape(1, TOK), coef, learn.reshape(1, DOMAINS), held.reshape(1, DOMAINS))
        return sol, hyp.reshape(DOMAINS)

    placed = (P(("dp", "fsdp"), None), P(("dp", "fsdp"), None), P(("dp", "fsdp")), P("fsdp", None), P(), P())
    return jax.shard_map(
        on_device, mesh=mesh, in_specs=placed, out_specs=(P("fsdp", None), P()), check_vma=False
    )
```

```python
import functools

import jax
import jax.numpy as jnp
from jax import lax
from jax.experimental import pallas as pl
from jax.experimental.pallas import tpu as pltpu
from jax.sharding import PartitionSpec as P

MESH = pl.DeviceIdType.MESH
HIGH = lax.Precision.HIGHEST
RANK = 64
DOMAINS = 64
TOK = 64
HALF = 32
WIDE = 256
F32 = jnp.float32
BF16 = jnp.bfloat16
NN = (((1,), (0,)), ((), ()))
NT = (((1,), (1,)), ((), ()))
TN = (((0,), (0,)), ((), ()))


def mm(a, b, dims=NN):
    return lax.dot_general(a, b, dims, preferred_element_type=F32)


def exact(a, b, dims=NN):
    return lax.dot_general(a, b, dims, precision=HIGH, preferred_element_type=F32)


def split(v):
    hi = v.astype(BF16)
    return hi, (v - hi.astype(F32)).astype(BF16)


def mm2(a, v):
    both = mm(a, jnp.concatenate(split(v), axis=1))
    half = v.shape[1]
    return both[:, :half] + both[:, half:]


def total(v):
    return jnp.sum(v, axis=(0, 1), keepdims=True)


def kernel(geo, x, o, cat, coef, tl, th, sol_out, hyp_out, *scratch):
    n_plane, n_line, xc, z_lo, n_sem = geo
    (
        xs, os_, ca, wg, xr, orow, am1, ab1, zp1, zb1, zm1, zg1, zp1b, zb1b, zm1b, zg1b,
        zp1z, zb1z, zm1z, zg1z,
        po2, rb2, am2, ab2, zp2, zb2, pz, rz,
        po3, rb3, am3, ab3, zp3, zb3,
        po4, rb4, fm, fb, fq, fz, pair_out, pair_in, send, recv, local,
    ) = scratch
    n_chip = n_plane // 2
    nx = xc // 2
    width = n_plane * WIDE
    rows = n_plane * n_line * TOK
    sd = width ** (-0.5)
    sr = RANK ** (-0.5)
    sr2 = 1.0 / RANK
    kappa = DOMAINS / (rows * width)
    mu = 0.1 * DOMAINS / (width * RANK)
    tall = n_plane * HALF
    two = 2 * RANK
    chunk = RANK // n_line

    dp = lax.axis_index("dp")
    fs = lax.axis_index("fsdp")
    y = lax.div(dp, z_lo)
    low_z = lax.rem(dp, z_lo)
    z_hi = lax.div(fs, xc)
    col = lax.rem(fs, xc)
    core = lax.rem(col, 2)
    chip = y * nx + lax.div(col, 2)
    here_x = lax.div(col, 2)
    ny = n_chip // nx
    me = core * n_chip + chip
    z = z_hi * z_lo + low_z

    def at_chip(q, which):
        return (lax.div(q, nx) * z_lo + low_z, z_hi * xc + lax.rem(q, nx) * 2 + which)

    def in_plane(j):
        return at_chip(lax.rem(j, n_chip), lax.div(j, n_chip))

    def in_line(k):
        return (y * z_lo + lax.rem(k, z_lo), lax.div(k, z_lo) * xc + col)

    def shard(j):
        q = lax.rem(j, n_chip)
        return lax.div(q, nx) * xc + lax.rem(q, nx) * 2 + lax.div(j, n_chip)

    partner = (z_hi * z_lo + low_z, y * xc + col)
    paired = y != z_hi
    alone = jnp.logical_not(paired)

    used = [0]

    def fresh():
        used[0] += 1
        assert used[0] <= n_sem
        return used[0] - 1

    sent = []

    def columns(ref, j):
        return ref.at[:, pl.ds(pl.multiple_of(shard(j) * WIDE, WIDE), WIDE)]

    own_x = pltpu.make_async_copy(columns(x, me), xs.at[me], local.at[0])
    own_o = pltpu.make_async_copy(columns(o, me), os_.at[me], local.at[1])
    rows_x = pltpu.make_async_copy(x, xr, local.at[2])
    rows_o = pltpu.make_async_copy(o, orow, local.at[3])
    for copy in (rows_x, rows_o, own_x, own_o):
        copy.start()

    by_far = sorted(range(nx), key=lambda d: -min(d, nx - d))

    def over_plane(go, cores):
        def at_row(yy, steps):
            for d in steps:
                xx = lax.rem(here_x + d, nx)
                for e in range(cores):
                    which = lax.rem(core + e, 2)
                    go(which * n_chip + yy * nx + xx, (yy * z_lo + low_z, z_hi * xc + xx * 2 + which))

        def far(t, c):
            d = ny // 2 - t + (ny - 1) * lax.div(t, ny // 2)
            at_row(lax.rem(y + d, ny), by_far)
            return c

        lax.fori_loop(0, ny - 1, far, 0)
        at_row(y, [d for d in by_far if d])
        if cores == 2:
            go((1 - core) * n_chip + chip, at_chip(chip, 1 - core))

    barrier = pltpu.get_barrier_semaphore()

    def greet_line(i, c):
        pl.semaphore_signal(barrier, inc=1, device_id=in_line(lax.rem(z + i, n_line)), device_id_type=MESH)
        return c

    lax.fori_loop(1, n_line, greet_line, 0)
    over_plane(
        lambda j, device: pl.semaphore_signal(barrier, inc=1, device_id=device, device_id_type=MESH), 2
    )

    sub = lax.broadcasted_iota(jnp.int32, (RANK, RANK), 0)
    lan = lax.broadcasted_iota(jnp.int32, (RANK, RANK), 1)
    eye = (sub == lan).astype(F32)
    sub2 = lax.broadcasted_iota(jnp.int32, (RANK, two), 0)
    lan2 = lax.broadcasted_iota(jnp.int32, (RANK, two), 1)
    put_l = (lan2 == sub2).astype(F32)
    put_r = (lan2 == sub2 + RANK).astype(F32)
    left_half = lan2 < RANK
    left32 = left_half[:HALF]
    sub8 = lax.broadcasted_iota(jnp.int32, (8, two), 0)
    hot_t = (cat[...] == sub).astype(F32)
    row_w = exact(exact(tl[...], hot_t), put_l) + exact(exact(th[...], hot_t), put_r)
    wg[me] = jnp.broadcast_to(row_w * kappa, (8, two))

    pl.semaphore_wait(barrier, n_plane + n_line - 2)

    def remote(src, dst, s, device):
        return pltpu.make_async_remote_copy(
            src_ref=src, dst_ref=dst, send_sem=send.at[s], recv_sem=recv.at[s], device_id=device, device_id_type=MESH
        )

    def plane_part(src_of, dst, s, first, stop):
        def body(i, c):
            j = lax.rem(me + i, n_plane)
            remote(src_of(j), dst.at[me], s, in_plane(j)).start()
            return c

        lax.fori_loop(first, stop, body, 0)

    def plane_send(src_of, dst, s):
        over_plane(lambda j, device: remote(src_of(j), dst.at[me], s, device).start(), 2)
        sent.append((dst, n_plane - 1, s))

    def chip_send(src_of, dst, slot, s):
        over_plane(lambda j, device: remote(src_of(j), dst.at[slot], s, device).start(), 1)
        sent.append((dst, n_chip - 1, s))

    def line_send(src_of, dst, s):
        def body(i, c):
            k = lax.rem(z + i, n_line)
            remote(src_of(k), dst.at[z], s, in_line(k)).start()
            return c

        lax.fori_loop(1, n_line, body, 0)
        sent.append((dst, n_line - 1, s))

    def sib_send(src, dst, s):
        remote(src, dst, s, at_chip(chip, 1 - core)).start()
        sent.append((dst, n_chip, s))

    def wait_for(buf, n, sem):
        part = buf.at[pl.ds(0, n)]
        pltpu.make_async_copy(part, part, sem).wait()

    def arrived(buf, n, s):
        wait_for(buf, n, recv.at[s])

    def sum_start(terms, po, rb):
        t = fresh()
        po[...] = terms
        rb[me] = po[me]
        plane_send(lambda j: po.at[j], rb, t)
        return t

    def sum_end(rb, t):
        arrived(rb, n_plane - 1, t)
        return jnp.sum(rb[...].astype(F32), axis=0)

    def line_start(zp, zb):
        s = fresh()
        zb[z] = zp[z]
        line_send(lambda k: zp.at[k], zb, s)
        return s

    def line_mid(zb, zm, zg, s):
        t = fresh()
        arrived(zb, n_line - 1, s)
        zm[...] = jnp.sum(zb[...], axis=0)
        zg[z] = zm[...]
        line_send(lambda k: zm, zg, t)
        return t

    s_c, s_w, s_x, s_o = fresh(), fresh(), fresh(), fresh()

    own_slot = ca.at[core, y, here_x]
    n_hi = n_line // z_lo
    own_c = pltpu.make_async_copy(coef, own_slot, local.at[4])

    @pl.when(alone)
    def _():
        def body(i, c):
            remote(coef, own_slot, s_c, (dp, lax.rem(z_hi + i, n_hi) * xc + col)).start()
            return c

        lax.fori_loop(1, n_hi, body, 0)
        own_c.start()

    plane_send(lambda j: wg.at[me], wg, s_w)
    plane_part(lambda j: columns(x, j), xs, s_x, 1, 3 * n_plane // 4)

    @pl.when(paired)
    def _():
        pltpu.make_async_copy(own_slot, own_slot, recv.at[s_c]).wait()

    @pl.when(alone)
    def _():
        own_c.wait()

    lower = pl.ds(0, WIDE // 2)
    upper = pl.ds(WIDE // 2, WIDE // 2)

    def along_y(ref, s):
        def body(i, c):
            remote(ref, ref, s, at_chip(lax.rem(y + i, ny) * nx + here_x, core)).start()
            return c

        lax.fori_loop(1, ny, body, 0)

    def along_x(ref, s):
        def body(i, c):
            remote(ref, ref, s, at_chip(y * nx + lax.rem(here_x + i, nx), core)).start()
            return c

        lax.fori_loop(1, nx, body, 0)

    def both_ends(part, s, n):
        for sem in (recv, send):
            for_all = part.at[pl.ds(0, n)]
            pltpu.make_async_copy(for_all, for_all, sem.at[s]).wait()

    g_a, g_b, g_a2, g_b2 = fresh(), fresh(), fresh(), fresh()
    along_y(ca.at[core, y, here_x, lower], g_a)
    along_x(ca.at[core, y, here_x, upper], g_b)

    n8 = HALF // 8
    deep = 8 * lax.broadcasted_iota(jnp.int32, (n8, 8, two), 0) + lax.broadcasted_iota(jnp.int32, (n8, 8, two), 1)
    wide = lax.broadcasted_iota(jnp.int32, (n8, 8, two), 2)
    big_l = lax.broadcasted_iota(jnp.int32, (two, two), 1) < RANK
    ones_l = big_l.astype(BF16)
    ones_r = jnp.logical_not(big_l).astype(BF16)

    def packed(v, base):
        n = v.shape[0]
        out = None
        for shift, ones in ((0, ones_l), (HALF, ones_r)):
            mask = (wide == deep + (base + shift)).astype(F32)
            picked = (v[:, None] * mask[None]).reshape(n * HALF, two)
            for part in split(picked):
                t = mm(part, ones)
                out = t if out is None else out + t
        return out

    own_wl = packed(wg[pl.ds(me, 1)], 0)

    arrived(wg, n_plane - 1, s_w)
    wlp = packed(wg[...], 0)
    whp = packed(wg[...], RANK)
    rows_x.wait()
    rows_o.wait()

    column_a = ca.at[core, :, here_x, lower]
    row_b = ca.at[core, y, :, upper]
    both_ends(column_a, g_a, ny - 1)
    along_x(column_a, g_a2)
    if nx > 1:
        both_ends(row_b, g_b, nx - 1)
    along_y(row_b, g_b2)
    plane_part(lambda j: columns(x, j), xs, s_x, 3 * n_plane // 4, n_plane)
    sent.append((xs, n_plane - 1, s_x))
    halves = []
    for span, s_p, n, kind in ((lower, g_a2, nx - 1, 0), (upper, g_b2, ny - 1, 1)):
        if n:
            rest = ca.at[core, :, pl.ds(0, n), span] if kind == 0 else ca.at[core, pl.ds(0, n), :, span]
            for sem in (recv, send):
                pltpu.make_async_copy(rest, rest, sem.at[s_p]).wait()
        whole = ca.at[core, :, :, span]
        s_p = fresh()
        remote(whole, whole, s_p, at_chip(chip, 1 - core)).start()
        halves.append((whole, s_p))
    both = None
    for piece, (whole, s_p) in enumerate(halves):
        pltpu.make_async_copy(whole, whole, recv.at[s_p]).wait()
        base = piece * (WIDE // 2)
        for j in range(n_plane):
            q = j % n_chip
            at = ((q // nx) * xc + (q % nx) * 2 + j // n_chip) * WIDE + base
            own_rows = jnp.concatenate(
                [xr[:, at : at + WIDE // 2], orow[:, at : at + WIDE // 2]], axis=0
            )
            t = mm(own_rows, ca[j // n_chip, q // nx, q % nx, base : base + WIDE // 2])
            both = t if both is None else both + t

    def spread(v, at):
        return jnp.broadcast_to(v[:, at : at + 1], (tall, two))

    f_own = jnp.where(left_half, (both[:TOK] * sd).astype(BF16).astype(F32), both[TOK:])
    am1[...] = f_own.astype(BF16)
    ab1[me] = am1[...]
    s_g, s_h2 = fresh(), fresh()
    chip_send(lambda q: am1, ab1, me, s_g)
    g_wide = None
    for j in range(n_plane):
        c = ca[j // n_chip, (j % n_chip) // nx, j % nx]
        t = mm(c, c, TN)
        g_wide = t if g_wide is None else g_wide + t
    g_wide = g_wide[RANK:]
    c_t = exact(put_r, ca[core, y, here_x].astype(F32), NT)
    nought = jnp.zeros_like(put_l)
    e_top = jnp.concatenate([put_l, nought], axis=0)
    e_top_r = jnp.concatenate([put_r, nought], axis=0)
    e_bot = jnp.concatenate([nought, put_l], axis=0)
    e_bot_r = jnp.concatenate([nought, put_r], axis=0)
    low_p = exact(f_own[:HALF], e_top) + exact(f_own[HALF:], e_top_r)
    ou_p = exact(f_own[:HALF], e_bot) + exact(f_own[HALF:], e_bot_r)
    hot = exact(hot_t, eye, TN)
    hot_l = exact(hot, put_l).astype(BF16)
    hot_r = exact(hot, put_r).astype(BF16)
    g_right = jnp.where(left_half, 0.0, g_wide)
    g_left = pltpu.roll(g_right, RANK, 1)
    g = g_left[:, :RANK]
    g_diag = jnp.concatenate([g_left, g_right], axis=0)
    k_l = jnp.concatenate([g_left * sr2, put_l * sr], axis=0)
    k_r = jnp.concatenate([g_right * sr2, put_r * sr], axis=0)
    wlp_in = wlp * sr2
    arrived(ab1, n_chip - 1, s_g)
    mine_half = ab1.at[pl.ds(core * n_chip, n_chip)]
    sib_send(mine_half, mine_half, s_h2)
    arrived(ab1, n_chip, s_h2)
    plane_part(lambda j: columns(o, j), os_, s_o, 1, n_plane)
    sent.append((os_, n_plane - 1, s_o))

    f_a = ab1[:, :HALF].reshape(tall, two)
    f_b = ab1[:, HALF:].reshape(tall, two)
    f_ab = jnp.concatenate([f_a, f_b], axis=1)
    p0 = (whp * mm2(f_ab, jnp.concatenate([k_l, k_r], axis=0))).astype(BF16)
    def fold(v, a, b):
        return mm(v, a, TN)[:RANK] + mm(v, b, TN)[RANK:]

    own_x.wait()
    arrived(xs, n_plane - 1, s_x)
    x_a = xs[:, :HALF].reshape(tall, WIDE)
    x_b = xs[:, HALF:].reshape(tall, WIDE)
    zp1[...] = (fold(p0, x_a, x_b) * sd).reshape(n_line, chunk, WIDE)
    s_r = line_start(zp1, zb1)
    wfh_a = (f_a.astype(F32) * spread(whp, 0)).astype(BF16)
    wfh_b = (f_b.astype(F32) * spread(whp, RANK)).astype(BF16)
    wfl_a = (f_a.astype(F32) * spread(wlp, 0)).astype(BF16)
    wfl_b = (f_b.astype(F32) * spread(wlp, RANK)).astype(BF16)
    q_h = mm(f_a, wfh_a, TN)[:RANK] + mm(f_b, wfh_b, TN)[:RANK]
    q_l = mm(f_a, wfl_a, TN)[:RANK] + mm(f_b, wfl_b, TN)[:RANK]
    zp1b[...] = jnp.concatenate([q_h, q_l], axis=1).reshape(n_line, chunk, WIDE)
    s_q = line_start(zp1b, zb1b)
    s_r = line_mid(zb1, zm1, zg1, s_r)
    s_q = line_mid(zb1b, zm1b, zg1b, s_q)
    eu_p = ou_p + sr * exact(low_p, g_diag)
    arrived(zg1, n_line - 1, s_r)

    d_t = zg1[...].reshape(RANK, WIDE)
    nil = jnp.zeros((RANK, WIDE), BF16)

    def apply(v, a, b, both):
        parts = split(v) if both else (v.astype(BF16),)
        w_a = jnp.concatenate([w for part in parts for w in (part, nil)], axis=0)
        w_b = jnp.concatenate([w for part in parts for w in (nil, part)], axis=0)
        out = mm(a, w_a, NT) + mm(b, w_b, NT)
        if both:
            out = out[:, :two] + out[:, two:]
        return out.astype(BF16).reshape(n_plane, HALF, two)

    t2 = sum_start(apply(d_t, x_a, x_b, True), po2, rb2)
    own_o.wait()
    arrived(os_, n_plane - 1, s_o)
    o_a = os_[:, :HALF].reshape(tall, WIDE)
    o_b = os_[:, HALF:].reshape(tall, WIDE)
    zp1z[...] = (mm(wfh_a, o_a, TN)[:RANK] + mm(wfh_b, o_b, TN)[:RANK]).reshape(n_line, chunk, WIDE)
    s_zz = line_start(zp1z, zb1z)

    pair_sems = [fresh(), fresh(), fresh()]

    def hand_over(k, both_halves):
        pair_out[k] = both_halves.T

        @pl.when(paired)
        def _():
            remote(pair_out.at[k], pair_in.at[k], pair_sems[k], partner).start()

        @pl.when(alone)
        def _():
            pair_in[k] = pair_out[k]

    d_l = sum_end(rb2, t2) * sd
    am2[...] = d_l.astype(BF16)
    ab2[me] = am2[...]
    s_a = fresh()
    plane_send(lambda j: am2, ab2, s_a)
    s_zz = line_mid(zb1z, zm1z, zg1z, s_zz)
    arrived(zg1b, n_line - 1, s_q)
    stats = zg1b[...].reshape(RANK, WIDE)
    s_h = stats[:, :RANK]
    zu = pltpu.roll(stats[:, :two], RANK, 1)[:, :RANK]
    s_l = stats[:, two : two + RANK]
    d_m = eye * sr
    d_n = s_h * sr2
    d_tu = exact(d_m, zu, TN) + exact(d_n, g, TN)

    def up_slice(m, n):
        return exact(m, z_t, TN) + exact(n, c_t, TN)


    put_l16, put_r16 = put_l.astype(BF16), put_r.astype(BF16)

    def place(m, put, dims=NN):
        hi, lo = split(m)
        return mm(hi, put, dims) + mm(lo, put, dims)

    def near(a, b):
        a_hi, a_lo = split(a)
        b_hi, b_lo = split(b)
        return mm(a_hi, b_hi) + (mm(a_hi, b_lo) + mm(a_lo, b_hi))

    def with_low(tu):
        tu_l = jnp.concatenate([place(tu, put_l16), nought], axis=0)
        tu_r = jnp.concatenate([place(tu, put_r16), nought], axis=0)
        return mm2(f_ab, jnp.concatenate([tu_l, tu_r], axis=0))

    def image_part(l_p, inner, zp):
        y_p = (wlp_in * (inner + mm2(l_p, g_diag))).astype(BF16)
        down = fold(y_p, x_a, x_b) * sd
        cross = fold(l_p, wfl_a, wfl_b)
        cross = jnp.where(left32, cross[:HALF], pltpu.roll(cross[HALF:], RANK, 1))
        zp[...] = jnp.concatenate([down[:, :two], down[:, two:], cross], axis=0).astype(BF16)

    inner = with_low(d_tu)
    arrived(ab2, n_plane - 1, s_a)
    gathered = ab2[...].reshape(tall, two)

    def diag(m):
        return jnp.concatenate([place(m, put_l16), place(m, put_r16)], axis=0)

    def diag_t(m):
        return jnp.concatenate([place(m, put_l16, TN), place(m, put_r16, TN)], axis=0)

    def up_rows(m, n, tu):
        return low_p * (near(oz_p, diag(m)) + late_rows(n, tu))

    def late_rows(n, tu):
        return near(ou_p, diag(n)) + sr * near(low_p, diag_t(tu))

    def by_domain(q, to):
        q_left = jnp.where(left32, q, 0.0)
        q_right = jnp.where(left32, 0.0, q)
        by = place(q_left, to[:HALF], TN) + place(q_right, to[HALF:], TN)
        return sr * jnp.sum(by, axis=0, keepdims=True)

    r_t, r_m, r_n, r_l, r_tu = d_t, d_m, d_n, d_l, d_tu
    first_l, first_m, first_n, first_tu = d_l, d_m, d_n, d_tu
    rounds = (
        (zp2, zb2, po3, rb3), (zp3, zb3, po4, rb4),
    )
    steps = []
    for turn, (zp, zb, po, rb) in enumerate(rounds):
        image_part(gathered, inner, zp)
        s_z = fresh()
        zb[z] = zp[...]
        line_send(lambda k: zp, zb, s_z)
        i_m = sr2 * exact(d_m, s_l) + mu * d_m
        i_n = sr2 * exact(d_n, s_l) + mu * d_n
        i_tu = exact(i_m, zu, TN) + exact(i_n, g, TN)
        if turn == 0:
            arrived(zg1z, n_line - 1, s_zz)
            z_t = zg1z[...].reshape(RANK, WIDE)
            d_t = jnp.concatenate([d_t, up_slice(d_m, d_n)], axis=0)
            r_t = d_t
        i_up = up_slice(i_m, i_n)
        if turn == 0:
            pz[...] = apply(z_t, o_a, o_b, False)
            s_pz = fresh()
            rz[me] = pz[me]
            plane_send(lambda j: pz.at[j], rz, s_pz)
        else:
            r_lt = near(low_p, diag(r_tu))
            d_lt = near(low_p, diag(d_tu))
        r_r_part = total(r_t * r_t)
        if turn == 0:
            hand_over(0, d_t)
        else:
            third_up = up_rows(i_m, i_n, i_tu)
            d_sv = exact(s_l, d_t[RANK:], TN)
            r_sv = exact(s_l, r_t[RANK:], TN)
        arrived(zb, n_line - 1, s_z)
        full = jnp.sum(zb[...].astype(F32), axis=0)
        down = jnp.concatenate([full[:RANK], full[RANK:two]], axis=1)
        cross = full[two:]
        cross = sr2 * jnp.concatenate([cross, pltpu.roll(cross, RANK, 1)], axis=0)[:, :RANK]
        i_t = jnp.concatenate(
            [down + mu * d_t[:RANK], i_up + exact(cross, c_t, TN)], axis=0
        )
        note = jnp.zeros((8, two), F32)
        for at, value in enumerate((total(d_t * i_t), total(r_t * i_t), total(i_t * i_t), r_r_part)):
            note = jnp.where(sub8 == at, value, note)

        note = jnp.concatenate([part.astype(F32)[:4] for part in split(note)], axis=0).astype(BF16)
        terms = jnp.concatenate(
            [apply(i_t[:RANK], x_a, x_b, True), jnp.broadcast_to(note[None], (n_plane, 8, two))], axis=1
        )
        t3 = sum_start(terms, po, rb)
        cross_tu = exact(cross, g, TN)
        i_n = i_n + cross
        i_tu = i_tu + cross_tu
        if turn == 1:
            third_up = third_up + low_p * late_rows(cross, cross_tu)
            i_lt = near(low_p, diag(i_tu))
            i_sv = exact(s_l, i_t[RANK:], TN)
        s = sum_end(rb, t3)
        i_l = s[:HALF] * sd
        sums = s[HALF : HALF + 4] + s[HALF + 4 :]
        di, ri, ii, r_r = [sums[at : at + 1, :1] for at in range(4)]
        alpha = r_r / di
        rr = r_r - 2.0 * alpha * ri + alpha * alpha * ii
        beta = rr / r_r
        steps.append((alpha, beta))
        r_l = r_l - alpha * i_l
        d_l = r_l + beta * d_l
        if turn == 0:
            am3[...] = d_l.astype(BF16)
            ab3[me] = am3[...]
            s_a = fresh()
            plane_send(lambda j: am3, ab3, s_a)
            r_tu = r_tu - alpha * i_tu
            d_tu = r_tu + beta * d_tu
            inner = with_low(d_tu)
            hand_over(1, i_t)
            arrived(rz, n_plane - 1, s_pz)
            oz_p = jnp.sum(rz[...].astype(F32), axis=0)
            second_by = by_domain(i_l * eu_p + up_rows(i_m, i_n, i_tu), hot_r)
            first_by = by_domain(first_l * eu_p + up_rows(first_m, first_n, first_tu), hot_l)
        else:
            d_lt = r_lt - alpha * i_lt + beta * d_lt
            d_sv = r_sv - alpha * i_sv + beta * d_sv
            third_by = by_domain(i_l * eu_p + third_up, hot_l)
        r_t, r_m, r_n = r_t - alpha * i_t, r_m - alpha * i_m, r_n - alpha * i_n
        d_t, d_m, d_n = r_t + beta * d_t, r_m + beta * d_m, r_n + beta * d_n
        if turn == 0:
            arrived(ab3, n_plane - 1, s_a)
            gathered = ab3[...].reshape(tall, two)

    d_lb = d_l.astype(BF16)
    quad = sr2 * own_wl * d_lb.astype(F32) * (mm2(d_lb, g_diag) + 2.0 * d_lt)
    slices = mu * total(d_t * d_t) + sr2 * total(d_sv * d_t[RANK:])
    curve = total(quad) + slices * (1.0 / n_line)
    s_f, s_l2 = fresh(), fresh()
    fm[...] = jnp.where(
        sub8 == 0, first_by + second_by, jnp.where(sub8 == 1, third_by, jnp.where(sub8 == 2, curve, 0.0))
    )[:4]
    fb[me] = fm[...]
    plane_send(lambda j: fm, fb, s_f)
    hand_over(2, i_t)
    arrived(fb, n_plane - 1, s_f)
    fq[...] = jnp.sum(fb[...], axis=0)
    fz[z] = fq[...]
    line_send(lambda k: fq, fz, s_l2)
    (a0, b0), (a1, b1) = steps
    for k in range(3):
        @pl.when(paired)
        def _(k=k):
            remote(pair_out.at[k], pair_in.at[k], pair_sems[k], partner).wait()

    @pl.when(alone)
    def _():
        given = ca.at[core, pl.ds(0, n_hi - 1), here_x]
        pltpu.make_async_copy(given, given, send.at[s_c]).wait()

    for whole, s_p in halves:
        pltpu.make_async_copy(whole, whole, send.at[s_p]).wait()
    for buf, n, s in sent[:-1]:
        wait_for(buf, n, send.at[s])
    arrived(fz, n_line - 1, s_l2)
    last = jnp.sum(fz[...], axis=0)
    a2 = rr / last[2:3, :1]
    w0 = a0 + a1 * (1.0 + b0) + a2 * (1.0 + b1 * (1.0 + b0))
    w1 = -a0 * (a1 + a2 * (1.0 + b1))
    w2 = -a1 * a2
    hyp = w0 * last[:1] + w1 * pltpu.roll(last, RANK, 1)[:1] + w2 * last[1:2]
    hyp_out[...] = -kappa * hyp[:, :RANK]
    sol_out[...] = w0 * pair_in[0] + w1 * pair_in[1] + w2 * pair_in[2]
    buf, n, s = sent[-1]
    wait_for(buf, n, send.at[s])


def solution(mesh, xc=8, z_lo=2):
    n_dp, n_fsdp = mesh.shape["dp"], mesh.shape["fsdp"]
    n_plane = (n_dp // z_lo) * xc
    n_line = (n_fsdp // xc) * z_lo
    n_chip = n_plane // 2
    n_sem = 48
    geo = (n_plane, n_line, xc, z_lo, n_sem)
    chunk = RANK // n_line
    two = 2 * RANK
    vm = pltpu.VMEM

    def sums(rows):
        return [vm((n_plane, rows, two), BF16)] * 2

    def gather(rows):
        return [vm((rows, two), BF16), vm((n_plane, rows, two), BF16)]

    def line(*shape):
        return [vm((n_line, *shape), F32), vm((n_line, *shape), F32), vm(shape, F32), vm((n_line, *shape), F32)]

    terms = [vm((two + HALF, two), BF16), vm((n_line, two + HALF, two), BF16)]
    late = vm((n_plane, HALF, two), BF16)
    scratch = [
        vm((n_plane, TOK, WIDE), BF16), vm((n_plane, TOK, WIDE), BF16), vm((2, n_chip // (xc // 2), xc // 2, WIDE, two), BF16),
        vm((n_plane, 8, two), F32), vm((TOK, n_plane * WIDE), BF16), vm((TOK, n_plane * WIDE), BF16),
        *gather(TOK), *line(chunk, WIDE), *line(chunk, WIDE), *line(chunk, WIDE),
        *sums(HALF), *gather(HALF), *terms, late, late,
        *sums(HALF + 8), *gather(HALF), *terms,
        *sums(HALF + 8),
        vm((4, two), F32), vm((n_plane, 4, two), F32), vm((4, two), F32), vm((n_line, 4, two), F32),
        vm((3, WIDE, two), F32), vm((3, WIDE, two), F32),
        pltpu.SemaphoreType.DMA((n_sem,)), pltpu.SemaphoreType.DMA((n_sem,)), pltpu.SemaphoreType.DMA((5,)),
    ]
    anywhere = pl.BlockSpec(memory_space=pl.ANY)
    inside = pl.BlockSpec(memory_space=pltpu.VMEM)

    def on_device(x, o, cat, coef, learn, held):
        sol, hyp = pl.pallas_call(
            functools.partial(kernel, geo),
            out_shape=(
                jax.ShapeDtypeStruct((WIDE, two), F32),
                jax.ShapeDtypeStruct((1, RANK), F32),
            ),
            in_specs=[anywhere, anywhere, inside, anywhere, inside, inside],
            out_specs=(inside, inside),
            scratch_shapes=scratch,
            compiler_params=pltpu.CompilerParams(
                collective_id=0, has_side_effects=True, vmem_limit_bytes=56 * 1024 * 1024
            ),
        )(x, o, cat.reshape(1, TOK), coef, learn.reshape(1, DOMAINS), held.reshape(1, DOMAINS))
        return sol, hyp.reshape(DOMAINS)

    placed = (P(("dp", "fsdp"), None), P(("dp", "fsdp"), None), P(("dp", "fsdp")), P("fsdp", None), P(), P())
    return jax.shard_map(
        on_device, mesh=mesh, in_specs=placed, out_specs=(P("fsdp", None), P()), check_vma=False
    )
```
